32 devices in a mesh: grp: 2 (over y), ep: 4 (over z), hd: 2 (over x), sub: 2 (over core).
Axes of the slice: x: 2, y: 2, z: 4, core: 2. Of those that a mesh axis runs over, the one named last changes fastest.
Arguments:
- queries: bfloat16 [2048, 4096], P(('grp', 'ep'), 'hd'), parts along dimension 0, may hold values from -1024 to 1024
- cache_keys: bfloat16 [2048, 512], P(('grp', 'ep', 'sub')), parts along dimension 0, may hold values from -4 to 4
- cache_values: bfloat16 [2048, 512], P(('grp', 'ep', 'sub')), parts along dimension 0, may hold values from -12 to 12
- page_len: int32 [16], P(('grp', 'ep', 'sub')), parts along dimension 0, may hold values from 1 to 128, 512 in all
- new_keys: bfloat16 [2048, 512], P(('grp', 'ep', 'sub')), parts along dimension 0, may hold values from -6 to 6
- new_values: bfloat16 [2048, 512], P(('grp', 'ep', 'sub')), parts along dimension 0, may hold values from -6 to 6
- out_proj: bfloat16 [4096, 2048], P('hd', 'sub'), may hold values from -0.09375 to 0.09375
- residual: bfloat16 [2048, 2048], P(('grp', 'ep', 'hd'), 'sub'), parts along dimension 0, may hold values from -6 to 6
- norm_gain: bfloat16 [2048], replicated, may hold values from 0.099609375 to 1.8984375
- gate_up: bfloat16 [8, 2, 384, 2048], P(('ep', 'hd'), None, 'sub'), may hold values from -0.125 to 0.125
- w_down: bfloat16 [8, 384, 2048], P(('ep', 'hd'), 'sub'), may hold values from -0.3125 to 0.3125
- expert_ids: int32 [2048, 8], P(('grp', 'ep', 'hd')), parts along dimension 0, may hold values from 0 to 7, as said below
- gates: bfloat16 [2048, 8], P(('grp', 'ep', 'hd')), parts along dimension 0, may hold values from 0.049804688 to 0.5
Outputs:
- layer_out: bfloat16 [2048, 2048], P(('grp', 'ep', 'hd'), 'sub'), parts along dimension 0
The draws below stay inside these ranges and needn't reach their ends.
There are 2 independent parts, one for each index of `grp`. The reference program is written for one: setup_inputs(seed, part) draws one part's arguments, and reference() takes and returns one part's arrays. A program takes and returns all parts, laid end to end along the dimension named above; an argument that names none is the same for every part. Nothing has to cross between parts.
Inputs may be any that keep to these rules, and one draw needn't show every extreme that they name: `expert_ids`: expert x belongs to group x // 2. Each row names 8 different experts, exactly two in each of 4 different groups. Among the rows of one block b (rows b * 128 to (b + 1) * 128 - 1), each group is named by at most 128 rows and each expert by at most 128; in every block some group is named by exactly 128 rows and some expert by exactly 128.
All inputs are finite; a program needn't handle non-finite values. No bound on the sum of `page_len` on one device may be relied on, other than what follows from the above.
Results may differ from the reference program's by a relative error of at most 0.02.
Values may be sent and summed in bfloat16 or wider, within the bound.
A program may use at most 64 MiB of HBM per device.

```python
import math
import jax
import jax.numpy as jnp
import numpy as np
from jax import lax

D = 2048
QH = 32
KVH = 4
HD = 128
FF = 384
TOPK = 8
GROUPS_ROW = 4
CACHE_DEV = 128
ROWS = 1024
PAGES = 8
CACHE = 1024
GROUPS = 4
GROUP_EXPERTS = 2
EXPERTS = 8
RM = 128
CAPG = 128
CAP = 128


def drawn_fields(key):
    key_field = jnp.clip(jax.random.normal(jax.random.fold_in(key, 101), (CACHE, KVH * HD), jnp.float32), -4.0, 4.0)
    query_field = jnp.clip(jax.random.normal(jax.random.fold_in(key, 102), (ROWS, QH * HD), jnp.float32), -4.0, 4.0)
    return (query_field, key_field)


def draw_queries(key, part):
    return drawn_fields(key)[0].astype(jnp.bfloat16)


def draw_cache_keys(key, part):
    return drawn_fields(key)[1].astype(jnp.bfloat16)


def draw_expert_ids(key, part):
    blocks = ROWS // RM
    order_keys = jax.random.split(jax.random.fold_in(key, 301), blocks)
    row_keys = jax.random.split(jax.random.fold_in(key, 302), blocks)
    group_orders = jax.vmap(lambda one_key: jax.random.permutation(one_key, GROUPS))(order_keys).astype(jnp.int32)
    row_orders = jax.vmap(lambda one_key: jax.random.permutation(one_key, RM))(row_keys).astype(jnp.int32)
    hot_group = group_orders[:, 0]
    others = group_orders[:, 1:]
    is_hot = (row_orders < CAPG).astype(jnp.int32)
    needed = GROUPS_ROW - is_hot
    offsets = jax.random.randint(jax.random.fold_in(key, 303), (blocks, 1), 0, GROUPS - 1).astype(jnp.int32)
    first_pick = jnp.cumsum(needed, axis=1) - needed + offsets
    columns = jnp.arange(GROUPS_ROW, dtype=jnp.int32)
    pick_index = (first_pick[:, :, None] + columns[None, None, :] - is_hot[:, :, None]) % (GROUPS - 1)
    other_pick = jnp.take_along_axis(jnp.broadcast_to(others[:, None, :], (blocks, RM, GROUPS - 1)), pick_index, axis=2)
    use_hot = (is_hot[:, :, None] > 0) & (columns[None, None, :] == 0)
    group_ids = jnp.where(use_hot, hot_group[:, None, None], other_pick).astype(jnp.int32)
    member = (group_ids[:, :, :, None] == jnp.arange(GROUPS, dtype=jnp.int32)[None, None, None, :]).astype(jnp.int32)
    row_member = jnp.sum(member, axis=2)
    ordinal_all = jnp.cumsum(row_member, axis=1) - row_member
    ordinal = jnp.sum(member * ordinal_all[:, :, None, :], axis=3)
    shifts = jax.random.randint(jax.random.fold_in(key, 304), (blocks, GROUPS), 0, GROUP_EXPERTS).astype(jnp.int32)
    shift_chosen = jnp.sum(member * shifts[:, None, None, :], axis=3)
    first_local = (2 * ordinal + shift_chosen) % GROUP_EXPERTS
    second_local = (2 * ordinal + 1 + shift_chosen) % GROUP_EXPERTS
    expert_pair = jnp.stack([group_ids * GROUP_EXPERTS + first_local, group_ids * GROUP_EXPERTS + second_local], axis=3)
    return expert_pair.reshape(ROWS, TOPK).astype(jnp.int32)


def level_of(key, extent, shards, low, high):
    gain, own = 1.0, jax.random.fold_in(key, 6)
    for position, shards_of in shards:
        heights = jnp.exp(jax.random.uniform(jax.random.fold_in(own, position), (shards_of,), jnp.float32, low / len(shards), high / len(shards)))
        gain = gain * jnp.repeat(heights, extent[position] // shards_of).reshape([-1 if axis == position else 1 for axis in range(len(extent))])
    return gain


def length_profile(amount, total, bound, skew):
    loads = [(1 << 20) // math.isqrt(rank ** skew) + 1 for rank in range(2, amount + 1)]
    rest, counts = total - bound - (amount - 1), [1] * (amount - 1)
    while rest > 0:
        movable = [i for i in range(amount - 1) if counts[i] < bound]
        mass, left = sum([loads[i] for i in movable]), rest
        for i in movable:
            more = min(bound - counts[i], max(1, left * loads[i] // mass), rest)
            counts[i] = counts[i] + more
            rest = rest - more
    return np.array([bound] + counts)


def uneven(key, number_of, total, reach, skew):
    if number_of == 2:
        one = jax.random.randint(key, (), max(1, total - reach), min(reach, total - 1) + 1)
        return jnp.stack([one, total - one])
    sizes = jnp.asarray(length_profile(number_of, total, reach, skew), jnp.int32)
    couples = (number_of - 1) // 2
    donor, sink = sizes[1:1 + 2 * couples:2], sizes[2:2 + 2 * couples:2]
    room = jnp.minimum(donor - 1, reach - sink)
    passed = jax.random.randint(jax.random.fold_in(key, 1), (couples,), 0, 1 << 20) % (room + 1)
    sizes = sizes.at[1:1 + 2 * couples:2].set(donor - passed).at[2:2 + 2 * couples:2].set(sink + passed)
    return sizes[jax.random.permutation(jax.random.fold_in(key, 2), number_of)]


def centred(stream_key, extent, width, bound, shards=(), held_as=jnp.bfloat16):
    array = width * jax.random.normal(stream_key, extent, jnp.float32)
    if shards:
        array = array * level_of(stream_key, extent, shards, -0.22, 0.18)
    return jnp.clip(array, -bound, bound).astype(held_as)


def setup_inputs(seed: int = 0, part: int = 0) -> dict:
    keys = jax.random.split(jax.random.key(seed), 14)
    own_keys = jax.random.split(jax.random.fold_in(keys[13], part), 14)
    return {
        "queries": draw_queries(jax.random.fold_in(jax.random.fold_in(keys[13], part), 71), part),
        "cache_keys": draw_cache_keys(jax.random.fold_in(jax.random.fold_in(keys[13], part), 71), part),
        "cache_values": centred(own_keys[2], (CACHE, KVH * HD), 2.0, 12.0, ((0, 8),)),
        "page_len": uneven(own_keys[3], PAGES, PAGES * CACHE_DEV // 2, CACHE_DEV, 2).astype(jnp.int32),
        "new_keys": centred(own_keys[4], (ROWS, KVH * HD), 1.0, 6.0, ((0, 8),)),
        "new_values": centred(own_keys[5], (ROWS, KVH * HD), 1.0, 6.0, ((0, 8),)),
        "out_proj": centred(keys[6], (QH * HD, D), (QH * HD) ** -0.5, 0.09375, ((0, 2), (1, 2))),
        "residual": centred(own_keys[7], (ROWS, D), 1.0, 6.0, ((0, 8), (1, 2))),
        "norm_gain": jnp.clip(1.0 + 0.18 * jax.random.normal(keys[8], (D,), jnp.float32), 0.099609375, 1.8984375).astype(jnp.bfloat16),
        "gate_up": centred(keys[9], (EXPERTS, 2, FF, D), D ** -0.5, 0.125, ((0, 8), (2, 2))),
        "w_down": centred(keys[10], (EXPERTS, FF, D), FF ** -0.5, 0.3125, ((0, 8), (1, 2))),
        "expert_ids": draw_expert_ids(jax.random.fold_in(jax.random.fold_in(keys[13], part), 71), part),
        "gates": jnp.clip(jnp.exp(math.log(0.5) - 2.306499 * jax.random.uniform(own_keys[12], (ROWS, TOPK), jnp.float32) ** level_of(own_keys[12], (ROWS, TOPK), ((0, 8),), -0.2, 0.2)), 0.049804688, 0.5).astype(jnp.bfloat16),
    }


EPSILON = 1e-06

def visible_mask(page_len):
    positions = jnp.arange(CACHE, dtype=jnp.int32)
    cache_ok = positions % CACHE_DEV < page_len[positions // CACHE_DEV]
    row_index = jnp.arange(ROWS, dtype=jnp.int32)
    causal = row_index[None, :] <= row_index[:, None]
    return jnp.concatenate([jnp.broadcast_to(cache_ok[None, :], (ROWS, CACHE)), causal], axis=1)

def attention(queries, joined_keys, joined_values, visible):
    score_scale = 1.0 / math.sqrt(HD)
    per_group = QH // KVH

    def one_head(head_index):
        kv_index = head_index // per_group
        query_head = lax.dynamic_slice_in_dim(queries, head_index * HD, HD, 1)
        key_head = lax.dynamic_slice_in_dim(joined_keys, kv_index * HD, HD, 1)
        value_head = lax.dynamic_slice_in_dim(joined_values, kv_index * HD, HD, 1)
        scores = jnp.dot(query_head, key_head.T, preferred_element_type=jnp.float32) * score_scale
        masked = jnp.where(visible, scores, -jnp.inf)
        row_max = lax.optimization_barrier(jnp.max(masked, axis=1, keepdims=True))
        exp_terms = jnp.where(visible, jnp.exp(scores - row_max), 0.0)
        weight_sum = lax.optimization_barrier(jnp.sum(exp_terms, axis=1, keepdims=True))
        mixed = jnp.dot(exp_terms.astype(jnp.bfloat16), value_head, preferred_element_type=jnp.float32)
        return mixed / weight_sum
    heads_out = lax.map(one_head, jnp.arange(QH, dtype=jnp.int32))
    return jnp.transpose(heads_out, (1, 0, 2)).reshape(ROWS, QH * HD).astype(jnp.bfloat16)

def experts_apply(normed, expert_ids, gates, gate_up, w_down):
    blocks = ROWS // RM
    flat_ids = expert_ids.reshape(blocks, RM * TOPK)
    onehot = (flat_ids[:, :, None] == jnp.arange(EXPERTS, dtype=jnp.int32)[None, None, :]).astype(jnp.int32)
    before = jnp.cumsum(onehot, axis=1) - onehot
    slot_index = lax.optimization_barrier(jnp.sum(before * onehot, axis=2))
    block_index = jnp.arange(blocks, dtype=jnp.int32)[:, None]
    row_index = block_index * RM + jnp.arange(RM * TOPK, dtype=jnp.int32)[None, :] // TOPK
    target = ((flat_ids * blocks + block_index) * CAP + slot_index).reshape(-1).astype(jnp.int32)
    table_rows = jnp.zeros((EXPERTS * blocks * CAP,), jnp.int32).at[target].set(row_index.reshape(-1).astype(jnp.int32))
    table_gates = jnp.zeros((EXPERTS * blocks * CAP,), jnp.float32).at[target].set(gates.reshape(-1).astype(jnp.float32))

    def one_expert(accumulated, operands):
        rows_x, gates_x, weight_pair, weight_down = operands
        inputs = normed[rows_x]
        gate_part = jnp.dot(inputs, weight_pair[0].T, preferred_element_type=jnp.float32)
        up_part = jnp.dot(inputs, weight_pair[1].T, preferred_element_type=jnp.float32)
        activation = (jax.nn.silu(gate_part) * up_part).astype(jnp.bfloat16)
        result = jnp.dot(activation, weight_down, preferred_element_type=jnp.float32).astype(jnp.bfloat16)
        accumulated = accumulated.at[rows_x].add(gates_x[:, None] * result.astype(jnp.float32))
        return (accumulated, None)
    accumulated, _ = lax.scan(one_expert, jnp.zeros((ROWS, D), jnp.float32), (table_rows.reshape(EXPERTS, blocks * CAP), table_gates.reshape(EXPERTS, blocks * CAP), gate_up, w_down))
    return accumulated

def reference(queries, cache_keys, cache_values, page_len, new_keys, new_values, out_proj, residual, norm_gain, gate_up, w_down, expert_ids, gates):
    visible = visible_mask(page_len)
    joined_keys = jnp.concatenate([cache_keys, new_keys], axis=0)
    joined_values = jnp.concatenate([cache_values, new_values], axis=0)
    attended = attention(queries, joined_keys, joined_values, visible)
    projected = jnp.dot(attended, out_proj, preferred_element_type=jnp.float32)
    hidden_state = (residual.astype(jnp.float32) + projected).astype(jnp.bfloat16)
    widened = hidden_state.astype(jnp.float32)
    mean_square = lax.optimization_barrier(jnp.mean(widened * widened, axis=1, keepdims=True))
    normed = (widened * lax.rsqrt(mean_square + EPSILON) * norm_gain.astype(jnp.float32)).astype(jnp.bfloat16)
    mixture = experts_apply(normed, expert_ids, gates, gate_up, w_down)
    return (widened + mixture).astype(jnp.bfloat16)
```

```python
import functools
import math

import jax
import jax.numpy as jnp
from jax import lax
from jax.experimental import pallas as pl
from jax.experimental.pallas import tpu as pltpu
from jax.sharding import PartitionSpec as P

QH = 32
KVH = 4
HD = 128
GROUPS_ROW = 4


NEG_FILL = -1e30
EPSILON = 1e-06
KEY_BLOCK = 1024
FAR_RANK = 1073741824
MESH = pl.DeviceIdType.MESH


def joined(x, axis, join):
    gathered = jax.tree.map(
        lambda a, kind: lax.all_gather(a.astype(kind), axis),
        x,
        jax.tree.map(lambda a: jnp.bfloat16 if a.dtype == jnp.float32 else a.dtype, x),
    )

    def take(source):
        return jax.tree.map(
            lambda a, own: lax.dynamic_index_in_dim(a, source, 0, False).astype(own.dtype),
            gathered,
            x,
        )

    return lax.fori_loop(
        1, lax.axis_size(axis), lambda source, state: join(state, take(source)), take(0)
    )


def block_sizes(block_rows, group_total, experts_group):
    group_slots = min(block_rows, 3 * GROUPS_ROW * block_rows // (2 * group_total))
    return (group_slots, 2 * group_slots // experts_group)


def attend_block(fold_state, packed, key_rank, query_heads, row_ids, kv_heads):
    running_max, weight_sum, weighted = fold_state
    half_cols = packed.shape[1] // 2
    length = packed.shape[0]
    key_part = packed[:, :half_cols].reshape(length, kv_heads, half_cols // kv_heads)
    value_part = packed[:, half_cols:].reshape(length, kv_heads, half_cols // kv_heads)
    scores = jnp.einsum(
        "rkqd,lkd->rkql", query_heads, key_part, preferred_element_type=jnp.float32
    ) * (1.0 / math.sqrt(HD))
    allowed = (key_rank[None, :] <= row_ids[:, None])[:, None, None, :]
    masked = jnp.where(allowed, scores, NEG_FILL)
    new_max = jnp.maximum(running_max, jnp.max(masked, axis=3))
    factor = jnp.exp(running_max - new_max)
    exp_terms = jnp.where(allowed, jnp.exp(scores - new_max[..., None]), 0.0)
    weight_sum = weight_sum * factor + jnp.sum(exp_terms, axis=3)
    weighted = weighted * factor[..., None] + jnp.einsum(
        "rkql,lkd->rkqd",
        exp_terms.astype(jnp.bfloat16),
        value_part,
        preferred_element_type=jnp.float32,
    )
    return (new_max, weight_sum, weighted)


def join_parts(first_part, second_part):
    first_max, first_sum, first_weighted = first_part
    second_max, second_sum, second_weighted = second_part
    joint_max = jnp.maximum(first_max, second_max)
    first_factor = jnp.exp(first_max - joint_max)
    second_factor = jnp.exp(second_max - joint_max)
    joint_sum = first_sum * first_factor + second_sum * second_factor
    joint_weighted = (
        first_weighted * first_factor[..., None] + second_weighted * second_factor[..., None]
    )
    return (joint_max, joint_sum, joint_weighted)


def shards(
    queries,
    cache_keys,
    cache_values,
    page_len,
    new_keys,
    new_values,
    out_proj,
    residual,
    norm_gain,
    gate_up,
    w_down,
    expert_ids,
    gates,
):
    query_rows = queries.shape[0]
    heads_here = queries.shape[1] // HD
    group_width = QH // KVH
    kv_heads = max(1, heads_here // group_width)
    per_kv = heads_here // kv_heads
    kv_first = lax.axis_index("hd") * heads_here // group_width

    def kv_columns(source):
        return lax.dynamic_slice_in_dim(source, kv_first * HD, kv_heads * HD, 1)

    local_keys = jnp.concatenate([kv_columns(cache_keys), kv_columns(new_keys)], axis=0)
    local_values = jnp.concatenate([kv_columns(cache_values), kv_columns(new_values)], axis=0)
    packed_local = jnp.concatenate([local_keys, local_values], axis=1)
    cache_rows = cache_keys.shape[0]
    new_rows = new_keys.shape[0]
    cache_rank = jnp.where(
        jnp.arange(cache_rows, dtype=jnp.int32) < page_len[0], -1, FAR_RANK
    ).astype(jnp.int32)
    new_block = lax.axis_index("ep") * lax.axis_size("sub") + lax.axis_index("sub")
    new_rank = new_block * new_rows + jnp.arange(new_rows, dtype=jnp.int32)
    rank_local = jnp.concatenate([cache_rank, new_rank], axis=0)
    row_ids = lax.axis_index("ep") * query_rows + jnp.arange(query_rows, dtype=jnp.int32)
    query_heads = queries.reshape(query_rows, kv_heads, per_kv, HD)

    def fold_keys(fold_state, piece_data):
        packed, key_rank = piece_data
        length = packed.shape[0]
        if length > KEY_BLOCK and length % KEY_BLOCK == 0:
            block_count = length // KEY_BLOCK

            def scan_step(inner_state, block_data):
                return (
                    attend_block(
                        inner_state, block_data[0], block_data[1], query_heads, row_ids, kv_heads
                    ),
                    None,
                )

            fold_state, _ = lax.scan(
                scan_step,
                fold_state,
                (
                    packed.reshape(block_count, KEY_BLOCK, packed.shape[1]),
                    key_rank.reshape(block_count, KEY_BLOCK),
                ),
            )
            return fold_state
        return attend_block(fold_state, packed, key_rank, query_heads, row_ids, kv_heads)

    start_state = (
        jnp.full((query_rows, kv_heads, per_kv), NEG_FILL, jnp.float32),
        jnp.zeros((query_rows, kv_heads, per_kv), jnp.float32),
        jnp.zeros((query_rows, kv_heads, per_kv, HD), jnp.float32),
    )
    fold_state = fold_keys(
        start_state,
        (
            lax.all_gather(packed_local, "ep", axis=0, tiled=True),
            lax.all_gather(rank_local, "ep", axis=0, tiled=True),
        ),
    )
    running_max, weight_sum, weighted = joined(fold_state, "sub", join_parts)
    attended = (
        (weighted / weight_sum[..., None]).reshape(query_rows, heads_here * HD).astype(jnp.bfloat16)
    )
    projected = lax.psum_scatter(
        jnp.dot(attended, out_proj, preferred_element_type=jnp.float32).astype(jnp.bfloat16),
        "hd",
        scatter_dimension=0,
        tiled=True,
    ).astype(jnp.float32)
    hidden_half = (residual.astype(jnp.float32) + projected).astype(jnp.bfloat16)
    widened = hidden_half.astype(jnp.float32)
    features = norm_gain.shape[0]
    half_width = hidden_half.shape[1]
    square_sum = lax.psum(jnp.sum(widened * widened, axis=1), "sub")
    gain_half = lax.dynamic_slice_in_dim(
        norm_gain, lax.axis_index("sub") * half_width, half_width, 0
    )
    normed = (
        widened
        * lax.rsqrt(square_sum[:, None] / features + EPSILON)
        * gain_half.astype(jnp.float32)
    ).astype(jnp.bfloat16)
    pair_weights = gate_up[0].reshape(-1, features)
    hidden_units = w_down.shape[1]
    group_total = lax.axis_size("ep")
    group_experts = lax.axis_size("hd")
    all_experts = group_total * group_experts
    block_rows = expert_ids.shape[0]
    group_slots, expert_slots = block_sizes(block_rows, group_total, group_experts)
    chosen = (
        expert_ids[:, :, None] == jnp.arange(all_experts, dtype=jnp.int32)[None, None, :]
    ).astype(jnp.int32)
    named_count = jnp.sum(chosen, axis=1)
    earlier = jnp.cumsum(named_count, axis=0) - named_count
    slot_index = jnp.sum(chosen * earlier[:, None, :], axis=2)
    position = expert_ids * expert_slots + slot_index
    slot_columns = jnp.arange(all_experts * expert_slots, dtype=jnp.int32)
    gate_table = jnp.sum(
        jnp.where(
            position[:, :, None] == slot_columns[None, None, :],
            gates.astype(jnp.float32)[:, :, None],
            0.0,
        ),
        axis=1,
    ).astype(jnp.bfloat16)
    placed = (gate_table != 0).astype(jnp.bfloat16)
    outgoing = jnp.einsum("rq,rd->qd", placed, normed, preferred_element_type=jnp.float32).astype(
        jnp.bfloat16
    )
    outgoing = outgoing.reshape(all_experts, expert_slots, normed.shape[1])
    arrived = lax.all_to_all(outgoing, ("ep", "hd"), split_axis=0, concat_axis=0, tiled=True)
    lead_shape = arrived.shape[:-1]
    rows_in = arrived.reshape(-1, arrived.shape[-1])
    rows_in = lax.all_gather(rows_in, "sub", axis=1, tiled=True)
    projected_pair = jnp.einsum(
        "rd,fd->rf", rows_in, pair_weights, preferred_element_type=jnp.float32
    )
    activation = (
        jax.nn.silu(projected_pair[:, :hidden_units]) * projected_pair[:, hidden_units:]
    ).astype(jnp.bfloat16)
    partial_out = jnp.dot(activation, w_down[0], preferred_element_type=jnp.float32)
    expert_out = lax.psum_scatter(
        partial_out.astype(jnp.bfloat16), "sub", scatter_dimension=1, tiled=True
    )
    results = expert_out.reshape(lead_shape + (expert_out.shape[1],))
    returned = lax.all_to_all(results, ("ep", "hd"), split_axis=0, concat_axis=0, tiled=True)
    mixture = jnp.dot(
        gate_table,
        returned.reshape(all_experts * expert_slots, half_width),
        preferred_element_type=jnp.float32,
    )
    return (widened + mixture).astype(jnp.bfloat16)


def slot_of(step, place, total):
    near = jnp.minimum(place, total - 1 - place)
    odd = place - (step + 1) // 2
    even = place + step // 2
    beside = jnp.where(step % 2 == 1, odd, even)
    beyond = jnp.where(place < total - 1 - place, step, total - 1 - step)
    return jnp.where(step <= 2 * near, beside, beyond)


(C_UP, C_DOWN, N_UP, X_UP, X_DOWN, W_SIDE, W_PART, Z_UP, Z_DOWN, P_SIDE) = range(10)
(C_IN, N_IN, X_IN, W_SIDE_IN, W_PART_IN, Z_IN, P_IN) = range(7)
SIB_COUNT = 17
LOG2_E = math.log2(math.e)


def layer_kernel(
    total, tiles,
    page_len, queries, cache_keys, cache_values, new_keys, new_values, out_proj, residual, gain_v,
    gate_up, w_down, ids_t, gates_t,
    out,
    q_v, cbuf, nbuf, m_v, l_v, acc_v, att, proj_w, part_out, part_in, res_v, hid, wgu,
    rows, results, chain_in,
    send_sem, recv_sem, load_sem, sib_send, sib_recv, proj_f, hid_out, gate_cols,
):
    e = lax.axis_index("ep")
    h = lax.axis_index("hd")
    s = lax.axis_index("sub")
    part = lax.axis_index("grp")
    last = total - 1
    heads = q_v.shape[0]
    page = new_keys.shape[0]
    page_c = cache_keys.shape[0]
    half = out.shape[2]
    own_rows = out.shape[1]
    features = 2 * half
    scale = LOG2_E / math.sqrt(HD)
    has_up = e < last
    has_down = e > 0

    def col(index, width):
        return pl.ds(pl.multiple_of(index * width, width), width)

    def local(index, src, dst):
        return pltpu.make_async_copy(src, dst, load_sem.at[index])

    mine = 2 * h + s
    loads = [
        local(0, cache_keys.at[:, col(mine, HD)], cbuf.at[e, s, pl.ds(0, page_c)]),
        local(1, cache_values.at[:, col(mine, HD)], cbuf.at[e, s, pl.ds(page_c, page_c)]),
        local(3, new_keys.at[:, col(mine, HD)], nbuf.at[e, s, pl.ds(0, page)]),
        local(4, new_values.at[:, col(mine, HD)], nbuf.at[e, s, pl.ds(page, page)]),
    ]
    q_loads = [
        local(16 + i, queries.at[:, col(s * heads + i, HD)], q_v.at[i]) for i in range(heads)
    ]
    w_loads = [
        local(5, out_proj, proj_w),
        local(6, residual, res_v),
        local(9, gate_up.at[0], wgu.at[h, pl.ds(0, 2), s]),
        local(10, w_down.at[0], wgu.at[h, 2, s]),
    ]
    for copy in loads + q_loads + w_loads:
        copy.start()

    experts = 2 * total
    lane = lax.broadcasted_iota(jnp.int32, (8, HD), 1)
    seen = jnp.where(lane < page_len[0], 0.0, NEG_FILL)
    ids = ids_t[...]
    gate_values = gates_t[...].astype(jnp.float32)
    place = lax.broadcasted_iota(jnp.int32, (8, HD), 0)
    by_expert = jnp.zeros((8, HD), jnp.float32)
    for x in range(experts):
        one_row = jnp.sum(jnp.where(ids == x, gate_values, 0.0), axis=0, keepdims=True)
        by_expert = jnp.where(place == x, one_row, by_expert)
    cbuf[e, s, 2 * page_c:2 * page_c + 16, :] = jnp.concatenate(
        [seen, by_expert], axis=0).astype(jnp.bfloat16)

    barrier = pltpu.get_barrier_semaphore()
    pl.semaphore_signal(barrier, inc=1, device_id={"sub": 1 - s}, device_id_type=MESH)
    pl.semaphore_signal(barrier, inc=1, device_id={"hd": 1 - h}, device_id_type=MESH)
    pl.semaphore_signal(barrier, inc=1, device_id={"grp": 1 - part}, device_id_type=MESH)

    @pl.when(has_up)
    def _():
        pl.semaphore_signal(barrier, inc=1, device_id={"ep": e + 1}, device_id_type=MESH)

    @pl.when(has_down)
    def _():
        pl.semaphore_signal(barrier, inc=1, device_id={"ep": e - 1}, device_id_type=MESH)

    pl.semaphore_wait(barrier, 3 + has_up.astype(jnp.int32) + has_down.astype(jnp.int32))

    def sibling(index, src, dst):
        return pltpu.make_async_remote_copy(
            src_ref=src, dst_ref=dst, send_sem=sib_send.at[index], recv_sem=sib_recv.at[index],
            device_id={"sub": 1 - s}, device_id_type=MESH)

    def remote(kind, index, arrival, slot, src, dst, where):
        return pltpu.make_async_remote_copy(
            src_ref=src, dst_ref=dst, send_sem=send_sem.at[kind, index],
            recv_sem=recv_sem.at[arrival, slot], device_id=where, device_id_type=MESH)

    theirs = 2 * h + 1 - s
    kv_sib = [
        sibling(0, cache_keys.at[:, col(theirs, HD)], cbuf.at[e, s, pl.ds(0, page_c)]),
        sibling(1, cache_values.at[:, col(theirs, HD)], cbuf.at[e, s, pl.ds(page_c, page_c)]),
        sibling(2, cbuf.at[e, s, pl.ds(2 * page_c, 16)], cbuf.at[e, s, pl.ds(2 * page_c, 16)]),
        sibling(3, new_keys.at[:, col(theirs, HD)], nbuf.at[e, s, pl.ds(0, page)]),
        sibling(4, new_values.at[:, col(theirs, HD)], nbuf.at[e, s, pl.ds(page, page)]),
    ]
    w_sib = [
        sibling(5, gate_up.at[0], wgu.at[h, pl.ds(0, 2), s]),
        sibling(6, w_down.at[0], wgu.at[h, 2, s]),
    ]
    for copy in kv_sib:
        copy.start()

    cut = wgu.shape[3] // 2

    def cut_rows(which):
        return pl.ds(pl.multiple_of(which * cut, cut), cut)

    def w_side(piece):
        src = (w_down.at[0, cut_rows(part)] if piece == 2
               else gate_up.at[0, piece, cut_rows(part)])
        return remote(W_SIDE, piece, W_SIDE_IN, piece, src,
                      wgu.at[h, piece, s, cut_rows(part)], {"hd": 1 - h})

    def w_part(piece):
        block_ref = wgu.at[1 - h, piece, s, cut_rows(part)]
        return remote(W_PART, piece, W_PART_IN, piece, block_ref, block_ref, {"grp": 1 - part})

    def w_near(piece, which):
        block_ref = wgu.at[1 - h, piece, s, cut_rows(jnp.where(which == 0, part, 1 - part))]
        return sibling(10 + 2 * piece + which, block_ref, block_ref)

    def w_from_side(piece):
        block_ref = wgu.at[1 - h, piece, s, cut_rows(part)]
        remote(W_SIDE, piece, W_SIDE_IN, piece, block_ref, block_ref, {"hd": 1 - h}).wait_recv()
        w_part(piece).start()
        w_near(piece, 0).start()

    def w_from_part(piece):
        w_part(piece).wait_recv()
        w_near(piece, 1).start()

    for piece in range(3):
        w_side(piece).start()

    def c_up(i):
        return remote(C_UP, i, C_IN, i, cbuf.at[i], cbuf.at[i], {"ep": e + 1})

    def c_down(i):
        return remote(C_DOWN, i, C_IN, i, cbuf.at[i], cbuf.at[i], {"ep": e - 1})

    def n_up(i):
        return remote(N_UP, i, N_IN, i, nbuf.at[i], nbuf.at[i], {"ep": e + 1})

    for copy in loads:
        copy.wait()
    for copy in kv_sib:
        copy.wait_recv()

    @pl.when(has_up)
    def _():
        n_up(e).start()
        c_up(e).start()

    @pl.when(has_down)
    def _():
        c_down(e).start()

    for copy in w_sib:
        copy.start()
    for copy in q_loads:
        copy.wait()

    def parts_of(buf, index, size):
        return (buf[index, :, 0:size, :].reshape(2 * size, HD),
                buf[index, :, size:2 * size, :].reshape(2 * size, HD))

    def attend(index, with_cache, with_new, causal, first=False):
        pieces = []
        if with_cache:
            pieces.append(parts_of(cbuf, index, page_c))
            line = jnp.concatenate(
                [cbuf[index, 0, 2 * page_c:2 * page_c + 16, :],
                 cbuf[index, 1, 2 * page_c:2 * page_c + 16, :]], axis=1)[0:1].astype(jnp.float32)
        if with_new:
            pieces.append(parts_of(nbuf, index, page))

        def one_head(i, carry):
            query = q_v[i]
            scores = []
            for place, (key_part, _) in enumerate(pieces):
                one = lax.dot_general(
                    query, key_part, (((1,), (1,)), ((), ())), preferred_element_type=jnp.float32)
                if with_cache and place == 0:
                    one = one + line
                elif causal:
                    r = lax.broadcasted_iota(jnp.int32, one.shape, 0)
                    c = lax.broadcasted_iota(jnp.int32, one.shape, 1)
                    one = jnp.where(c <= r, one, NEG_FILL)
                scores.append(one)
            top = jnp.max(functools.reduce(
                jnp.maximum, [one[:, j:j + HD] for one in scores for j in range(0, one.shape[1], HD)]),
                axis=1, keepdims=True)
            if first:
                new = jnp.broadcast_to(top, m_v.shape[1:])
            else:
                old = m_v[i]
                new = jnp.maximum(old, top)
                factor = jnp.exp2((old - new) * scale)
            new_col = new[:, 0:1]
            weighted = None
            lane_sum = None
            for one, (_, value_part) in zip(scores, pieces):
                p = jnp.exp2((one - new_col) * scale)
                term = jnp.dot(p.astype(jnp.bfloat16), value_part, preferred_element_type=jnp.float32)
                weighted = term if weighted is None else weighted + term
                for j in range(0, p.shape[1], HD):
                    piece_sum = p[:, j:j + HD]
                    lane_sum = piece_sum if lane_sum is None else lane_sum + piece_sum
            m_v[i] = new
            if first:
                l_v[i] = lane_sum
                acc_v[i] = weighted
            else:
                l_v[i] = l_v[i] * factor + lane_sum
                acc_v[i] = acc_v[i] * factor + weighted
            return carry

        lax.fori_loop(0, heads, one_head, 0, unroll=2)

    attend(e, True, True, True, True)

    def kv_step(t, carry):
        i = slot_of(t, e, total)
        below = i < e

        @pl.when(below)
        def _():
            n_up(i).wait_recv()
        c_up(i).wait_recv()

        @pl.when(jnp.logical_and(below, has_up))
        def _():
            n_up(i).start()
            c_up(i).start()

        @pl.when(jnp.logical_and(jnp.logical_not(below), has_down))
        def _():
            c_down(i).start()

        @pl.when(below)
        def _():
            attend(i, True, True, False)

        @pl.when(jnp.logical_not(below))
        def _():
            attend(i, True, False, False)

        @pl.when(t == 1)
        def _():
            w_from_side(0)

        @pl.when(t == 3)
        def _():
            w_from_side(1)
        return carry

    lax.fori_loop(1, total, kv_step, 0)

    def gate_step(i, carry):
        flat = cbuf[i, 0, 2 * page_c:2 * page_c + 16, :].astype(jnp.float32)[8:16]
        gate_cols[i] = jnp.concatenate(
            [flat, jnp.zeros((HD - 8, HD), jnp.float32)], axis=0).T
        return carry

    def finish_head(i, carry):
        att[s, :, col(i, HD)] = (
            acc_v[i] / jnp.sum(l_v[i], axis=1, keepdims=True)).astype(jnp.bfloat16)
        return carry

    lax.fori_loop(0, heads, finish_head, 0)
    block = 2 * own_rows

    def att_rows(which):
        return att.at[s, pl.ds(pl.multiple_of(which * block, block), block)]

    att_sib = sibling(7, att_rows(1 - h), att_rows(1 - h))
    att_sib.start()
    att_own = sibling(9, att_rows(h), att_rows(h))
    att_own.start()
    for copy in w_loads[:2]:
        copy.wait()
    att_sib.wait_recv()

    width = half // tiles
    contract = att.shape[2]

    def project(first_row, j):
        a0 = att[0, pl.ds(pl.multiple_of(first_row, block), block), :]
        a1 = att[1, pl.ds(pl.multiple_of(first_row, block), block), :]
        return jnp.dot(a0, proj_w[0:contract, col(j, width)], preferred_element_type=jnp.float32) + jnp.dot(
            a1, proj_w[contract:2 * contract, col(j, width)], preferred_element_type=jnp.float32)

    def p_side(j):
        return remote(P_SIDE, j, P_IN, j, part_out.at[j], part_in.at[j], {"hd": 1 - h})

    def project_theirs(j, carry):
        part_out[j] = project((1 - h) * block, j).astype(jnp.bfloat16)
        p_side(j).start()
        return carry

    lax.fori_loop(0, tiles, project_theirs, 0)
    w_from_part(0)
    att_own.wait_recv()

    def project_keep(j, carry):
        proj_f[j] = project(h * block, j)
        return carry

    lax.fori_loop(0, tiles, project_keep, 0)
    lax.fori_loop(0, total, gate_step, 0)
    w_from_side(2)

    def hidden_tile(j, carry):
        p_side(j).wait_recv()
        res_v[:, col(j, width)] = (
            res_v[:, col(j, width)].astype(jnp.float32)
            + (proj_f[j] + part_in[j].astype(jnp.float32))).astype(jnp.bfloat16)
        return carry

    lax.fori_loop(0, tiles, hidden_tile, 0)

    def my_rows(which):
        return pl.ds(pl.multiple_of(which * own_rows, own_rows), own_rows)

    hid_sib = sibling(8, res_v.at[my_rows(1 - s)], hid.at[s])
    hid_sib.start()
    hid[s] = res_v[my_rows(s), :]
    hid_sib.wait_recv()
    h0 = hid[0].astype(jnp.float32)
    h1 = hid[1].astype(jnp.float32)
    square = jnp.sum(h0 * h0, axis=1, keepdims=True) + jnp.sum(h1 * h1, axis=1, keepdims=True)
    inverse = lax.rsqrt(square / features + EPSILON)
    g = gain_v[...].astype(jnp.float32).reshape(1, features)
    rows[e, :, 0:half] = (h0 * inverse * g[0:1, 0:half]).astype(jnp.bfloat16)
    rows[e, :, half:features] = (h1 * inverse * g[0:1, half:features]).astype(jnp.bfloat16)
    for copy in w_loads[2:]:
        copy.wait()
    for copy in w_sib:
        copy.wait_recv()

    def x_up(i):
        return remote(X_UP, i, X_IN, i, rows.at[i], rows.at[i], {"ep": e + 1})

    def x_down(i):
        return remote(X_DOWN, i, X_IN, i, rows.at[i], rows.at[i], {"ep": e - 1})

    def z_up(i, c):
        place = i + c * (total + 1)
        return remote(Z_UP, place, Z_IN, place, results.at[i, c], chain_in.at[i, c], {"ep": e + 1})

    def z_down(i, c):
        slot = jnp.where(i == e - 1, total, i)
        return remote(Z_DOWN, i + c * (total + 1), Z_IN, slot + c * (total + 1),
                      results.at[i, c], chain_in.at[slot, c], {"ep": e - 1})

    @pl.when(has_up)
    def _():
        x_up(e).start()

    @pl.when(has_down)
    def _():
        x_down(e).start()

    w_from_part(1)
    for piece in range(2):
        for which in range(2):
            w_near(piece, which).wait_recv()

    units = 2 * wgu.shape[3]
    dims = (((1,), (1,)), ((), ()))
    down_width = features // 4

    def arrive(step):
        n = slot_of(step, e, total)
        below = n < e
        x_up(n).wait_recv()

        @pl.when(jnp.logical_and(below, has_up))
        def _():
            x_up(n).start()

        @pl.when(jnp.logical_and(jnp.logical_not(below), has_down))
        def _():
            x_down(n).start()

    middle = jnp.logical_and(has_up, has_down)

    def expert_step(t, carry):
        i = slot_of(t, e, total)
        x = rows[i]
        activations = []
        for which in range(2):
            gate_part = lax.dot_general(
                x, wgu[which, 0].reshape(units, features), dims, preferred_element_type=jnp.float32)
            up_part = lax.dot_general(
                x, wgu[which, 1].reshape(units, features), dims, preferred_element_type=jnp.float32)
            activations.append(
                (gate_part / (1.0 + jnp.exp(-gate_part)) * up_part).astype(jnp.bfloat16))
        gates_all = gate_cols[i, my_rows(s), :]
        gate_lane = lax.broadcasted_iota(jnp.int32, gates_all.shape, 1)
        weight = [
            jnp.sum(jnp.where(gate_lane == 2 * e + which, gates_all, 0.0), axis=1, keepdims=True)
            for which in range(2)
        ]
        @pl.when(t == 0)
        def _():
            w_from_part(2)
            for which in range(2):
                w_near(2, which).wait_recv()

        for c in range(2):
            for j in range(2):
                span = slice((2 * c + j) * down_width, (2 * c + j + 1) * down_width)
                mixed = None
                for which in range(2):
                    piece = weight[which] * jnp.dot(
                        activations[which], wgu[which, 2, :, :, span].reshape(units, down_width),
                        preferred_element_type=jnp.float32)
                    mixed = piece if mixed is None else mixed + piece
                results[i, c, :, j * down_width:(j + 1) * down_width] = mixed.astype(jnp.bfloat16)

            @pl.when(jnp.logical_and(i > e, jnp.logical_not(has_down)))
            def _():
                z_up(i, c).start()

            @pl.when(jnp.logical_and(i < e, jnp.logical_not(has_up)))
            def _():
                z_down(i, c).start()

        @pl.when(t < jnp.where(middle, 1, last))
        def _():
            arrive(t + 1)

        @pl.when(jnp.logical_and(middle, t < last - 1))
        def _():
            arrive(t + 2)
        return carry

    lax.fori_loop(0, total, expert_step, 0)

    def add_chain(i, c):
        z_up(i, c).wait_recv()
        results[i, c] = (
            results[i, c].astype(jnp.float32) + chain_in[i, c].astype(jnp.float32)
        ).astype(jnp.bfloat16)

    def pass_up(i):
        @pl.when(jnp.logical_and(i <= last, has_down))
        def _():
            for c in range(2):
                add_chain(i, c)
                z_up(i, c).start()

    def pass_down(i):
        @pl.when(jnp.logical_and(i >= 0, has_up))
        def _():
            for c in range(2):
                add_chain(i, c)
                z_down(i, c).start()

    low_side = e < total // 2
    for phase in range(2):
        def chain_step(j, carry):
            up_now = low_side if phase == 0 else jnp.logical_not(low_side)

            @pl.when(up_now)
            def _():
                pass_up(e + j)

            @pl.when(jnp.logical_not(up_now))
            def _():
                pass_down(e - j)
            return carry

        lax.fori_loop(1, total, chain_step, 0)

    for c in range(2):
        @pl.when(has_down)
        def _():
            z_up(e, c).wait_recv()

        @pl.when(has_up)
        def _():
            place = total + c * (total + 1)
            remote(Z_UP, place, Z_IN, place, chain_in.at[total, c], chain_in.at[total, c],
                   {"ep": e + 1}).wait_recv()

    def side_sum(c):
        value = results[e, c].astype(jnp.float32)
        up_value = chain_in[e, c].astype(jnp.float32)
        down_value = chain_in[total, c].astype(jnp.float32)
        value = value + jnp.where(has_down, up_value, 0.0)
        return value + jnp.where(has_up, down_value, 0.0)

    first_half = (hid[0].astype(jnp.float32) + side_sum(0)).astype(jnp.bfloat16)
    second_half = (hid[1].astype(jnp.float32) + side_sum(1)).astype(jnp.bfloat16)
    is_first = s == 0
    out[s] = jnp.where(is_first, first_half, second_half)
    hid_out[...] = jnp.where(is_first, second_half, first_half)
    out_sib = sibling(16, hid_out, out.at[s])
    out_sib.start()
    out_sib.wait_recv()

    for piece in range(3):
        w_side(piece).wait_send()
        w_part(piece).wait_send()
        w_near(piece, 0).wait_send()
        w_near(piece, 1).wait_send()
    for copy in kv_sib + w_sib + [att_sib, att_own, hid_sib, out_sib]:
        copy.wait_send()

    def drain_tile(j, carry):
        p_side(j).wait_send()
        return carry

    lax.fori_loop(0, tiles, drain_tile, 0)

    def drain(i, carry):
        @pl.when(jnp.logical_and(i <= e, has_up))
        def _():
            n_up(i).wait_send()
            c_up(i).wait_send()
            x_up(i).wait_send()

        @pl.when(jnp.logical_and(i >= e, has_down))
        def _():
            c_down(i).wait_send()
            x_down(i).wait_send()

        @pl.when(i > e)
        def _():
            z_up(i, 0).wait_send()
            z_up(i, 1).wait_send()

        @pl.when(i < e)
        def _():
            z_down(i, 0).wait_send()
            z_down(i, 1).wait_send()
        return carry

    lax.fori_loop(0, total, drain, 0)


def fused_shards(
    queries, cache_keys, cache_values, page_len, new_keys, new_values, out_proj, residual,
    norm_gain, gate_up, w_down, expert_ids, gates,
):
    total = lax.axis_size("ep")
    all_experts = total * lax.axis_size("hd")
    query_rows = queries.shape[0]
    heads = queries.shape[1] // HD // 2
    block_rows, half = residual.shape
    features = 2 * half
    own_rows = block_rows // 2
    page_c, page = cache_keys.shape[0], new_keys.shape[0]
    hidden = w_down.shape[1]
    tiles = 4
    slots = max(2 * (total + 1), tiles)
    anywhere = pl.BlockSpec(memory_space=pl.ANY)
    vmem = pl.BlockSpec(memory_space=pltpu.VMEM)
    bf, f32 = jnp.bfloat16, jnp.float32
    out = pl.pallas_call(
        functools.partial(layer_kernel, total, tiles),
        out_shape=jax.ShapeDtypeStruct((2, own_rows, half), bf),
        in_specs=[pl.BlockSpec(memory_space=pltpu.SMEM)] + [anywhere] * 7 + [vmem] + [anywhere] * 2
        + [vmem] * 2,
        out_specs=pl.BlockSpec(memory_space=pltpu.VMEM),
        scratch_shapes=[
            pltpu.VMEM((heads, query_rows, HD), bf),
            pltpu.VMEM((total, 2, 2 * page_c + 16, HD), bf),
            pltpu.VMEM((total, 2, 2 * page, HD), bf),
            pltpu.VMEM((heads, query_rows, HD), f32),
            pltpu.VMEM((heads, query_rows, HD), f32),
            pltpu.VMEM((heads, query_rows, HD), f32),
            pltpu.VMEM((2, query_rows, heads * HD), bf),
            pltpu.VMEM(out_proj.shape, bf),
            pltpu.VMEM((tiles, block_rows, half // tiles), bf),
            pltpu.VMEM((tiles, block_rows, half // tiles), bf),
            pltpu.VMEM((block_rows, half), bf),
            pltpu.VMEM((2, own_rows, half), bf),
            pltpu.VMEM((2, 3, 2, hidden, features), bf),
            pltpu.VMEM((total, own_rows, features), bf),
            pltpu.VMEM((total, 2, own_rows, half), bf),
            pltpu.VMEM((total + 1, 2, own_rows, half), bf),
            pltpu.SemaphoreType.DMA((10, slots)),
            pltpu.SemaphoreType.DMA((7, slots)),
            pltpu.SemaphoreType.DMA((16 + heads,)),
            pltpu.SemaphoreType.DMA((SIB_COUNT,)),
            pltpu.SemaphoreType.DMA((SIB_COUNT,)),
            pltpu.VMEM((tiles, block_rows, half // tiles), f32),
            pltpu.VMEM((own_rows, half), bf),
            pltpu.VMEM((total, 2 * own_rows, 128), f32),
        ],
        compiler_params=pltpu.CompilerParams(
            collective_id=0, has_side_effects=True, vmem_limit_bytes=58 * 1024 * 1024
        ),
    )(page_len, queries, cache_keys, cache_values, new_keys, new_values, out_proj, residual,
      norm_gain, gate_up, w_down, expert_ids.T, gates.T)
    return out.reshape(block_rows, half)


def layer(*arguments):
    queries, page_rows, ids = arguments[0], arguments[4].shape[0], arguments[11]
    pair = lax.axis_size("ep") >= 4 and lax.axis_size("grp") == 2
    pair = pair and lax.axis_size("hd") == 2 and lax.axis_size("sub") == 2
    slots = block_sizes(ids.shape[0], lax.axis_size("ep"), lax.axis_size("hd"))[1]
    group_width = QH // KVH
    whole_heads = queries.shape[1] == 2 * group_width * HD
    whole_pages = page_rows == 128 and arguments[1].shape[0] == 128
    rows_fit = queries.shape[0] == 2 * page_rows and ids.shape == (128, 8)
    rows_fit = rows_fit and lax.axis_size("ep") == 4
    if pair and slots == ids.shape[0] and whole_heads and whole_pages and rows_fit:
        return fused_shards(*arguments)
    return shards(*arguments)


def solution(mesh):
    return jax.shard_map(
        layer,
        mesh=mesh,
        in_specs=(
            P(("grp", "ep"), "hd"),
            P(("grp", "ep", "sub"), None),
            P(("grp", "ep", "sub"), None),
            P(("grp", "ep", "sub")),
            P(("grp", "ep", "sub"), None),
            P(("grp", "ep", "sub"), None),
            P("hd", "sub"),
            P(("grp", "ep", "hd"), "sub"),
            P(),
            P(("ep", "hd"), None, "sub", None),
            P(("ep", "hd"), "sub", None),
            P(("grp", "ep", "hd"), None),
            P(("grp", "ep", "hd"), None),
        ),
        out_specs=P(("grp", "ep", "hd"), "sub"),
        check_vma=False,
    )
```

```python
import functools
import math

import jax
import jax.numpy as jnp
from jax import lax
from jax.experimental import pallas as pl
from jax.experimental.pallas import tpu as pltpu
from jax.sharding import PartitionSpec as P

QH = 32
KVH = 4
HD = 128
GROUPS_ROW = 4


NEG_FILL = -1e30
EPSILON = 1e-06
KEY_BLOCK = 1024
FAR_RANK = 1073741824
MESH = pl.DeviceIdType.MESH


def joined(x, axis, join):
    gathered = jax.tree.map(
        lambda a, kind: lax.all_gather(a.astype(kind), axis),
        x,
        jax.tree.map(lambda a: jnp.bfloat16 if a.dtype == jnp.float32 else a.dtype, x),
    )

    def take(source):
        return jax.tree.map(
            lambda a, own: lax.dynamic_index_in_dim(a, source, 0, False).astype(own.dtype),
            gathered,
            x,
        )

    return lax.fori_loop(
        1, lax.axis_size(axis), lambda source, state: join(state, take(source)), take(0)
    )


def block_sizes(block_rows, group_total, experts_group):
    group_slots = min(block_rows, 3 * GROUPS_ROW * block_rows // (2 * group_total))
    return (group_slots, 2 * group_slots // experts_group)


def attend_block(fold_state, packed, key_rank, query_heads, row_ids, kv_heads):
    running_max, weight_sum, weighted = fold_state
    half_cols = packed.shape[1] // 2
    length = packed.shape[0]
    key_part = packed[:, :half_cols].reshape(length, kv_heads, half_cols // kv_heads)
    value_part = packed[:, half_cols:].reshape(length, kv_heads, half_cols // kv_heads)
    scores = jnp.einsum(
        "rkqd,lkd->rkql", query_heads, key_part, preferred_element_type=jnp.float32
    ) * (1.0 / math.sqrt(HD))
    allowed = (key_rank[None, :] <= row_ids[:, None])[:, None, None, :]
    masked = jnp.where(allowed, scores, NEG_FILL)
    new_max = jnp.maximum(running_max, jnp.max(masked, axis=3))
    factor = jnp.exp(running_max - new_max)
    exp_terms = jnp.where(allowed, jnp.exp(scores - new_max[..., None]), 0.0)
    weight_sum = weight_sum * factor + jnp.sum(exp_terms, axis=3)
    weighted = weighted * factor[..., None] + jnp.einsum(
        "rkql,lkd->rkqd",
        exp_terms.astype(jnp.bfloat16),
        value_part,
        preferred_element_type=jnp.float32,
    )
    return (new_max, weight_sum, weighted)


def join_parts(first_part, second_part):
    first_max, first_sum, first_weighted = first_part
    second_max, second_sum, second_weighted = second_part
    joint_max = jnp.maximum(first_max, second_max)
    first_factor = jnp.exp(first_max - joint_max)
    second_factor = jnp.exp(second_max - joint_max)
    joint_sum = first_sum * first_factor + second_sum * second_factor
    joint_weighted = (
        first_weighted * first_factor[..., None] + second_weighted * second_factor[..., None]
    )
    return (joint_max, joint_sum, joint_weighted)


def shards(
    queries,
    cache_keys,
    cache_values,
    page_len,
    new_keys,
    new_values,
    out_proj,
    residual,
    norm_gain,
    gate_up,
    w_down,
    expert_ids,
    gates,
):
    query_rows = queries.shape[0]
    heads_here = queries.shape[1] // HD
    group_width = QH // KVH
    kv_heads = max(1, heads_here // group_width)
    per_kv = heads_here // kv_heads
    kv_first = lax.axis_index("hd") * heads_here // group_width

    def kv_columns(source):
        return lax.dynamic_slice_in_dim(source, kv_first * HD, kv_heads * HD, 1)

    local_keys = jnp.concatenate([kv_columns(cache_keys), kv_columns(new_keys)], axis=0)
    local_values = jnp.concatenate([kv_columns(cache_values), kv_columns(new_values)], axis=0)
    packed_local = jnp.concatenate([local_keys, local_values], axis=1)
    cache_rows = cache_keys.shape[0]
    new_rows = new_keys.shape[0]
    cache_rank = jnp.where(
        jnp.arange(cache_rows, dtype=jnp.int32) < page_len[0], -1, FAR_RANK
    ).astype(jnp.int32)
    new_block = lax.axis_index("ep") * lax.axis_size("sub") + lax.axis_index("sub")
    new_rank = new_block * new_rows + jnp.arange(new_rows, dtype=jnp.int32)
    rank_local = jnp.concatenate([cache_rank, new_rank], axis=0)
    row_ids = lax.axis_index("ep") * query_rows + jnp.arange(query_rows, dtype=jnp.int32)
    query_heads = queries.reshape(query_rows, kv_heads, per_kv, HD)

    def fold_keys(fold_state, piece_data):
        packed, key_rank = piece_data
        length = packed.shape[0]
        if length > KEY_BLOCK and length % KEY_BLOCK == 0:
            block_count = length // KEY_BLOCK

            def scan_step(inner_state, block_data):
                return (
                    attend_block(
                        inner_state, block_data[0], block_data[1], query_heads, row_ids, kv_heads
                    ),
                    None,
                )

            fold_state, _ = lax.scan(
                scan_step,
                fold_state,
                (
                    packed.reshape(block_count, KEY_BLOCK, packed.shape[1]),
                    key_rank.reshape(block_count, KEY_BLOCK),
                ),
            )
            return fold_state
        return attend_block(fold_state, packed, key_rank, query_heads, row_ids, kv_heads)

    start_state = (
        jnp.full((query_rows, kv_heads, per_kv), NEG_FILL, jnp.float32),
        jnp.zeros((query_rows, kv_heads, per_kv), jnp.float32),
        jnp.zeros((query_rows, kv_heads, per_kv, HD), jnp.float32),
    )
    fold_state = fold_keys(
        start_state,
        (
            lax.all_gather(packed_local, "ep", axis=0, tiled=True),
            lax.all_gather(rank_local, "ep", axis=0, tiled=True),
        ),
    )
    running_max, weight_sum, weighted = joined(fold_state, "sub", join_parts)
    attended = (
        (weighted / weight_sum[..., None]).reshape(query_rows, heads_here * HD).astype(jnp.bfloat16)
    )
    projected = lax.psum_scatter(
        jnp.dot(attended, out_proj, preferred_element_type=jnp.float32).astype(jnp.bfloat16),
        "hd",
        scatter_dimension=0,
        tiled=True,
    ).astype(jnp.float32)
    hidden_half = (residual.astype(jnp.float32) + projected).astype(jnp.bfloat16)
    widened = hidden_half.astype(jnp.float32)
    features = norm_gain.shape[0]
    half_width = hidden_half.shape[1]
    square_sum = lax.psum(jnp.sum(widened * widened, axis=1), "sub")
    gain_half = lax.dynamic_slice_in_dim(
        norm_gain, lax.axis_index("sub") * half_width, half_width, 0
    )
    normed = (
        widened
        * lax.rsqrt(square_sum[:, None] / features + EPSILON)
        * gain_half.astype(jnp.float32)
    ).astype(jnp.bfloat16)
    pair_weights = gate_up[0].reshape(-1, features)
    hidden_units = w_down.shape[1]
    group_total = lax.axis_size("ep")
    group_experts = lax.axis_size("hd")
    all_experts = group_total * group_experts
    block_rows = expert_ids.shape[0]
    group_slots, expert_slots = block_sizes(block_rows, group_total, group_experts)
    chosen = (
        expert_ids[:, :, None] == jnp.arange(all_experts, dtype=jnp.int32)[None, None, :]
    ).astype(jnp.int32)
    named_count = jnp.sum(chosen, axis=1)
    earlier = jnp.cumsum(named_count, axis=0) - named_count
    slot_index = jnp.sum(chosen * earlier[:, None, :], axis=2)
    position = expert_ids * expert_slots + slot_index
    slot_columns = jnp.arange(all_experts * expert_slots, dtype=jnp.int32)
    gate_table = jnp.sum(
        jnp.where(
            position[:, :, None] == slot_columns[None, None, :],
            gates.astype(jnp.float32)[:, :, None],
            0.0,
        ),
        axis=1,
    ).astype(jnp.bfloat16)
    placed = (gate_table != 0).astype(jnp.bfloat16)
    outgoing = jnp.einsum("rq,rd->qd", placed, normed, preferred_element_type=jnp.float32).astype(
        jnp.bfloat16
    )
    outgoing = outgoing.reshape(all_experts, expert_slots, normed.shape[1])
    arrived = lax.all_to_all(outgoing, ("ep", "hd"), split_axis=0, concat_axis=0, tiled=True)
    lead_shape = arrived.shape[:-1]
    rows_in = arrived.reshape(-1, arrived.shape[-1])
    rows_in = lax.all_gather(rows_in, "sub", axis=1, tiled=True)
    projected_pair = jnp.einsum(
        "rd,fd->rf", rows_in, pair_weights, preferred_element_type=jnp.float32
    )
    activation = (
        jax.nn.silu(projected_pair[:, :hidden_units]) * projected_pair[:, hidden_units:]
    ).astype(jnp.bfloat16)
    partial_out = jnp.dot(activation, w_down[0], preferred_element_type=jnp.float32)
    expert_out = lax.psum_scatter(
        partial_out.astype(jnp.bfloat16), "sub", scatter_dimension=1, tiled=True
    )
    results = expert_out.reshape(lead_shape + (expert_out.shape[1],))
    returned = lax.all_to_all(results, ("ep", "hd"), split_axis=0, concat_axis=0, tiled=True)
    mixture = jnp.dot(
        gate_table,
        returned.reshape(all_experts * expert_slots, half_width),
        preferred_element_type=jnp.float32,
    )
    return (widened + mixture).astype(jnp.bfloat16)


def slot_of(step, place, total):
    near = jnp.minimum(place, total - 1 - place)
    odd = place - (step + 1) // 2
    even = place + step // 2
    beside = jnp.where(step % 2 == 1, odd, even)
    beyond = jnp.where(place < total - 1 - place, step, total - 1 - step)
    return jnp.where(step <= 2 * near, beside, beyond)


(C_UP, C_DOWN, N_UP, X_UP, X_DOWN, W_SIDE, W_PART, Z_UP, Z_DOWN, P_SIDE) = range(10)
(C_IN, N_IN, X_IN, W_SIDE_IN, W_PART_IN, Z_IN, P_IN) = range(7)
SIB_COUNT = 25
W_PIECES = 6
X_CUTS = 2
Z_CUTS = 4
LOG2_E = math.log2(math.e)


def semaphore_places(total, tiles):
    sent = (total, total, total, X_CUTS * total, X_CUTS * total, W_PIECES, W_PIECES,
            Z_CUTS * total, Z_CUTS * total, tiles)
    arrived = (total, total, X_CUTS * total, W_PIECES, W_PIECES, Z_CUTS * (total + 1), tiles)
    return [[sum(sizes[:i]) for i in range(len(sizes) + 1)] for sizes in (sent, arrived)]


def layer_kernel(
    total, tiles,
    page_len, queries, cache_keys, cache_values, new_keys, new_values, out_proj, residual, gain_v,
    gate_up, w_down, ids_t, gates_t,
    out,
    q_v, cbuf, nbuf, m_v, l_v, acc_v, att, proj_w, part_out, part_in, res_v, hid, wgu,
    rows, results, chain_in,
    send_sem, recv_sem, load_sem, sib_send, sib_recv, proj_f, out_buf, gate_cols,
):
    e = lax.axis_index("ep")
    h = lax.axis_index("hd")
    s = lax.axis_index("sub")
    part = lax.axis_index("grp")
    last = total - 1
    heads = q_v.shape[0]
    page = new_keys.shape[0]
    page_c = cache_keys.shape[0]
    half = out.shape[2]
    own_rows = out.shape[1]
    features = 2 * half
    scale = LOG2_E / math.sqrt(HD)
    has_up = e < last
    sent_at, arrived_at = semaphore_places(total, tiles)
    has_down = e > 0

    def col(index, width):
        return pl.ds(pl.multiple_of(index * width, width), width)

    def local(index, src, dst):
        return pltpu.make_async_copy(src, dst, load_sem.at[index])

    mine = 2 * h + s
    loads = [
        local(0, cache_keys.at[:, col(mine, HD)], cbuf.at[e, s, pl.ds(0, page_c)]),
        local(1, cache_values.at[:, col(mine, HD)], cbuf.at[e, s, pl.ds(page_c, page_c)]),
        local(3, new_keys.at[:, col(mine, HD)], nbuf.at[e, s, pl.ds(0, page)]),
        local(4, new_values.at[:, col(mine, HD)], nbuf.at[e, s, pl.ds(page, page)]),
    ]
    q_loads = [
        local(16 + i, queries.at[:, col(s * heads + i, HD)], q_v.at[i]) for i in range(heads)
    ]
    w_loads = [
        local(5, out_proj, proj_w),
        local(6, residual, res_v),
        local(9, gate_up.at[0], wgu.at[h, pl.ds(0, 2), s]),
        local(10, w_down.at[0], wgu.at[h, 2, s]),
    ]
    for copy in loads + q_loads + w_loads:
        copy.start()

    experts = 2 * total
    lane = lax.broadcasted_iota(jnp.int32, (8, HD), 1)
    seen = jnp.where(lane < page_len[0], 0.0, NEG_FILL)
    ids = ids_t[...]
    gate_values = gates_t[...].astype(jnp.float32)
    place = lax.broadcasted_iota(jnp.int32, (8, HD), 0)
    by_expert = jnp.zeros((8, HD), jnp.float32)
    for x in range(experts):
        one_row = jnp.sum(jnp.where(ids == x, gate_values, 0.0), axis=0, keepdims=True)
        by_expert = jnp.where(place == x, one_row, by_expert)
    cbuf[e, s, 2 * page_c:2 * page_c + 16, :] = jnp.concatenate(
        [seen, by_expert], axis=0).astype(jnp.bfloat16)

    barrier = pltpu.get_barrier_semaphore()
    pl.semaphore_signal(barrier, inc=1, device_id={"sub": 1 - s}, device_id_type=MESH)
    pl.semaphore_signal(barrier, inc=1, device_id={"hd": 1 - h}, device_id_type=MESH)
    pl.semaphore_signal(barrier, inc=1, device_id={"grp": 1 - part}, device_id_type=MESH)

    @pl.when(has_up)
    def _():
        pl.semaphore_signal(barrier, inc=1, device_id={"ep": e + 1}, device_id_type=MESH)

    @pl.when(has_down)
    def _():
        pl.semaphore_signal(barrier, inc=1, device_id={"ep": e - 1}, device_id_type=MESH)

    pl.semaphore_wait(barrier, 3 + has_up.astype(jnp.int32) + has_down.astype(jnp.int32))

    def sibling(index, src, dst):
        return pltpu.make_async_remote_copy(
            src_ref=src, dst_ref=dst, send_sem=sib_send.at[index], recv_sem=sib_recv.at[index],
            device_id={"sub": 1 - s}, device_id_type=MESH)

    def remote(kind, index, arrival, slot, src, dst, where):
        return pltpu.make_async_remote_copy(
            src_ref=src, dst_ref=dst, send_sem=send_sem.at[sent_at[kind] + index],
            recv_sem=recv_sem.at[arrived_at[arrival] + slot], device_id=where, device_id_type=MESH)

    theirs = 2 * h + 1 - s
    kv_sib = [
        sibling(0, cache_keys.at[:, col(theirs, HD)], cbuf.at[e, s, pl.ds(0, page_c)]),
        sibling(1, cache_values.at[:, col(theirs, HD)], cbuf.at[e, s, pl.ds(page_c, page_c)]),
        sibling(2, cbuf.at[e, s, pl.ds(2 * page_c, 16)], cbuf.at[e, s, pl.ds(2 * page_c, 16)]),
        sibling(3, new_keys.at[:, col(theirs, HD)], nbuf.at[e, s, pl.ds(0, page)]),
        sibling(4, new_values.at[:, col(theirs, HD)], nbuf.at[e, s, pl.ds(page, page)]),
    ]
    w_sib = [
        sibling(5, gate_up.at[0], wgu.at[h, pl.ds(0, 2), s]),
        sibling(6, w_down.at[0], wgu.at[h, 2, s]),
    ]
    for copy in kv_sib:
        copy.start()

    cut = wgu.shape[3] // 2
    piece_rows = cut // 2

    def cut_rows(which, piece):
        return pl.ds(pl.multiple_of(which * cut + piece % 2 * piece_rows, piece_rows), piece_rows)

    def w_block(piece, which):
        return wgu.at[1 - h, piece // 2, s, cut_rows(which, piece)]

    def w_side(piece):
        kind = piece // 2
        src = (w_down.at[0, cut_rows(part, piece)] if kind == 2
               else gate_up.at[0, kind, cut_rows(part, piece)])
        return remote(W_SIDE, piece, W_SIDE_IN, piece, src,
                      wgu.at[h, kind, s, cut_rows(part, piece)], {"hd": 1 - h})

    def w_part(piece):
        block_ref = w_block(piece, part)
        return remote(W_PART, piece, W_PART_IN, piece, block_ref, block_ref, {"grp": 1 - part})

    def w_near(piece, which):
        block_ref = w_block(piece, jnp.where(which == 0, part, 1 - part))
        return sibling(11 + 2 * piece + which, block_ref, block_ref)

    def w_from_side(piece):
        block_ref = w_block(piece, part)
        remote(W_SIDE, piece, W_SIDE_IN, piece, block_ref, block_ref, {"hd": 1 - h}).wait_recv()
        w_part(piece).start()
        w_near(piece, 0).start()

    def w_from_part(piece):
        w_part(piece).wait_recv()
        w_near(piece, 1).start()

    for piece in range(W_PIECES):
        w_side(piece).start()

    def c_up(i):
        return remote(C_UP, i, C_IN, i, cbuf.at[i], cbuf.at[i], {"ep": e + 1})

    def c_down(i):
        return remote(C_DOWN, i, C_IN, i, cbuf.at[i], cbuf.at[i], {"ep": e - 1})

    def n_up(i):
        return remote(N_UP, i, N_IN, i, nbuf.at[i], nbuf.at[i], {"ep": e + 1})

    for copy in loads:
        copy.wait()
    for copy in kv_sib:
        copy.wait_recv()

    @pl.when(has_up)
    def _():
        n_up(e).start()
        c_up(e).start()

    @pl.when(has_down)
    def _():
        c_down(e).start()

    for copy in w_sib:
        copy.start()
    for copy in q_loads:
        copy.wait()

    def parts_of(buf, index, size):
        return (buf[index, :, 0:size, :].reshape(2 * size, HD),
                buf[index, :, size:2 * size, :].reshape(2 * size, HD))

    def attend(index, with_cache, with_new, causal, first=False):
        pieces = []
        if with_cache:
            pieces.append(parts_of(cbuf, index, page_c))
            line = jnp.concatenate(
                [cbuf[index, 0, 2 * page_c:2 * page_c + 16, :],
                 cbuf[index, 1, 2 * page_c:2 * page_c + 16, :]], axis=1)[0:1].astype(jnp.float32)
        if with_new:
            pieces.append(parts_of(nbuf, index, page))

        def one_head(i, carry):
            query = q_v[i]
            scores = []
            for place, (key_part, _) in enumerate(pieces):
                one = lax.dot_general(
                    query, key_part, (((1,), (1,)), ((), ())), preferred_element_type=jnp.float32)
                if with_cache and place == 0:
                    one = one + line
                elif causal:
                    r = lax.broadcasted_iota(jnp.int32, one.shape, 0)
                    c = lax.broadcasted_iota(jnp.int32, one.shape, 1)
                    one = jnp.where(c <= r, one, NEG_FILL)
                scores.append(one)
            top = jnp.max(functools.reduce(
                jnp.maximum, [one[:, j:j + HD] for one in scores for j in range(0, one.shape[1], HD)]),
                axis=1, keepdims=True)
            if first:
                new = jnp.broadcast_to(top, m_v.shape[1:])
            else:
                old = m_v[i]
                new = jnp.maximum(old, top)
                factor = jnp.exp2((old - new) * scale)
            new_col = new[:, 0:1]
            weighted = None
            lane_sum = None
            for one, (_, value_part) in zip(scores, pieces):
                p = jnp.exp2((one - new_col) * scale)
                term = jnp.dot(p.astype(jnp.bfloat16), value_part, preferred_element_type=jnp.float32)
                weighted = term if weighted is None else weighted + term
                for j in range(0, p.shape[1], HD):
                    piece_sum = p[:, j:j + HD]
                    lane_sum = piece_sum if lane_sum is None else lane_sum + piece_sum
            m_v[i] = new
            if first:
                l_v[i] = lane_sum
                acc_v[i] = weighted
            else:
                l_v[i] = l_v[i] * factor + lane_sum
                acc_v[i] = acc_v[i] * factor + weighted
            return carry

        lax.fori_loop(0, heads, one_head, 0, unroll=8)

    attend(e, True, True, True, True)

    middle = jnp.logical_and(has_up, has_down)
    low_side = e < total // 2

    def kv_arrive(t):
        @pl.when(jnp.logical_not(middle))
        def _():
            i = slot_of(t, e, total)

            @pl.when(i < e)
            def _():
                n_up(i).wait_recv()
            c_up(i).wait_recv()

        @pl.when(jnp.logical_and(middle, t == 1))
        def _():
            n_up(e - 1).wait_recv()
            n_up(e - 1).start()
            c_down(e + 1).wait_recv()
            c_down(e + 1).start()
            c_up(e - 1).wait_recv()
            c_up(e - 1).start()

        @pl.when(jnp.logical_and(jnp.logical_and(middle, low_side), t == 2))
        def _():
            c_down(last).wait_recv()
            c_down(last).start()

        @pl.when(jnp.logical_and(middle, jnp.logical_not(low_side)))
        def _():
            @pl.when(t == 2)
            def _():
                n_up(0).wait_recv()
                n_up(0).start()

            @pl.when(t == 3)
            def _():
                c_up(0).wait_recv()
                c_up(0).start()

    def kv_step(t, carry):
        i = slot_of(t, e, total)
        below = i < e
        kv_arrive(t)

        @pl.when(t == 1)
        def _():
            w_from_side(0)

        @pl.when(jnp.logical_and(t == 3, jnp.logical_not(middle)))
        def _():
            w_from_side(3)

        @pl.when(below)
        def _():
            attend(i, True, True, False)

        @pl.when(jnp.logical_not(below))
        def _():
            attend(i, True, False, False)

        @pl.when(t == 1)
        def _():
            w_from_side(1)

        @pl.when(t == 2)
        def _():
            w_from_side(2)

        @pl.when(t == 3)
        def _():
            @pl.when(middle)
            def _():
                w_from_side(3)
            w_from_part(0)
        return carry

    lax.fori_loop(1, total, kv_step, 0)

    def gate_step(i, carry):
        flat = cbuf[i, 0, 2 * page_c:2 * page_c + 16, :].astype(jnp.float32)[8:16]
        gate_cols[i] = jnp.concatenate(
            [flat, jnp.zeros((HD - 8, HD), jnp.float32)], axis=0).T
        return carry

    def finish_head(i, carry):
        att[s, :, col(i, HD)] = (
            acc_v[i] / jnp.sum(l_v[i], axis=1, keepdims=True)).astype(jnp.bfloat16)
        return carry

    lax.fori_loop(0, heads, finish_head, 0)
    block = 2 * own_rows

    def att_rows(which):
        return att.at[s, pl.ds(pl.multiple_of(which * block, block), block)]

    att_sib = sibling(7, att_rows(1 - h), att_rows(1 - h))
    att_sib.start()
    att_own = sibling(9, att_rows(h), att_rows(h))
    att_own.start()
    for copy in w_loads[:2]:
        copy.wait()
    att_sib.wait_recv()

    width = half // tiles
    side_width = half // (tiles // X_CUTS)
    contract = att.shape[2]

    x_rows = own_rows // X_CUTS

    def x_cut(i, k):
        return rows.at[i, pl.ds(k * x_rows, x_rows)]

    def x_up(i, k):
        return remote(X_UP, X_CUTS * i + k, X_IN, X_CUTS * i + k, x_cut(i, k), x_cut(i, k),
                      {"ep": e + 1})

    def x_down(i, k):
        return remote(X_DOWN, X_CUTS * i + k, X_IN, X_CUTS * i + k, x_cut(i, k), x_cut(i, k),
                      {"ep": e - 1})

    def z_up(i, c):
        place = i + c * (total + 1)
        return remote(Z_UP, i + c * total, Z_IN, place, results.at[i, c], chain_in.at[i, c], {"ep": e + 1})

    def z_down(i, c):
        slot = jnp.where(i == e - 1, total, i)
        return remote(Z_DOWN, i + c * total, Z_IN, slot + c * (total + 1),
                      results.at[i, c], chain_in.at[slot, c], {"ep": e - 1})

    def project(a0, a1, j, size):
        return jnp.dot(
            a0, proj_w[0:contract, col(j, size)], preferred_element_type=jnp.float32
        ) + jnp.dot(
            a1, proj_w[contract:2 * contract, col(j, size)], preferred_element_type=jnp.float32)

    def p_side(j):
        return remote(P_SIDE, j, P_IN, j, part_out.at[j], part_in.at[j], {"hd": 1 - h})

    def project_theirs(j, carry):
        first = (1 - h) * block + j // (tiles // X_CUTS) * x_rows
        a0, a1 = [
            jnp.concatenate([
                att[which, pl.ds(pl.multiple_of(first + u * own_rows, x_rows), x_rows), :]
                for u in range(2)], axis=0)
            for which in range(2)]
        part_out[j] = project(a0, a1, j % (tiles // X_CUTS), side_width).astype(jnp.bfloat16)
        p_side(j).start()
        return carry

    lax.fori_loop(0, tiles, project_theirs, 0)
    w_from_side(4)
    w_from_part(1)
    att_own.wait_recv()

    def project_keep(j, carry):
        own = pl.ds(pl.multiple_of(h * block, block), block)
        proj_f[:, col(j, width)] = project(att[0, own, :], att[1, own, :], j, width)
        return carry

    lax.fori_loop(0, tiles, project_keep, 0)
    lax.fori_loop(0, total, gate_step, 0)
    w_from_side(5)
    w_from_part(2)
    w_from_part(3)

    def my_rows(which):
        return pl.ds(pl.multiple_of(which * own_rows, own_rows), own_rows)

    def my_cut(which, k):
        return pl.ds(pl.multiple_of(which * own_rows + k * x_rows, x_rows), x_rows)

    def hid_sib(k):
        return sibling(8 + 2 * k, res_v.at[my_cut(1 - s, k)], hid.at[s, pl.ds(k * x_rows, x_rows)])

    for copy in w_loads[2:]:
        copy.wait()
    for copy in w_sib:
        copy.wait_recv()
    g = gain_v[...].astype(jnp.float32).reshape(1, features)
    for k in range(X_CUTS):
        for j in range(tiles // X_CUTS):
            place = k * (tiles // X_CUTS) + j
            span = slice(j * side_width, (j + 1) * side_width)
            p_side(place).wait_recv()
            for u in range(2):
                cut_u = slice(u * own_rows + k * x_rows, u * own_rows + (k + 1) * x_rows)
                res_v[cut_u, span] = (
                    res_v[cut_u, span].astype(jnp.float32)
                    + (proj_f[cut_u, span]
                       + part_in[place, u * x_rows:(u + 1) * x_rows, :].astype(jnp.float32))
                ).astype(jnp.bfloat16)
        hid_sib(k).start()
        at_k = slice(k * x_rows, (k + 1) * x_rows)
        hid[s, at_k] = res_v[my_cut(s, k), :]
        hid_sib(k).wait_recv()
        h0 = hid[0, at_k].astype(jnp.float32)
        h1 = hid[1, at_k].astype(jnp.float32)
        square = jnp.sum(h0 * h0, axis=1, keepdims=True) + jnp.sum(h1 * h1, axis=1, keepdims=True)
        inverse = lax.rsqrt(square / features + EPSILON)
        rows[e, at_k, 0:half] = (h0 * inverse * g[0:1, 0:half]).astype(jnp.bfloat16)
        rows[e, at_k, half:features] = (h1 * inverse * g[0:1, half:features]).astype(jnp.bfloat16)

        @pl.when(has_up)
        def _():
            x_up(e, k).start()

        @pl.when(has_down)
        def _():
            x_down(e, k).start()

    w_from_part(4)
    units = 2 * wgu.shape[3]
    dims = (((1,), (1,)), ((), ()))
    down_width = features // Z_CUTS

    def turn(k):
        return Z_CUTS // 2 * jnp.where(k < Z_CUTS // 2, 1 - s, s) + k % (Z_CUTS // 2)

    def arrive_near(k):
        @pl.when(middle)
        def _():
            x_up(e - 1, k).wait_recv()
            x_up(e - 1, k).start()
            x_down(e + 1, k).wait_recv()
            x_down(e + 1, k).start()

    def arrive(t):
        @pl.when(jnp.logical_and(jnp.logical_not(middle), t > 0))
        def _():
            for k in range(X_CUTS):
                x_up(slot_of(t, e, total), k).wait_recv()

        @pl.when(t == 1)
        def _():
            for k in range(X_CUTS):
                arrive_near(k)

    def arrive_far(t):
        for k in range(X_CUTS):
            @pl.when(jnp.logical_and(middle, t == 1 + k))
            def _():
                @pl.when(low_side)
                def _():
                    x_down(last, k).wait_recv()
                    x_down(last, k).start()

                @pl.when(jnp.logical_not(low_side))
                def _():
                    x_up(0, k).wait_recv()
                    x_up(0, k).start()

    def expert_step(t, carry):
        i = slot_of(t, e, total)

        @pl.when(t == 0)
        def _():
            for piece in range(4):
                for which in range(2):
                    w_near(piece, which).wait_recv()

        arrive(t)
        x = rows[i]
        activations = []
        for which in range(2):
            gate_part = lax.dot_general(
                x, wgu[which, 0].reshape(units, features), dims, preferred_element_type=jnp.float32)
            up_part = lax.dot_general(
                x, wgu[which, 1].reshape(units, features), dims, preferred_element_type=jnp.float32)
            activations.append(
                (gate_part / (1.0 + jnp.exp(-gate_part)) * up_part).astype(jnp.bfloat16))
        gates_all = gate_cols[i, my_rows(s), :]
        gate_lane = lax.broadcasted_iota(jnp.int32, gates_all.shape, 1)
        weight = [
            jnp.sum(jnp.where(gate_lane == 2 * e + which, gates_all, 0.0), axis=1, keepdims=True)
            for which in range(2)
        ]

        arrive_far(t)

        @pl.when(t == 0)
        def _():
            w_from_part(5)
            for piece in range(4, 6):
                for which in range(2):
                    w_near(piece, which).wait_recv()

        for k in range(Z_CUTS):
            c = turn(k)
            mixed = None
            for which in range(2):
                piece = weight[which] * jnp.dot(
                    activations[which],
                    wgu[which, 2, :, :, col(c, down_width)].reshape(units, down_width),
                    preferred_element_type=jnp.float32)
                mixed = piece if mixed is None else mixed + piece
            results[i, c] = mixed.astype(jnp.bfloat16)

            @pl.when(jnp.logical_and(i > e, jnp.logical_not(has_down)))
            def _():
                z_up(i, c).start()

            @pl.when(jnp.logical_and(i < e, jnp.logical_not(has_up)))
            def _():
                z_down(i, c).start()
        return carry

    lax.fori_loop(0, total, expert_step, 0)

    def add_chain(i, c):
        z_up(i, c).wait_recv()
        results[i, c] = (
            results[i, c].astype(jnp.float32) + chain_in[i, c].astype(jnp.float32)
        ).astype(jnp.bfloat16)

    def relay_up(i, k):
        c = turn(k)
        add_chain(i, c)
        z_up(i, c).start()

    def relay_down(i, k):
        c = turn(k)
        add_chain(i, c)
        z_down(i, c).start()

    @pl.when(jnp.logical_and(middle, low_side))
    def _():
        for k in range(Z_CUTS):
            relay_up(e + 1, k)
        for k in range(Z_CUTS + 2):
            if k < Z_CUTS:
                relay_up(last, k)
            if k >= 2:
                relay_down(0, k - 2)

    @pl.when(jnp.logical_and(middle, jnp.logical_not(low_side)))
    def _():
        for k in range(Z_CUTS):
            relay_down(e - 1, k)
        for k in range(Z_CUTS + 2):
            if k < Z_CUTS:
                relay_down(0, k)
            if k >= 2:
                relay_up(last, k - 2)

    def out_sib(q):
        return sibling(23 + q, out_buf.at[0, q], out.at[s, :, pl.ds(q * down_width, down_width)])

    def out_local(q):
        return local(7 + q, out_buf.at[1, q], out.at[s, :, pl.ds(q * down_width, down_width)])

    for k in range(Z_CUTS):
        c = turn(k)
        q = k % 2

        @pl.when(has_down)
        def _():
            z_up(e, c).wait_recv()

        @pl.when(has_up)
        def _():
            place = total + c * (total + 1)
            block_ref = chain_in.at[total, c]
            remote(Z_UP, 0, Z_IN, place, block_ref, block_ref, {"ep": e + 1}).wait_recv()
        side = jnp.where(k < Z_CUTS // 2, 1 - s, s)
        value = results[e, c].astype(jnp.float32)
        value = value + jnp.where(has_down, chain_in[e, c].astype(jnp.float32), 0.0)
        value = value + jnp.where(has_up, chain_in[total, c].astype(jnp.float32), 0.0)
        value = hid[side, :, q * down_width:(q + 1) * down_width].astype(jnp.float32) + value
        out_buf[k // 2, q] = value.astype(jnp.bfloat16)
        if k < Z_CUTS // 2:
            out_sib(q).start()
        else:
            out_local(q).start()
    for q in range(2):
        out_sib(q).wait_recv()
        out_local(q).wait()

    for piece in range(W_PIECES):
        w_side(piece).wait_send()
        w_part(piece).wait_send()
        w_near(piece, 0).wait_send()
        w_near(piece, 1).wait_send()
    for copy in kv_sib + w_sib + [att_sib, att_own, hid_sib(0), hid_sib(1), out_sib(0), out_sib(1)]:
        copy.wait_send()

    def drain_tile(j, carry):
        p_side(j).wait_send()
        return carry

    lax.fori_loop(0, tiles, drain_tile, 0)

    def drain(i, carry):
        @pl.when(jnp.logical_and(i <= e, has_up))
        def _():
            n_up(i).wait_send()
            c_up(i).wait_send()
            for k in range(X_CUTS):
                x_up(i, k).wait_send()

        @pl.when(jnp.logical_and(i >= e, has_down))
        def _():
            c_down(i).wait_send()
            for k in range(X_CUTS):
                x_down(i, k).wait_send()

        @pl.when(i > e)
        def _():
            for c in range(Z_CUTS):
                z_up(i, c).wait_send()

        @pl.when(i < e)
        def _():
            for c in range(Z_CUTS):
                z_down(i, c).wait_send()
        return carry

    lax.fori_loop(0, total, drain, 0)


def fused_shards(
    queries, cache_keys, cache_values, page_len, new_keys, new_values, out_proj, residual,
    norm_gain, gate_up, w_down, expert_ids, gates,
):
    total = lax.axis_size("ep")
    all_experts = total * lax.axis_size("hd")
    query_rows = queries.shape[0]
    heads = queries.shape[1] // HD // 2
    block_rows, half = residual.shape
    features = 2 * half
    own_rows = block_rows // 2
    page_c, page = cache_keys.shape[0], new_keys.shape[0]
    hidden = w_down.shape[1]
    tiles = 4
    sent, arrived = (places[-1] for places in semaphore_places(total, tiles))
    anywhere = pl.BlockSpec(memory_space=pl.ANY)
    vmem = pl.BlockSpec(memory_space=pltpu.VMEM)
    bf, f32 = jnp.bfloat16, jnp.float32
    out = pl.pallas_call(
        functools.partial(layer_kernel, total, tiles),
        out_shape=jax.ShapeDtypeStruct((2, own_rows, half), bf),
        in_specs=[pl.BlockSpec(memory_space=pltpu.SMEM)] + [anywhere] * 7 + [vmem] + [anywhere] * 2
        + [vmem] * 2,
        out_specs=anywhere,
        scratch_shapes=[
            pltpu.VMEM((heads, query_rows, HD), bf),
            pltpu.VMEM((total, 2, 2 * page_c + 16, HD), bf),
            pltpu.VMEM((total, 2, 2 * page, HD), bf),
            pltpu.VMEM((heads, query_rows, HD), f32),
            pltpu.VMEM((heads, query_rows, HD), f32),
            pltpu.VMEM((heads, query_rows, HD), f32),
            pltpu.VMEM((2, query_rows, heads * HD), bf),
            pltpu.VMEM(out_proj.shape, bf),
            pltpu.VMEM((tiles, own_rows, half // 2), bf),
            pltpu.VMEM((tiles, own_rows, half // 2), bf),
            pltpu.VMEM((block_rows, half), bf),
            pltpu.VMEM((2, own_rows, half), bf),
            pltpu.VMEM((2, 3, 2, hidden, features), bf),
            pltpu.VMEM((total, own_rows, features), bf),
            pltpu.VMEM((total, Z_CUTS, own_rows, features // Z_CUTS), bf),
            pltpu.VMEM((total + 1, Z_CUTS, own_rows, features // Z_CUTS), bf),
            pltpu.SemaphoreType.DMA((sent,)),
            pltpu.SemaphoreType.DMA((arrived,)),
            pltpu.SemaphoreType.DMA((16 + heads,)),
            pltpu.SemaphoreType.DMA((SIB_COUNT,)),
            pltpu.SemaphoreType.DMA((SIB_COUNT,)),
            pltpu.VMEM((block_rows, half), f32),
            pltpu.VMEM((2, 2, own_rows, features // Z_CUTS), bf),
            pltpu.VMEM((total, 2 * own_rows, 128), f32),
        ],
        compiler_params=pltpu.CompilerParams(
            collective_id=0, has_side_effects=True, vmem_limit_bytes=58 * 1024 * 1024
        ),
    )(page_len, queries, cache_keys, cache_values, new_keys, new_values, out_proj, residual,
      norm_gain, gate_up, w_down, expert_ids.T, gates.T)
    return out.reshape(block_rows, half)


def layer(*arguments):
    queries, page_rows, ids = arguments[0], arguments[4].shape[0], arguments[11]
    pair = lax.axis_size("ep") >= 4 and lax.axis_size("grp") == 2
    pair = pair and lax.axis_size("hd") == 2 and lax.axis_size("sub") == 2
    slots = block_sizes(ids.shape[0], lax.axis_size("ep"), lax.axis_size("hd"))[1]
    group_width = QH // KVH
    whole_heads = queries.shape[1] == 2 * group_width * HD
    whole_pages = page_rows == 128 and arguments[1].shape[0] == 128
    rows_fit = queries.shape[0] == 2 * page_rows and ids.shape == (128, 8)
    rows_fit = rows_fit and lax.axis_size("ep") == 4
    if pair and slots == ids.shape[0] and whole_heads and whole_pages and rows_fit:
        return fused_shards(*arguments)
    return shards(*arguments)


def solution(mesh):
    return jax.shard_map(
        layer,
        mesh=mesh,
        in_specs=(
            P(("grp", "ep"), "hd"),
            P(("grp", "ep", "sub"), None),
            P(("grp", "ep", "sub"), None),
            P(("grp", "ep", "sub")),
            P(("grp", "ep", "sub"), None),
            P(("grp", "ep", "sub"), None),
            P("hd", "sub"),
            P(("grp", "ep", "hd"), "sub"),
            P(),
            P(("ep", "hd"), None, "sub", None),
            P(("ep", "hd"), "sub", None),
            P(("grp", "ep", "hd"), None),
            P(("grp", "ep", "hd"), None),
        ),
        out_specs=P(("grp", "ep", "hd"), "sub"),
        check_vma=False,
    )
```

```python
import functools
import math

import jax
import jax.numpy as jnp
from jax import lax
from jax.experimental import pallas as pl
from jax.experimental.pallas import tpu as pltpu
from jax.sharding import PartitionSpec as P

QH = 32
KVH = 4
HD = 128
GROUPS_ROW = 4


NEG_FILL = -1e30
EPSILON = 1e-06
KEY_BLOCK = 1024
FAR_RANK = 1073741824
MESH = pl.DeviceIdType.MESH


def joined(x, axis, join):
    gathered = jax.tree.map(
        lambda a, kind: lax.all_gather(a.astype(kind), axis),
        x,
        jax.tree.map(lambda a: jnp.bfloat16 if a.dtype == jnp.float32 else a.dtype, x),
    )

    def take(source):
        return jax.tree.map(
            lambda a, own: lax.dynamic_index_in_dim(a, source, 0, False).astype(own.dtype),
            gathered,
            x,
        )

    return lax.fori_loop(
        1, lax.axis_size(axis), lambda source, state: join(state, take(source)), take(0)
    )


def block_sizes(block_rows, group_total, experts_group):
    group_slots = min(block_rows, 3 * GROUPS_ROW * block_rows // (2 * group_total))
    return (group_slots, 2 * group_slots // experts_group)


def attend_block(fold_state, packed, key_rank, query_heads, row_ids, kv_heads):
    running_max, weight_sum, weighted = fold_state
    half_cols = packed.shape[1] // 2
    length = packed.shape[0]
    key_part = packed[:, :half_cols].reshape(length, kv_heads, half_cols // kv_heads)
    value_part = packed[:, half_cols:].reshape(length, kv_heads, half_cols // kv_heads)
    scores = jnp.einsum(
        "rkqd,lkd->rkql", query_heads, key_part, preferred_element_type=jnp.float32
    ) * (1.0 / math.sqrt(HD))
    allowed = (key_rank[None, :] <= row_ids[:, None])[:, None, None, :]
    masked = jnp.where(allowed, scores, NEG_FILL)
    new_max = jnp.maximum(running_max, jnp.max(masked, axis=3))
    factor = jnp.exp(running_max - new_max)
    exp_terms = jnp.where(allowed, jnp.exp(scores - new_max[..., None]), 0.0)
    weight_sum = weight_sum * factor + jnp.sum(exp_terms, axis=3)
    weighted = weighted * factor[..., None] + jnp.einsum(
        "rkql,lkd->rkqd",
        exp_terms.astype(jnp.bfloat16),
        value_part,
        preferred_element_type=jnp.float32,
    )
    return (new_max, weight_sum, weighted)


def join_parts(first_part, second_part):
    first_max, first_sum, first_weighted = first_part
    second_max, second_sum, second_weighted = second_part
    joint_max = jnp.maximum(first_max, second_max)
    first_factor = jnp.exp(first_max - joint_max)
    second_factor = jnp.exp(second_max - joint_max)
    joint_sum = first_sum * first_factor + second_sum * second_factor
    joint_weighted = (
        first_weighted * first_factor[..., None] + second_weighted * second_factor[..., None]
    )
    return (joint_max, joint_sum, joint_weighted)


def shards(
    queries,
    cache_keys,
    cache_values,
    page_len,
    new_keys,
    new_values,
    out_proj,
    residual,
    norm_gain,
    gate_up,
    w_down,
    expert_ids,
    gates,
):
    query_rows = queries.shape[0]
    heads_here = queries.shape[1] // HD
    group_width = QH // KVH
    kv_heads = max(1, heads_here // group_width)
    per_kv = heads_here // kv_heads
    kv_first = lax.axis_index("hd") * heads_here // group_width

    def kv_columns(source):
        return lax.dynamic_slice_in_dim(source, kv_first * HD, kv_heads * HD, 1)

    local_keys = jnp.concatenate([kv_columns(cache_keys), kv_columns(new_keys)], axis=0)
    local_values = jnp.concatenate([kv_columns(cache_values), kv_columns(new_values)], axis=0)
    packed_local = jnp.concatenate([local_keys, local_values], axis=1)
    cache_rows = cache_keys.shape[0]
    new_rows = new_keys.shape[0]
    cache_rank = jnp.where(
        jnp.arange(cache_rows, dtype=jnp.int32) < page_len[0], -1, FAR_RANK
    ).astype(jnp.int32)
    new_block = lax.axis_index("ep") * lax.axis_size("sub") + lax.axis_index("sub")
    new_rank = new_block * new_rows + jnp.arange(new_rows, dtype=jnp.int32)
    rank_local = jnp.concatenate([cache_rank, new_rank], axis=0)
    row_ids = lax.axis_index("ep") * query_rows + jnp.arange(query_rows, dtype=jnp.int32)
    query_heads = queries.reshape(query_rows, kv_heads, per_kv, HD)

    def fold_keys(fold_state, piece_data):
        packed, key_rank = piece_data
        length = packed.shape[0]
        if length > KEY_BLOCK and length % KEY_BLOCK == 0:
            block_count = length // KEY_BLOCK

            def scan_step(inner_state, block_data):
                return (
                    attend_block(
                        inner_state, block_data[0], block_data[1], query_heads, row_ids, kv_heads
                    ),
                    None,
                )

            fold_state, _ = lax.scan(
                scan_step,
                fold_state,
                (
                    packed.reshape(block_count, KEY_BLOCK, packed.shape[1]),
                    key_rank.reshape(block_count, KEY_BLOCK),
                ),
            )
            return fold_state
        return attend_block(fold_state, packed, key_rank, query_heads, row_ids, kv_heads)

    start_state = (
        jnp.full((query_rows, kv_heads, per_kv), NEG_FILL, jnp.float32),
        jnp.zeros((query_rows, kv_heads, per_kv), jnp.float32),
        jnp.zeros((query_rows, kv_heads, per_kv, HD), jnp.float32),
    )
    fold_state = fold_keys(
        start_state,
        (
            lax.all_gather(packed_local, "ep", axis=0, tiled=True),
            lax.all_gather(rank_local, "ep", axis=0, tiled=True),
        ),
    )
    running_max, weight_sum, weighted = joined(fold_state, "sub", join_parts)
    attended = (
        (weighted / weight_sum[..., None]).reshape(query_rows, heads_here * HD).astype(jnp.bfloat16)
    )
    projected = lax.psum_scatter(
        jnp.dot(attended, out_proj, preferred_element_type=jnp.float32).astype(jnp.bfloat16),
        "hd",
        scatter_dimension=0,
        tiled=True,
    ).astype(jnp.float32)
    hidden_half = (residual.astype(jnp.float32) + projected).astype(jnp.bfloat16)
    widened = hidden_half.astype(jnp.float32)
    features = norm_gain.shape[0]
    half_width = hidden_half.shape[1]
    square_sum = lax.psum(jnp.sum(widened * widened, axis=1), "sub")
    gain_half = lax.dynamic_slice_in_dim(
        norm_gain, lax.axis_index("sub") * half_width, half_width, 0
    )
    normed = (
        widened
        * lax.rsqrt(square_sum[:, None] / features + EPSILON)
        * gain_half.astype(jnp.float32)
    ).astype(jnp.bfloat16)
    pair_weights = gate_up[0].reshape(-1, features)
    hidden_units = w_down.shape[1]
    group_total = lax.axis_size("ep")
    group_experts = lax.axis_size("hd")
    all_experts = group_total * group_experts
    block_rows = expert_ids.shape[0]
    group_slots, expert_slots = block_sizes(block_rows, group_total, group_experts)
    chosen = (
        expert_ids[:, :, None] == jnp.arange(all_experts, dtype=jnp.int32)[None, None, :]
    ).astype(jnp.int32)
    named_count = jnp.sum(chosen, axis=1)
    earlier = jnp.cumsum(named_count, axis=0) - named_count
    slot_index = jnp.sum(chosen * earlier[:, None, :], axis=2)
    position = expert_ids * expert_slots + slot_index
    slot_columns = jnp.arange(all_experts * expert_slots, dtype=jnp.int32)
    gate_table = jnp.sum(
        jnp.where(
            position[:, :, None] == slot_columns[None, None, :],
            gates.astype(jnp.float32)[:, :, None],
            0.0,
        ),
        axis=1,
    ).astype(jnp.bfloat16)
    placed = (gate_table != 0).astype(jnp.bfloat16)
    outgoing = jnp.einsum("rq,rd->qd", placed, normed, preferred_element_type=jnp.float32).astype(
        jnp.bfloat16
    )
    outgoing = outgoing.reshape(all_experts, expert_slots, normed.shape[1])
    arrived = lax.all_to_all(outgoing, ("ep", "hd"), split_axis=0, concat_axis=0, tiled=True)
    lead_shape = arrived.shape[:-1]
    rows_in = arrived.reshape(-1, arrived.shape[-1])
    rows_in = lax.all_gather(rows_in, "sub", axis=1, tiled=True)
    projected_pair = jnp.einsum(
        "rd,fd->rf", rows_in, pair_weights, preferred_element_type=jnp.float32
    )
    activation = (
        jax.nn.silu(projected_pair[:, :hidden_units]) * projected_pair[:, hidden_units:]
    ).astype(jnp.bfloat16)
    partial_out = jnp.dot(activation, w_down[0], preferred_element_type=jnp.float32)
    expert_out = lax.psum_scatter(
        partial_out.astype(jnp.bfloat16), "sub", scatter_dimension=1, tiled=True
    )
    results = expert_out.reshape(lead_shape + (expert_out.shape[1],))
    returned = lax.all_to_all(results, ("ep", "hd"), split_axis=0, concat_axis=0, tiled=True)
    mixture = jnp.dot(
        gate_table,
        returned.reshape(all_experts * expert_slots, half_width),
        preferred_element_type=jnp.float32,
    )
    return (widened + mixture).astype(jnp.bfloat16)


def slot_of(step, place, total):
    near = jnp.minimum(place, total - 1 - place)
    odd = place - (step + 1) // 2
    even = place + step // 2
    beside = jnp.where(step % 2 == 1, odd, even)
    beyond = jnp.where(place < total - 1 - place, step, total - 1 - step)
    return jnp.where(step <= 2 * near, beside, beyond)


(C_UP, C_DOWN, N_UP, X_UP, X_DOWN, W_SIDE, W_PART, Z_UP, Z_DOWN, P_SIDE) = range(10)
(C_IN, N_IN, X_IN, W_SIDE_IN, W_PART_IN, Z_IN, P_IN) = range(7)
SIB_COUNT = 25
W_PIECES = 6
X_CUTS = 2
Z_CUTS = 4
LOG2_E = math.log2(math.e)


def semaphore_places(total, tiles):
    sent = (total, total, total, X_CUTS * total, X_CUTS * total, W_PIECES, W_PIECES,
            Z_CUTS * total, Z_CUTS * total, tiles)
    arrived = (total, total, X_CUTS * total, W_PIECES, W_PIECES, Z_CUTS * (total + 1), tiles)
    return [[sum(sizes[:i]) for i in range(len(sizes) + 1)] for sizes in (sent, arrived)]


def layer_kernel(
    total, tiles,
    page_len, queries, cache_keys, cache_values, new_keys, new_values, out_proj, residual, gain,
    gate_up, w_down, ids_t, gates_t,
    out,
    q_v, cbuf, nbuf, m_v, l_v, acc_v, att, proj_w, part_out, part_in, res_v, hid, wgu,
    rows, results, chain_in,
    send_sem, recv_sem, load_sem, sib_send, sib_recv, proj_f, out_buf, gate_cols, ids_v, gates_v, gain_v,
):
    e = lax.axis_index("ep")
    h = lax.axis_index("hd")
    s = lax.axis_index("sub")
    part = lax.axis_index("grp")
    last = total - 1
    heads = q_v.shape[0]
    page = new_keys.shape[0]
    page_c = cache_keys.shape[0]
    half = out.shape[2]
    own_rows = out.shape[1]
    features = 2 * half
    scale = LOG2_E / math.sqrt(HD)
    has_up = e < last
    sent_at, arrived_at = semaphore_places(total, tiles)
    has_down = e > 0

    def col(index, width):
        return pl.ds(pl.multiple_of(index * width, width), width)

    def local(index, src, dst):
        return pltpu.make_async_copy(src, dst, load_sem.at[index])

    barrier = pltpu.get_barrier_semaphore()
    pl.semaphore_signal(barrier, inc=1, device_id={"sub": 1 - s}, device_id_type=MESH)
    pl.semaphore_signal(barrier, inc=1, device_id={"hd": 1 - h}, device_id_type=MESH)
    pl.semaphore_signal(barrier, inc=1, device_id={"grp": 1 - part}, device_id_type=MESH)

    @pl.when(has_up)
    def _():
        pl.semaphore_signal(barrier, inc=1, device_id={"ep": e + 1}, device_id_type=MESH)

    @pl.when(has_down)
    def _():
        pl.semaphore_signal(barrier, inc=1, device_id={"ep": e - 1}, device_id_type=MESH)

    mine = 2 * h + s
    loads = [
        local(0, cache_keys.at[:, col(mine, HD)], cbuf.at[e, s, pl.ds(0, page_c)]),
        local(1, cache_values.at[:, col(mine, HD)], cbuf.at[e, s, pl.ds(page_c, page_c)]),
        local(3, new_keys.at[:, col(mine, HD)], nbuf.at[e, s, pl.ds(0, page)]),
        local(4, new_values.at[:, col(mine, HD)], nbuf.at[e, s, pl.ds(page, page)]),
    ]
    q_loads = [
        local(16 + i, queries.at[:, col(s * heads + i, HD)], q_v.at[i]) for i in range(heads)
    ]
    w_loads = [
        local(5, out_proj, proj_w),
        local(6, residual, res_v),
        local(9, gate_up.at[0], wgu.at[h, pl.ds(0, 2), s]),
        local(10, w_down.at[0], wgu.at[h, 2, s]),
    ]
    small_loads = [local(2, ids_t, ids_v), local(11, gates_t, gates_v), local(12, gain, gain_v)]
    for copy in small_loads + loads + q_loads + w_loads:
        copy.start()

    experts = 2 * total
    lane = lax.broadcasted_iota(jnp.int32, (8, HD), 1)
    seen = jnp.where(lane < page_len[0], 0.0, NEG_FILL)
    for copy in small_loads:
        copy.wait()
    ids = ids_v[...]
    gate_values = gates_v[...].astype(jnp.float32)
    place = lax.broadcasted_iota(jnp.int32, (8, HD), 0)
    by_expert = jnp.zeros((8, HD), jnp.float32)
    for x in range(experts):
        one_row = jnp.sum(jnp.where(ids == x, gate_values, 0.0), axis=0, keepdims=True)
        by_expert = jnp.where(place == x, one_row, by_expert)
    cbuf[e, s, 2 * page_c:2 * page_c + 16, :] = jnp.concatenate(
        [seen, by_expert], axis=0).astype(jnp.bfloat16)

    pl.semaphore_wait(barrier, 3 + has_up.astype(jnp.int32) + has_down.astype(jnp.int32))

    def sibling(index, src, dst):
        return pltpu.make_async_remote_copy(
            src_ref=src, dst_ref=dst, send_sem=sib_send.at[index], recv_sem=sib_recv.at[index],
            device_id={"sub": 1 - s}, device_id_type=MESH)

    def remote(kind, index, arrival, slot, src, dst, where):
        return pltpu.make_async_remote_copy(
            src_ref=src, dst_ref=dst, send_sem=send_sem.at[sent_at[kind] + index],
            recv_sem=recv_sem.at[arrived_at[arrival] + slot], device_id=where, device_id_type=MESH)

    theirs = 2 * h + 1 - s
    kv_sib = [
        sibling(0, cache_keys.at[:, col(theirs, HD)], cbuf.at[e, s, pl.ds(0, page_c)]),
        sibling(1, cache_values.at[:, col(theirs, HD)], cbuf.at[e, s, pl.ds(page_c, page_c)]),
        sibling(2, cbuf.at[e, s, pl.ds(2 * page_c, 16)], cbuf.at[e, s, pl.ds(2 * page_c, 16)]),
        sibling(3, new_keys.at[:, col(theirs, HD)], nbuf.at[e, s, pl.ds(0, page)]),
        sibling(4, new_values.at[:, col(theirs, HD)], nbuf.at[e, s, pl.ds(page, page)]),
    ]
    w_sib = [
        sibling(5, gate_up.at[0], wgu.at[h, pl.ds(0, 2), s]),
        sibling(6, w_down.at[0], wgu.at[h, 2, s]),
    ]
    for copy in kv_sib:
        copy.start()

    cut = wgu.shape[3] // 2
    piece_rows = cut // 2

    def cut_rows(which, piece):
        return pl.ds(pl.multiple_of(which * cut + piece % 2 * piece_rows, piece_rows), piece_rows)

    def w_block(piece, which):
        return wgu.at[1 - h, piece // 2, s, cut_rows(which, piece)]

    def w_side(piece):
        kind = piece // 2
        src = (w_down.at[0, cut_rows(part, piece)] if kind == 2
               else gate_up.at[0, kind, cut_rows(part, piece)])
        return remote(W_SIDE, piece, W_SIDE_IN, piece, src,
                      wgu.at[h, kind, s, cut_rows(part, piece)], {"hd": 1 - h})

    def w_part(piece):
        block_ref = w_block(piece, part)
        return remote(W_PART, piece, W_PART_IN, piece, block_ref, block_ref, {"grp": 1 - part})

    def w_near(piece, which):
        block_ref = w_block(piece, jnp.where(which == 0, part, 1 - part))
        return sibling(11 + 2 * piece + which, block_ref, block_ref)

    def w_from_side(piece):
        block_ref = w_block(piece, part)
        remote(W_SIDE, piece, W_SIDE_IN, piece, block_ref, block_ref, {"hd": 1 - h}).wait_recv()
        w_part(piece).start()
        w_near(piece, 0).start()

    def w_from_part(piece):
        w_part(piece).wait_recv()
        w_near(piece, 1).start()

    for piece in range(W_PIECES):
        w_side(piece).start()

    def c_up(i):
        return remote(C_UP, i, C_IN, i, cbuf.at[i], cbuf.at[i], {"ep": e + 1})

    def c_down(i):
        return remote(C_DOWN, i, C_IN, i, cbuf.at[i], cbuf.at[i], {"ep": e - 1})

    def n_up(i):
        return remote(N_UP, i, N_IN, i, nbuf.at[i], nbuf.at[i], {"ep": e + 1})

    for copy in loads:
        copy.wait()
    for copy in kv_sib:
        copy.wait_recv()

    @pl.when(has_up)
    def _():
        n_up(e).start()
        c_up(e).start()

    @pl.when(has_down)
    def _():
        c_down(e).start()

    for copy in w_sib:
        copy.start()
    for copy in q_loads:
        copy.wait()

    def parts_of(buf, index, size):
        return (buf[index, :, 0:size, :].reshape(2 * size, HD),
                buf[index, :, size:2 * size, :].reshape(2 * size, HD))

    def attend(index, with_cache, with_new, causal, first=False):
        pieces = []
        if with_cache:
            pieces.append(parts_of(cbuf, index, page_c))
            line = jnp.concatenate(
                [cbuf[index, 0, 2 * page_c:2 * page_c + 16, :],
                 cbuf[index, 1, 2 * page_c:2 * page_c + 16, :]], axis=1)[0:1].astype(jnp.float32)
        if with_new:
            pieces.append(parts_of(nbuf, index, page))

        def one_head(i, carry):
            query = q_v[i]
            scores = []
            for place, (key_part, _) in enumerate(pieces):
                one = lax.dot_general(
                    query, key_part, (((1,), (1,)), ((), ())), preferred_element_type=jnp.float32)
                if with_cache and place == 0:
                    one = one + line
                elif causal:
                    r = lax.broadcasted_iota(jnp.int32, one.shape, 0)
                    c = lax.broadcasted_iota(jnp.int32, one.shape, 1)
                    one = jnp.where(c <= r, one, NEG_FILL)
                scores.append(one)
            top = jnp.max(functools.reduce(
                jnp.maximum, [one[:, j:j + HD] for one in scores for j in range(0, one.shape[1], HD)]),
                axis=1, keepdims=True)
            if first:
                new = jnp.broadcast_to(top, m_v.shape[1:])
            else:
                old = m_v[i]
                new = jnp.maximum(old, top)
                factor = jnp.exp2((old - new) * scale)
            new_col = new[:, 0:1]
            weighted = None
            lane_sum = None
            for one, (_, value_part) in zip(scores, pieces):
                p = jnp.exp2((one - new_col) * scale)
                term = jnp.dot(p.astype(jnp.bfloat16), value_part, preferred_element_type=jnp.float32)
                weighted = term if weighted is None else weighted + term
                for j in range(0, p.shape[1], HD):
                    piece_sum = p[:, j:j + HD]
                    lane_sum = piece_sum if lane_sum is None else lane_sum + piece_sum
            m_v[i] = new
            if first:
                l_v[i] = lane_sum
                acc_v[i] = weighted
            else:
                l_v[i] = l_v[i] * factor + lane_sum
                acc_v[i] = acc_v[i] * factor + weighted
            return carry

        lax.fori_loop(0, heads, one_head, 0, unroll=8)

    attend(e, True, True, True, True)

    middle = jnp.logical_and(has_up, has_down)
    low_side = e < total // 2

    def kv_arrive(t):
        @pl.when(jnp.logical_not(middle))
        def _():
            i = slot_of(t, e, total)

            @pl.when(i < e)
            def _():
                n_up(i).wait_recv()
            c_up(i).wait_recv()

        @pl.when(jnp.logical_and(middle, t == 1))
        def _():
            n_up(e - 1).wait_recv()
            n_up(e - 1).start()
            c_down(e + 1).wait_recv()
            c_down(e + 1).start()
            c_up(e - 1).wait_recv()
            c_up(e - 1).start()

        @pl.when(jnp.logical_and(jnp.logical_and(middle, low_side), t == 2))
        def _():
            c_down(last).wait_recv()
            c_down(last).start()

        @pl.when(jnp.logical_and(middle, jnp.logical_not(low_side)))
        def _():
            @pl.when(t == 2)
            def _():
                n_up(0).wait_recv()
                n_up(0).start()

            @pl.when(t == 3)
            def _():
                c_up(0).wait_recv()
                c_up(0).start()

    def kv_step(t, carry):
        i = slot_of(t, e, total)
        below = i < e
        kv_arrive(t)

        @pl.when(t == 1)
        def _():
            w_from_side(0)

        @pl.when(jnp.logical_and(t == 3, jnp.logical_not(middle)))
        def _():
            w_from_side(3)

        @pl.when(below)
        def _():
            attend(i, True, True, False)

        @pl.when(jnp.logical_not(below))
        def _():
            attend(i, True, False, False)

        @pl.when(t == 1)
        def _():
            w_from_side(1)

        @pl.when(t == 2)
        def _():
            w_from_side(2)

        @pl.when(t == 3)
        def _():
            @pl.when(middle)
            def _():
                w_from_side(3)
            w_from_part(0)
        return carry

    lax.fori_loop(1, total, kv_step, 0)

    def gate_step(i, carry):
        flat = cbuf[i, 0, 2 * page_c:2 * page_c + 16, :].astype(jnp.float32)[8:16]
        gate_cols[i] = jnp.concatenate(
            [flat, jnp.zeros((HD - 8, HD), jnp.float32)], axis=0).T
        return carry

    def finish_head(i, carry):
        att[s, :, col(i, HD)] = (
            acc_v[i] / jnp.sum(l_v[i], axis=1, keepdims=True)).astype(jnp.bfloat16)
        return carry

    lax.fori_loop(0, heads, finish_head, 0)
    block = 2 * own_rows

    def att_rows(which):
        return att.at[s, pl.ds(pl.multiple_of(which * block, block), block)]

    att_sib = sibling(7, att_rows(1 - h), att_rows(1 - h))
    att_sib.start()
    att_own = sibling(9, att_rows(h), att_rows(h))
    att_own.start()
    for copy in w_loads[:2]:
        copy.wait()
    att_sib.wait_recv()

    width = half // tiles
    side_width = half // (tiles // X_CUTS)
    contract = att.shape[2]

    x_rows = own_rows // X_CUTS

    def x_cut(i, k):
        return rows.at[i, pl.ds(k * x_rows, x_rows)]

    def x_up(i, k):
        return remote(X_UP, X_CUTS * i + k, X_IN, X_CUTS * i + k, x_cut(i, k), x_cut(i, k),
                      {"ep": e + 1})

    def x_down(i, k):
        return remote(X_DOWN, X_CUTS * i + k, X_IN, X_CUTS * i + k, x_cut(i, k), x_cut(i, k),
                      {"ep": e - 1})

    def z_up(i, c):
        place = i + c * (total + 1)
        return remote(Z_UP, i + c * total, Z_IN, place, results.at[i, c], chain_in.at[i, c], {"ep": e + 1})

    def z_down(i, c):
        slot = jnp.where(i == e - 1, total, i)
        return remote(Z_DOWN, i + c * total, Z_IN, slot + c * (total + 1),
                      results.at[i, c], chain_in.at[slot, c], {"ep": e - 1})

    def project(a0, a1, j, size):
        return jnp.dot(
            a0, proj_w[0:contract, col(j, size)], preferred_element_type=jnp.float32
        ) + jnp.dot(
            a1, proj_w[contract:2 * contract, col(j, size)], preferred_element_type=jnp.float32)

    def p_side(j):
        return remote(P_SIDE, j, P_IN, j, part_out.at[j], part_in.at[j], {"hd": 1 - h})

    def project_theirs(j, carry):
        first = (1 - h) * block + j // (tiles // X_CUTS) * x_rows
        a0, a1 = [
            jnp.concatenate([
                att[which, pl.ds(pl.multiple_of(first + u * own_rows, x_rows), x_rows), :]
                for u in range(2)], axis=0)
            for which in range(2)]
        part_out[j] = project(a0, a1, j % (tiles // X_CUTS), side_width).astype(jnp.bfloat16)
        p_side(j).start()
        return carry

    lax.fori_loop(0, tiles, project_theirs, 0)
    w_from_side(4)
    w_from_part(1)
    att_own.wait_recv()

    def project_keep(j, carry):
        own = pl.ds(pl.multiple_of(h * block, block), block)
        proj_f[:, col(j, width)] = project(att[0, own, :], att[1, own, :], j, width)
        return carry

    lax.fori_loop(0, tiles, project_keep, 0)
    lax.fori_loop(0, total, gate_step, 0)
    w_from_side(5)
    w_from_part(2)
    w_from_part(3)

    def my_rows(which):
        return pl.ds(pl.multiple_of(which * own_rows, own_rows), own_rows)

    def my_cut(which, k):
        return pl.ds(pl.multiple_of(which * own_rows + k * x_rows, x_rows), x_rows)

    def hid_sib(k):
        return sibling(8 + 2 * k, res_v.at[my_cut(1 - s, k)], hid.at[s, pl.ds(k * x_rows, x_rows)])

    for copy in w_loads[2:]:
        copy.wait()
    for copy in w_sib:
        copy.wait_recv()
    g = gain_v[...].astype(jnp.float32).reshape(1, features)
    for k in range(X_CUTS):
        for j in range(tiles // X_CUTS):
            place = k * (tiles // X_CUTS) + j
            span = slice(j * side_width, (j + 1) * side_width)
            p_side(place).wait_recv()
            for u in range(2):
                cut_u = slice(u * own_rows + k * x_rows, u * own_rows + (k + 1) * x_rows)
                res_v[cut_u, span] = (
                    res_v[cut_u, span].astype(jnp.float32)
                    + (proj_f[cut_u, span]
                       + part_in[place, u * x_rows:(u + 1) * x_rows, :].astype(jnp.float32))
                ).astype(jnp.bfloat16)
        hid_sib(k).start()
        at_k = slice(k * x_rows, (k + 1) * x_rows)
        hid[s, at_k] = res_v[my_cut(s, k), :]
        hid_sib(k).wait_recv()
        h0 = hid[0, at_k].astype(jnp.float32)
        h1 = hid[1, at_k].astype(jnp.float32)
        square = jnp.sum(h0 * h0, axis=1, keepdims=True) + jnp.sum(h1 * h1, axis=1, keepdims=True)
        inverse = lax.rsqrt(square / features + EPSILON)
        rows[e, at_k, 0:half] = (h0 * inverse * g[0:1, 0:half]).astype(jnp.bfloat16)
        rows[e, at_k, half:features] = (h1 * inverse * g[0:1, half:features]).astype(jnp.bfloat16)

        @pl.when(has_up)
        def _():
            x_up(e, k).start()

        @pl.when(has_down)
        def _():
            x_down(e, k).start()

    w_from_part(4)
    units = 2 * wgu.shape[3]
    dims = (((1,), (1,)), ((), ()))
    down_width = features // Z_CUTS

    def turn(k):
        return Z_CUTS // 2 * jnp.where(k < Z_CUTS // 2, 1 - s, s) + k % (Z_CUTS // 2)

    def arrive_near(k):
        @pl.when(middle)
        def _():
            x_up(e - 1, k).wait_recv()
            x_up(e - 1, k).start()
            x_down(e + 1, k).wait_recv()
            x_down(e + 1, k).start()

    def arrive(t):
        @pl.when(jnp.logical_and(jnp.logical_not(middle), t > 0))
        def _():
            for k in range(X_CUTS):
                x_up(slot_of(t, e, total), k).wait_recv()

        @pl.when(t == 1)
        def _():
            for k in range(X_CUTS):
                arrive_near(k)

    def arrive_far(t):
        for k in range(X_CUTS):
            @pl.when(jnp.logical_and(middle, t == 1 + k))
            def _():
                @pl.when(low_side)
                def _():
                    x_down(last, k).wait_recv()
                    x_down(last, k).start()

                @pl.when(jnp.logical_not(low_side))
                def _():
                    x_up(0, k).wait_recv()
                    x_up(0, k).start()

    def expert_step(t, carry):
        i = slot_of(t, e, total)

        @pl.when(t == 0)
        def _():
            for piece in range(4):
                for which in range(2):
                    w_near(piece, which).wait_recv()

        arrive(t)
        x = rows[i]
        activations = []
        for which in range(2):
            gate_part = lax.dot_general(
                x, wgu[which, 0].reshape(units, features), dims, preferred_element_type=jnp.float32)
            up_part = lax.dot_general(
                x, wgu[which, 1].reshape(units, features), dims, preferred_element_type=jnp.float32)
            activations.append(
                (gate_part / (1.0 + jnp.exp(-gate_part)) * up_part).astype(jnp.bfloat16))
        gates_all = gate_cols[i, my_rows(s), :]
        gate_lane = lax.broadcasted_iota(jnp.int32, gates_all.shape, 1)
        weight = [
            jnp.sum(jnp.where(gate_lane == 2 * e + which, gates_all, 0.0), axis=1, keepdims=True)
            for which in range(2)
        ]

        arrive_far(t)

        @pl.when(t == 0)
        def _():
            w_from_part(5)
            for piece in range(4, 6):
                for which in range(2):
                    w_near(piece, which).wait_recv()

        for k in range(Z_CUTS):
            c = turn(k)
            mixed = None
            for which in range(2):
                piece = weight[which] * jnp.dot(
                    activations[which],
                    wgu[which, 2, :, :, col(c, down_width)].reshape(units, down_width),
                    preferred_element_type=jnp.float32)
                mixed = piece if mixed is None else mixed + piece
            results[i, c] = mixed.astype(jnp.bfloat16)

            @pl.when(jnp.logical_and(i > e, jnp.logical_not(has_down)))
            def _():
                z_up(i, c).start()

            @pl.when(jnp.logical_and(i < e, jnp.logical_not(has_up)))
            def _():
                z_down(i, c).start()
        return carry

    lax.fori_loop(0, total, expert_step, 0)

    def add_chain(i, c):
        z_up(i, c).wait_recv()
        results[i, c] = (
            results[i, c].astype(jnp.float32) + chain_in[i, c].astype(jnp.float32)
        ).astype(jnp.bfloat16)

    def relay_up(i, k):
        c = turn(k)
        add_chain(i, c)
        z_up(i, c).start()

    def relay_down(i, k):
        c = turn(k)
        add_chain(i, c)
        z_down(i, c).start()

    @pl.when(jnp.logical_and(middle, low_side))
    def _():
        for k in range(Z_CUTS):
            relay_up(e + 1, k)
        for k in range(Z_CUTS + 2):
            if k < Z_CUTS:
                relay_up(last, k)
            if k >= 2:
                relay_down(0, k - 2)

    @pl.when(jnp.logical_and(middle, jnp.logical_not(low_side)))
    def _():
        for k in range(Z_CUTS):
            relay_down(e - 1, k)
        for k in range(Z_CUTS + 2):
            if k < Z_CUTS:
                relay_down(0, k)
            if k >= 2:
                relay_up(last, k - 2)

    def out_sib(q):
        return sibling(23 + q, out_buf.at[q], out.at[s, :, pl.ds(q * down_width, down_width)])

    for k in range(Z_CUTS):
        c = turn(k)
        q = k % 2

        @pl.when(has_down)
        def _():
            z_up(e, c).wait_recv()

        @pl.when(has_up)
        def _():
            place = total + c * (total + 1)
            block_ref = chain_in.at[total, c]
            remote(Z_UP, 0, Z_IN, place, block_ref, block_ref, {"ep": e + 1}).wait_recv()
        side = jnp.where(k < Z_CUTS // 2, 1 - s, s)
        value = results[e, c].astype(jnp.float32)
        value = value + jnp.where(has_down, chain_in[e, c].astype(jnp.float32), 0.0)
        value = value + jnp.where(has_up, chain_in[total, c].astype(jnp.float32), 0.0)
        value = hid[side, :, q * down_width:(q + 1) * down_width].astype(jnp.float32) + value
        if k < Z_CUTS // 2:
            out_buf[q] = value.astype(jnp.bfloat16)
            out_sib(q).start()
        else:
            out[s, :, q * down_width:(q + 1) * down_width] = value.astype(jnp.bfloat16)
    for q in range(2):
        out_sib(q).wait_recv()

    for piece in range(W_PIECES):
        w_side(piece).wait_send()
        w_part(piece).wait_send()
        w_near(piece, 0).wait_send()
        w_near(piece, 1).wait_send()
    for copy in kv_sib + w_sib + [att_sib, att_own, hid_sib(0), hid_sib(1), out_sib(0), out_sib(1)]:
        copy.wait_send()

    def drain_tile(j, carry):
        p_side(j).wait_send()
        return carry

    lax.fori_loop(0, tiles, drain_tile, 0)

    def drain(i, carry):
        @pl.when(jnp.logical_and(i <= e, has_up))
        def _():
            n_up(i).wait_send()
            c_up(i).wait_send()
            for k in range(X_CUTS):
                x_up(i, k).wait_send()

        @pl.when(jnp.logical_and(i >= e, has_down))
        def _():
            c_down(i).wait_send()
            for k in range(X_CUTS):
                x_down(i, k).wait_send()

        @pl.when(i > e)
        def _():
            for c in range(Z_CUTS):
                z_up(i, c).wait_send()

        @pl.when(i < e)
        def _():
            for c in range(Z_CUTS):
                z_down(i, c).wait_send()
        return carry

    lax.fori_loop(0, total, drain, 0)


def fused_shards(
    queries, cache_keys, cache_values, page_len, new_keys, new_values, out_proj, residual,
    norm_gain, gate_up, w_down, expert_ids, gates,
):
    total = lax.axis_size("ep")
    all_experts = total * lax.axis_size("hd")
    query_rows = queries.shape[0]
    heads = queries.shape[1] // HD // 2
    block_rows, half = residual.shape
    features = 2 * half
    own_rows = block_rows // 2
    page_c, page = cache_keys.shape[0], new_keys.shape[0]
    hidden = w_down.shape[1]
    tiles = 4
    sent, arrived = (places[-1] for places in semaphore_places(total, tiles))
    anywhere = pl.BlockSpec(memory_space=pl.ANY)
    bf, f32 = jnp.bfloat16, jnp.float32
    ids_rows, gate_rows = expert_ids.T, gates.T
    out = pl.pallas_call(
        functools.partial(layer_kernel, total, tiles),
        out_shape=pltpu.VMEM((2, own_rows, half), bf),
        in_specs=[pl.BlockSpec(memory_space=pltpu.SMEM)] + [anywhere] * 12,
        out_specs=pl.BlockSpec(memory_space=pltpu.VMEM),
        scratch_shapes=[
            pltpu.VMEM((heads, query_rows, HD), bf),
            pltpu.VMEM((total, 2, 2 * page_c + 16, HD), bf),
            pltpu.VMEM((total, 2, 2 * page, HD), bf),
            pltpu.VMEM((heads, query_rows, HD), f32),
            pltpu.VMEM((heads, query_rows, HD), f32),
            pltpu.VMEM((heads, query_rows, HD), f32),
            pltpu.VMEM((2, query_rows, heads * HD), bf),
            pltpu.VMEM(out_proj.shape, bf),
            pltpu.VMEM((tiles, own_rows, half // 2), bf),
            pltpu.VMEM((tiles, own_rows, half // 2), bf),
            pltpu.VMEM((block_rows, half), bf),
            pltpu.VMEM((2, own_rows, half), bf),
            pltpu.VMEM((2, 3, 2, hidden, features), bf),
            pltpu.VMEM((total, own_rows, features), bf),
            pltpu.VMEM((total, Z_CUTS, own_rows, features // Z_CUTS), bf),
            pltpu.VMEM((total + 1, Z_CUTS, own_rows, features // Z_CUTS), bf),
            pltpu.SemaphoreType.DMA((sent,)),
            pltpu.SemaphoreType.DMA((arrived,)),
            pltpu.SemaphoreType.DMA((16 + heads,)),
            pltpu.SemaphoreType.DMA((SIB_COUNT,)),
            pltpu.SemaphoreType.DMA((SIB_COUNT,)),
            pltpu.VMEM((block_rows, half), f32),
            pltpu.VMEM((2, own_rows, features // Z_CUTS), bf),
            pltpu.VMEM((total, 2 * own_rows, 128), f32),
            pltpu.VMEM(ids_rows.shape, jnp.int32),
            pltpu.VMEM(gate_rows.shape, bf),
            pltpu.VMEM(norm_gain.shape, bf),
        ],
        compiler_params=pltpu.CompilerParams(
            collective_id=0, has_side_effects=True, vmem_limit_bytes=58 * 1024 * 1024
        ),
    )(page_len, queries, cache_keys, cache_values, new_keys, new_values, out_proj, residual,
      norm_gain, gate_up, w_down, ids_rows, gate_rows)
    return out.reshape(block_rows, half)


def layer(*arguments):
    queries, page_rows, ids = arguments[0], arguments[4].shape[0], arguments[11]
    pair = lax.axis_size("ep") >= 4 and lax.axis_size("grp") == 2
    pair = pair and lax.axis_size("hd") == 2 and lax.axis_size("sub") == 2
    slots = block_sizes(ids.shape[0], lax.axis_size("ep"), lax.axis_size("hd"))[1]
    group_width = QH // KVH
    whole_heads = queries.shape[1] == 2 * group_width * HD
    whole_pages = page_rows == 128 and arguments[1].shape[0] == 128
    rows_fit = queries.shape[0] == 2 * page_rows and ids.shape == (128, 8)
    rows_fit = rows_fit and lax.axis_size("ep") == 4
    if pair and slots == ids.shape[0] and whole_heads and whole_pages and rows_fit:
        return fused_shards(*arguments)
    return shards(*arguments)


def solution(mesh):
    return jax.shard_map(
        layer,
        mesh=mesh,
        in_specs=(
            P(("grp", "ep"), "hd"),
            P(("grp", "ep", "sub"), None),
            P(("grp", "ep", "sub"), None),
            P(("grp", "ep", "sub")),
            P(("grp", "ep", "sub"), None),
            P(("grp", "ep", "sub"), None),
            P("hd", "sub"),
            P(("grp", "ep", "hd"), "sub"),
            P(),
            P(("ep", "hd"), None, "sub", None),
            P(("ep", "hd"), "sub", None),
            P(("grp", "ep", "hd"), None),
            P(("grp", "ep", "hd"), None),
        ),
        out_specs=P(("grp", "ep", "hd"), "sub"),
        check_vma=False,
    )
```

```python
import functools
import math

import jax
import jax.numpy as jnp
from jax import lax
from jax.experimental import pallas as pl
from jax.experimental.pallas import tpu as pltpu
from jax.sharding import PartitionSpec as P

QH = 32
KVH = 4
HD = 128
GROUPS_ROW = 4


NEG_FILL = -1e30
EPSILON = 1e-06
KEY_BLOCK = 1024
FAR_RANK = 1073741824
MESH = pl.DeviceIdType.MESH


def joined(x, axis, join):
    gathered = jax.tree.map(
        lambda a, kind: lax.all_gather(a.astype(kind), axis),
        x,
        jax.tree.map(lambda a: jnp.bfloat16 if a.dtype == jnp.float32 else a.dtype, x),
    )

    def take(source):
        return jax.tree.map(
            lambda a, own: lax.dynamic_index_in_dim(a, source, 0, False).astype(own.dtype),
            gathered,
            x,
        )

    return lax.fori_loop(
        1, lax.axis_size(axis), lambda source, state: join(state, take(source)), take(0)
    )


def block_sizes(block_rows, group_total, experts_group):
    group_slots = min(block_rows, 3 * GROUPS_ROW * block_rows // (2 * group_total))
    return (group_slots, 2 * group_slots // experts_group)


def attend_block(fold_state, packed, key_rank, query_heads, row_ids, kv_heads):
    running_max, weight_sum, weighted = fold_state
    half_cols = packed.shape[1] // 2
    length = packed.shape[0]
    key_part = packed[:, :half_cols].reshape(length, kv_heads, half_cols // kv_heads)
    value_part = packed[:, half_cols:].reshape(length, kv_heads, half_cols // kv_heads)
    scores = jnp.einsum(
        "rkqd,lkd->rkql", query_heads, key_part, preferred_element_type=jnp.float32
    ) * (1.0 / math.sqrt(HD))
    allowed = (key_rank[None, :] <= row_ids[:, None])[:, None, None, :]
    masked = jnp.where(allowed, scores, NEG_FILL)
    new_max = jnp.maximum(running_max, jnp.max(masked, axis=3))
    factor = jnp.exp(running_max - new_max)
    exp_terms = jnp.where(allowed, jnp.exp(scores - new_max[..., None]), 0.0)
    weight_sum = weight_sum * factor + jnp.sum(exp_terms, axis=3)
    weighted = weighted * factor[..., None] + jnp.einsum(
        "rkql,lkd->rkqd",
        exp_terms.astype(jnp.bfloat16),
        value_part,
        preferred_element_type=jnp.float32,
    )
    return (new_max, weight_sum, weighted)


def join_parts(first_part, second_part):
    first_max, first_sum, first_weighted = first_part
    second_max, second_sum, second_weighted = second_part
    joint_max = jnp.maximum(first_max, second_max)
    first_factor = jnp.exp(first_max - joint_max)
    second_factor = jnp.exp(second_max - joint_max)
    joint_sum = first_sum * first_factor + second_sum * second_factor
    joint_weighted = (
        first_weighted * first_factor[..., None] + second_weighted * second_factor[..., None]
    )
    return (joint_max, joint_sum, joint_weighted)


def shards(
    queries,
    cache_keys,
    cache_values,
    page_len,
    new_keys,
    new_values,
    out_proj,
    residual,
    norm_gain,
    gate_up,
    w_down,
    expert_ids,
    gates,
):
    query_rows = queries.shape[0]
    heads_here = queries.shape[1] // HD
    group_width = QH // KVH
    kv_heads = max(1, heads_here // group_width)
    per_kv = heads_here // kv_heads
    kv_first = lax.axis_index("hd") * heads_here // group_width

    def kv_columns(source):
        return lax.dynamic_slice_in_dim(source, kv_first * HD, kv_heads * HD, 1)

    local_keys = jnp.concatenate([kv_columns(cache_keys), kv_columns(new_keys)], axis=0)
    local_values = jnp.concatenate([kv_columns(cache_values), kv_columns(new_values)], axis=0)
    packed_local = jnp.concatenate([local_keys, local_values], axis=1)
    cache_rows = cache_keys.shape[0]
    new_rows = new_keys.shape[0]
    cache_rank = jnp.where(
        jnp.arange(cache_rows, dtype=jnp.int32) < page_len[0], -1, FAR_RANK
    ).astype(jnp.int32)
    new_block = lax.axis_index("ep") * lax.axis_size("sub") + lax.axis_index("sub")
    new_rank = new_block * new_rows + jnp.arange(new_rows, dtype=jnp.int32)
    rank_local = jnp.concatenate([cache_rank, new_rank], axis=0)
    row_ids = lax.axis_index("ep") * query_rows + jnp.arange(query_rows, dtype=jnp.int32)
    query_heads = queries.reshape(query_rows, kv_heads, per_kv, HD)

    def fold_keys(fold_state, piece_data):
        packed, key_rank = piece_data
        length = packed.shape[0]
        if length > KEY_BLOCK and length % KEY_BLOCK == 0:
            block_count = length // KEY_BLOCK

            def scan_step(inner_state, block_data):
                return (
                    attend_block(
                        inner_state, block_data[0], block_data[1], query_heads, row_ids, kv_heads
                    ),
                    None,
                )

            fold_state, _ = lax.scan(
                scan_step,
                fold_state,
                (
                    packed.reshape(block_count, KEY_BLOCK, packed.shape[1]),
                    key_rank.reshape(block_count, KEY_BLOCK),
                ),
            )
            return fold_state
        return attend_block(fold_state, packed, key_rank, query_heads, row_ids, kv_heads)

    start_state = (
        jnp.full((query_rows, kv_heads, per_kv), NEG_FILL, jnp.float32),
        jnp.zeros((query_rows, kv_heads, per_kv), jnp.float32),
        jnp.zeros((query_rows, kv_heads, per_kv, HD), jnp.float32),
    )
    fold_state = fold_keys(
        start_state,
        (
            lax.all_gather(packed_local, "ep", axis=0, tiled=True),
            lax.all_gather(rank_local, "ep", axis=0, tiled=True),
        ),
    )
    running_max, weight_sum, weighted = joined(fold_state, "sub", join_parts)
    attended = (
        (weighted / weight_sum[..., None]).reshape(query_rows, heads_here * HD).astype(jnp.bfloat16)
    )
    projected = lax.psum_scatter(
        jnp.dot(attended, out_proj, preferred_element_type=jnp.float32).astype(jnp.bfloat16),
        "hd",
        scatter_dimension=0,
        tiled=True,
    ).astype(jnp.float32)
    hidden_half = (residual.astype(jnp.float32) + projected).astype(jnp.bfloat16)
    widened = hidden_half.astype(jnp.float32)
    features = norm_gain.shape[0]
    half_width = hidden_half.shape[1]
    square_sum = lax.psum(jnp.sum(widened * widened, axis=1), "sub")
    gain_half = lax.dynamic_slice_in_dim(
        norm_gain, lax.axis_index("sub") * half_width, half_width, 0
    )
    normed = (
        widened
        * lax.rsqrt(square_sum[:, None] / features + EPSILON)
        * gain_half.astype(jnp.float32)
    ).astype(jnp.bfloat16)
    pair_weights = gate_up[0].reshape(-1, features)
    hidden_units = w_down.shape[1]
    group_total = lax.axis_size("ep")
    group_experts = lax.axis_size("hd")
    all_experts = group_total * group_experts
    block_rows = expert_ids.shape[0]
    group_slots, expert_slots = block_sizes(block_rows, group_total, group_experts)
    chosen = (
        expert_ids[:, :, None] == jnp.arange(all_experts, dtype=jnp.int32)[None, None, :]
    ).astype(jnp.int32)
    named_count = jnp.sum(chosen, axis=1)
    earlier = jnp.cumsum(named_count, axis=0) - named_count
    slot_index = jnp.sum(chosen * earlier[:, None, :], axis=2)
    position = expert_ids * expert_slots + slot_index
    slot_columns = jnp.arange(all_experts * expert_slots, dtype=jnp.int32)
    gate_table = jnp.sum(
        jnp.where(
            position[:, :, None] == slot_columns[None, None, :],
            gates.astype(jnp.float32)[:, :, None],
            0.0,
        ),
        axis=1,
    ).astype(jnp.bfloat16)
    placed = (gate_table != 0).astype(jnp.bfloat16)
    outgoing = jnp.einsum("rq,rd->qd", placed, normed, preferred_element_type=jnp.float32).astype(
        jnp.bfloat16
    )
    outgoing = outgoing.reshape(all_experts, expert_slots, normed.shape[1])
    arrived = lax.all_to_all(outgoing, ("ep", "hd"), split_axis=0, concat_axis=0, tiled=True)
    lead_shape = arrived.shape[:-1]
    rows_in = arrived.reshape(-1, arrived.shape[-1])
    rows_in = lax.all_gather(rows_in, "sub", axis=1, tiled=True)
    projected_pair = jnp.einsum(
        "rd,fd->rf", rows_in, pair_weights, preferred_element_type=jnp.float32
    )
    activation = (
        jax.nn.silu(projected_pair[:, :hidden_units]) * projected_pair[:, hidden_units:]
    ).astype(jnp.bfloat16)
    partial_out = jnp.dot(activation, w_down[0], preferred_element_type=jnp.float32)
    expert_out = lax.psum_scatter(
        partial_out.astype(jnp.bfloat16), "sub", scatter_dimension=1, tiled=True
    )
    results = expert_out.reshape(lead_shape + (expert_out.shape[1],))
    returned = lax.all_to_all(results, ("ep", "hd"), split_axis=0, concat_axis=0, tiled=True)
    mixture = jnp.dot(
        gate_table,
        returned.reshape(all_experts * expert_slots, half_width),
        preferred_element_type=jnp.float32,
    )
    return (widened + mixture).astype(jnp.bfloat16)


def slot_of(step, place, total):
    near = jnp.minimum(place, total - 1 - place)
    odd = place - (step + 1) // 2
    even = place + step // 2
    beside = jnp.where(step % 2 == 1, odd, even)
    beyond = jnp.where(place < total - 1 - place, step, total - 1 - step)
    return jnp.where(step <= 2 * near, beside, beyond)


(C_UP, C_DOWN, N_UP, X_UP, X_DOWN, W_SIDE, W_PART, Z_UP, Z_DOWN, P_SIDE) = range(10)
(C_IN, N_IN, X_IN, W_SIDE_IN, W_PART_IN, Z_IN, P_IN) = range(7)
SIB_COUNT = 15
W_PIECES = 6
X_CUTS = 2
Z_CUTS = 4
LOG2_E = math.log2(math.e)


def semaphore_places(total, tiles):
    arrived = (total, total, X_CUTS * total, W_PIECES, W_PIECES, Z_CUTS * (total + 1), tiles)
    return [sum(arrived[:i]) for i in range(len(arrived) + 1)]


def layer_kernel(
    total, tiles,
    page_len, queries, cache_keys, cache_values, new_keys, new_values, out_proj, residual, gain,
    gate_up, w_down, ids_t, gates_t,
    out,
    q_v, cbuf, nbuf, m_v, l_v, acc_v, att, proj_w, part_out, part_in, res_v, hid, wgu,
    rows, results, chain_in,
    send_sem, recv_sem, load_sem, sib_send, sib_recv, proj_f, out_buf, gate_cols, ids_v, gates_v, gain_v,
):
    e = lax.axis_index("ep")
    h = lax.axis_index("hd")
    s = lax.axis_index("sub")
    part = lax.axis_index("grp")
    last = total - 1
    heads = q_v.shape[0]
    page = new_keys.shape[0]
    page_c = cache_keys.shape[0]
    half = out.shape[2]
    own_rows = out.shape[1]
    features = 2 * half
    scale = LOG2_E / math.sqrt(HD)
    has_up = e < last
    arrived_at = semaphore_places(total, tiles)
    has_down = e > 0

    def col(index, width):
        return pl.ds(pl.multiple_of(index * width, width), width)

    def local(index, src, dst):
        return pltpu.make_async_copy(src, dst, load_sem.at[index])

    barrier = pltpu.get_barrier_semaphore()
    pl.semaphore_signal(barrier, inc=1, device_id={"sub": 1 - s}, device_id_type=MESH)
    pl.semaphore_signal(barrier, inc=1, device_id={"hd": 1 - h}, device_id_type=MESH)
    pl.semaphore_signal(barrier, inc=1, device_id={"grp": 1 - part}, device_id_type=MESH)

    @pl.when(has_up)
    def _():
        pl.semaphore_signal(barrier, inc=1, device_id={"ep": e + 1}, device_id_type=MESH)

    @pl.when(has_down)
    def _():
        pl.semaphore_signal(barrier, inc=1, device_id={"ep": e - 1}, device_id_type=MESH)

    def whole(ref, semaphore):
        pltpu.make_async_copy(ref, ref, semaphore).wait()

    mine = 2 * h + s
    loads = [
        local(0, cache_keys.at[:, col(mine, HD)], cbuf.at[e, s, pl.ds(0, page_c)]),
        local(1, cache_values.at[:, col(mine, HD)], cbuf.at[e, s, pl.ds(page_c, page_c)]),
        local(3, new_keys.at[:, col(mine, HD)], nbuf.at[e, s, pl.ds(0, page)]),
        local(4, new_values.at[:, col(mine, HD)], nbuf.at[e, s, pl.ds(page, page)]),
    ]
    q_loads = [
        local(13, queries.at[:, col(s * heads + i, HD)], q_v.at[i]) for i in range(heads)
    ]
    w_loads = [
        local(5, out_proj, proj_w),
        local(6, residual, res_v),
        local(9, gate_up.at[0], wgu.at[h, pl.ds(0, 2), s]),
        local(10, w_down.at[0], wgu.at[h, 2, s]),
    ]
    small_loads = [local(2, ids_t, ids_v), local(11, gates_t, gates_v), local(12, gain, gain_v)]
    for copy in small_loads + loads + q_loads + w_loads:
        copy.start()

    experts = 2 * total
    lane = lax.broadcasted_iota(jnp.int32, (8, HD), 1)
    seen = jnp.where(lane < page_len[0], 0.0, NEG_FILL)
    for copy in small_loads:
        copy.wait()
    ids = ids_v[...]
    gate_values = gates_v[...].astype(jnp.float32)
    place = lax.broadcasted_iota(jnp.int32, (8, HD), 0)
    by_expert = jnp.zeros((8, HD), jnp.float32)
    for x in range(experts):
        one_row = jnp.sum(jnp.where(ids == x, gate_values, 0.0), axis=0, keepdims=True)
        by_expert = jnp.where(place == x, one_row, by_expert)
    cbuf[e, s, 2 * page_c:2 * page_c + 16, :] = jnp.concatenate(
        [seen, by_expert], axis=0).astype(jnp.bfloat16)

    pl.semaphore_wait(barrier, 3 + has_up.astype(jnp.int32) + has_down.astype(jnp.int32))

    def sibling(index, src, dst, arrival=None):
        return pltpu.make_async_remote_copy(
            src_ref=src, dst_ref=dst, send_sem=sib_send.at[index],
            recv_sem=sib_recv.at[index if arrival is None else arrival],
            device_id={"sub": 1 - s}, device_id_type=MESH)

    def remote(kind, index, arrival, slot, src, dst, where):
        return pltpu.make_async_remote_copy(
            src_ref=src, dst_ref=dst, send_sem=send_sem.at[kind],
            recv_sem=recv_sem.at[arrived_at[arrival] + slot], device_id=where, device_id_type=MESH)

    theirs = 2 * h + 1 - s
    kv_sib = [
        sibling(0, cache_keys.at[:, col(theirs, HD)], cbuf.at[e, s, pl.ds(0, page_c)]),
        sibling(1, cache_values.at[:, col(theirs, HD)], cbuf.at[e, s, pl.ds(page_c, page_c)]),
        sibling(2, cbuf.at[e, s, pl.ds(2 * page_c, 16)], cbuf.at[e, s, pl.ds(2 * page_c, 16)]),
        sibling(3, new_keys.at[:, col(theirs, HD)], nbuf.at[e, s, pl.ds(0, page)]),
        sibling(4, new_values.at[:, col(theirs, HD)], nbuf.at[e, s, pl.ds(page, page)]),
    ]
    w_sib = [
        sibling(5, gate_up.at[0], wgu.at[h, pl.ds(0, 2), s]),
        sibling(6, w_down.at[0], wgu.at[h, 2, s]),
    ]
    for copy in kv_sib:
        copy.start()

    cut = wgu.shape[3] // 2
    piece_rows = cut // 2

    def cut_rows(which, piece):
        return pl.ds(pl.multiple_of(which * cut + piece % 2 * piece_rows, piece_rows), piece_rows)

    def w_block(piece, which):
        return wgu.at[1 - h, piece // 2, s, cut_rows(which, piece)]

    def w_side(piece):
        kind = piece // 2
        src = (w_down.at[0, cut_rows(part, piece)] if kind == 2
               else gate_up.at[0, kind, cut_rows(part, piece)])
        return remote(W_SIDE, piece, W_SIDE_IN, piece, src,
                      wgu.at[h, kind, s, cut_rows(part, piece)], {"hd": 1 - h})

    def w_part(piece):
        block_ref = w_block(piece, part)
        return remote(W_PART, piece, W_PART_IN, piece, block_ref, block_ref, {"grp": 1 - part})

    def w_near(piece, which):
        block_ref = w_block(piece, jnp.where(which == 0, part, 1 - part))
        return sibling(11, block_ref, block_ref, 11 + piece // 4)

    def w_from_side(piece):
        block_ref = w_block(piece, part)
        remote(W_SIDE, piece, W_SIDE_IN, piece, block_ref, block_ref, {"hd": 1 - h}).wait_recv()
        w_part(piece).start()
        w_near(piece, 0).start()

    def w_from_part(piece):
        w_part(piece).wait_recv()
        w_near(piece, 1).start()

    for piece in range(W_PIECES):
        w_side(piece).start()

    def c_up(i):
        return remote(C_UP, i, C_IN, i, cbuf.at[i], cbuf.at[i], {"ep": e + 1})

    def c_down(i):
        return remote(C_DOWN, i, C_IN, i, cbuf.at[i], cbuf.at[i], {"ep": e - 1})

    def n_up(i):
        return remote(N_UP, i, N_IN, i, nbuf.at[i], nbuf.at[i], {"ep": e + 1})

    for copy in loads:
        copy.wait()
    for copy in kv_sib:
        copy.wait_recv()

    @pl.when(has_up)
    def _():
        n_up(e).start()
        c_up(e).start()

    @pl.when(has_down)
    def _():
        c_down(e).start()

    for copy in w_sib:
        copy.start()
    whole(q_v, load_sem.at[13])

    def parts_of(buf, index, size):
        return (buf[index, :, 0:size, :].reshape(2 * size, HD),
                buf[index, :, size:2 * size, :].reshape(2 * size, HD))

    def attend(index, with_cache, with_new, causal, first=False):
        pieces = []
        if with_cache:
            pieces.append(parts_of(cbuf, index, page_c))
            line = jnp.concatenate(
                [cbuf[index, 0, 2 * page_c:2 * page_c + 16, :],
                 cbuf[index, 1, 2 * page_c:2 * page_c + 16, :]], axis=1)[0:1].astype(jnp.float32)
        if with_new:
            pieces.append(parts_of(nbuf, index, page))

        def one_head(i, carry):
            query = q_v[i]
            scores = []
            for place, (key_part, _) in enumerate(pieces):
                one = lax.dot_general(
                    query, key_part, (((1,), (1,)), ((), ())), preferred_element_type=jnp.float32)
                if with_cache and place == 0:
                    one = one + line
                elif causal:
                    r = lax.broadcasted_iota(jnp.int32, one.shape, 0)
                    c = lax.broadcasted_iota(jnp.int32, one.shape, 1)
                    one = jnp.where(c <= r, one, NEG_FILL)
                scores.append(one)
            top = jnp.max(functools.reduce(
                jnp.maximum, [one[:, j:j + HD] for one in scores for j in range(0, one.shape[1], HD)]),
                axis=1, keepdims=True)
            if first:
                new = jnp.broadcast_to(top, m_v.shape[1:])
            else:
                old = m_v[i]
                new = jnp.maximum(old, top)
                factor = jnp.exp2((old - new) * scale)
            new_col = new[:, 0:1]
            weighted = None
            lane_sum = None
            for one, (_, value_part) in zip(scores, pieces):
                p = jnp.exp2((one - new_col) * scale)
                term = jnp.dot(p.astype(jnp.bfloat16), value_part, preferred_element_type=jnp.float32)
                weighted = term if weighted is None else weighted + term
                for j in range(0, p.shape[1], HD):
                    piece_sum = p[:, j:j + HD]
                    lane_sum = piece_sum if lane_sum is None else lane_sum + piece_sum
            m_v[i] = new
            if first:
                l_v[i] = lane_sum
                acc_v[i] = weighted
            else:
                l_v[i] = l_v[i] * factor + lane_sum
                acc_v[i] = acc_v[i] * factor + weighted
            return carry

        lax.fori_loop(0, heads, one_head, 0, unroll=8)

    attend(e, True, True, True, True)

    middle = jnp.logical_and(has_up, has_down)
    low_side = e < total // 2

    def kv_arrive(t):
        @pl.when(jnp.logical_not(middle))
        def _():
            i = slot_of(t, e, total)

            @pl.when(i < e)
            def _():
                n_up(i).wait_recv()
            c_up(i).wait_recv()

        @pl.when(jnp.logical_and(middle, t == 1))
        def _():
            n_up(e - 1).wait_recv()
            n_up(e - 1).start()
            c_down(e + 1).wait_recv()
            c_down(e + 1).start()
            c_up(e - 1).wait_recv()
            c_up(e - 1).start()

        @pl.when(jnp.logical_and(jnp.logical_and(middle, low_side), t == 2))
        def _():
            c_down(last).wait_recv()
            c_down(last).start()

        @pl.when(jnp.logical_and(middle, jnp.logical_not(low_side)))
        def _():
            @pl.when(t == 2)
            def _():
                n_up(0).wait_recv()
                n_up(0).start()

            @pl.when(t == 3)
            def _():
                c_up(0).wait_recv()
                c_up(0).start()

    def kv_step(t, carry):
        i = slot_of(t, e, total)
        below = i < e
        kv_arrive(t)

        @pl.when(t == 1)
        def _():
            w_from_side(0)

        @pl.when(jnp.logical_and(t == 3, jnp.logical_not(middle)))
        def _():
            w_from_side(3)

        @pl.when(below)
        def _():
            attend(i, True, True, False)

        @pl.when(jnp.logical_not(below))
        def _():
            attend(i, True, False, False)

        @pl.when(t == 1)
        def _():
            w_from_side(1)

        @pl.when(t == 2)
        def _():
            w_from_side(2)

        @pl.when(t == 3)
        def _():
            @pl.when(middle)
            def _():
                w_from_side(3)
            w_from_part(0)
        return carry

    lax.fori_loop(1, total, kv_step, 0)

    def gate_step(i, carry):
        flat = cbuf[i, 0, 2 * page_c:2 * page_c + 16, :].astype(jnp.float32)[8:16]
        gate_cols[i] = jnp.concatenate(
            [flat, jnp.zeros((HD - 8, HD), jnp.float32)], axis=0).T
        return carry

    block = 2 * own_rows

    def block_at(which):
        return pl.ds(pl.multiple_of(which * block, block), block)

    def att_rows(which):
        return att.at[s, block_at(which)]

    def finish(which):
        for i in range(heads):
            att[s, block_at(which), i * HD:(i + 1) * HD] = (
                acc_v[i, block_at(which), :]
                / jnp.sum(l_v[i, block_at(which), :], axis=1, keepdims=True)).astype(jnp.bfloat16)

    finish(1 - h)
    att_sib = sibling(7, att_rows(1 - h), att_rows(1 - h))
    att_sib.start()
    finish(h)
    att_own = sibling(9, att_rows(h), att_rows(h))
    att_own.start()
    for copy in w_loads[:2]:
        copy.wait()
    att_sib.wait_recv()

    width = half // tiles
    side_width = half // (tiles // X_CUTS)
    contract = att.shape[2]

    x_rows = own_rows // X_CUTS

    def x_cut(i, k):
        return rows.at[i, pl.ds(k * x_rows, x_rows)]

    def x_up(i, k):
        return remote(X_UP, X_CUTS * i + k, X_IN, X_CUTS * i + k, x_cut(i, k), x_cut(i, k),
                      {"ep": e + 1})

    def x_down(i, k):
        return remote(X_DOWN, X_CUTS * i + k, X_IN, X_CUTS * i + k, x_cut(i, k), x_cut(i, k),
                      {"ep": e - 1})

    def z_up(i, c):
        place = i + c * (total + 1)
        return remote(Z_UP, i + c * total, Z_IN, place, results.at[i, c], chain_in.at[i, c], {"ep": e + 1})

    def z_down(i, c):
        slot = jnp.where(i == e - 1, total, i)
        return remote(Z_DOWN, i + c * total, Z_IN, slot + c * (total + 1),
                      results.at[i, c], chain_in.at[slot, c], {"ep": e - 1})

    def project(a0, a1, j, size):
        return jnp.dot(
            a0, proj_w[0:contract, col(j, size)], preferred_element_type=jnp.float32
        ) + jnp.dot(
            a1, proj_w[contract:2 * contract, col(j, size)], preferred_element_type=jnp.float32)

    def p_side(j):
        return remote(P_SIDE, j, P_IN, j, part_out.at[j], part_in.at[j], {"hd": 1 - h})

    def project_theirs(j, carry):
        first = (1 - h) * block + j // (tiles // X_CUTS) * x_rows
        a0, a1 = [
            jnp.concatenate([
                att[which, pl.ds(pl.multiple_of(first + u * own_rows, x_rows), x_rows), :]
                for u in range(2)], axis=0)
            for which in range(2)]
        part_out[j] = project(a0, a1, j % (tiles // X_CUTS), side_width).astype(jnp.bfloat16)
        p_side(j).start()
        return carry

    lax.fori_loop(0, tiles, project_theirs, 0)
    w_from_side(4)
    w_from_part(1)
    att_own.wait_recv()

    def project_keep(j, carry):
        own = pl.ds(pl.multiple_of(h * block, block), block)
        proj_f[:, col(j, width)] = project(att[0, own, :], att[1, own, :], j, width)
        return carry

    lax.fori_loop(0, tiles, project_keep, 0)
    lax.fori_loop(0, total, gate_step, 0)
    w_from_side(5)
    w_from_part(2)
    w_from_part(3)

    def my_rows(which):
        return pl.ds(pl.multiple_of(which * own_rows, own_rows), own_rows)

    def my_cut(which, k):
        return pl.ds(pl.multiple_of(which * own_rows + k * x_rows, x_rows), x_rows)

    def hid_sib(k):
        return sibling(8 + 2 * k, res_v.at[my_cut(1 - s, k)], hid.at[s, pl.ds(k * x_rows, x_rows)])

    for copy in w_loads[2:]:
        copy.wait()
    for copy in w_sib:
        copy.wait_recv()
    g = gain_v[...].astype(jnp.float32).reshape(1, features)
    for k in range(X_CUTS):
        for j in range(tiles // X_CUTS):
            place = k * (tiles // X_CUTS) + j
            span = slice(j * side_width, (j + 1) * side_width)
            p_side(place).wait_recv()
            for u in range(2):
                cut_u = slice(u * own_rows + k * x_rows, u * own_rows + (k + 1) * x_rows)
                res_v[cut_u, span] = (
                    res_v[cut_u, span].astype(jnp.float32)
                    + (proj_f[cut_u, span]
                       + part_in[place, u * x_rows:(u + 1) * x_rows, :].astype(jnp.float32))
                ).astype(jnp.bfloat16)
        hid_sib(k).start()
        at_k = slice(k * x_rows, (k + 1) * x_rows)
        hid[s, at_k] = res_v[my_cut(s, k), :]
        hid_sib(k).wait_recv()
        h0 = hid[0, at_k].astype(jnp.float32)
        h1 = hid[1, at_k].astype(jnp.float32)
        square = jnp.sum(h0 * h0, axis=1, keepdims=True) + jnp.sum(h1 * h1, axis=1, keepdims=True)
        inverse = lax.rsqrt(square / features + EPSILON)
        rows[e, at_k, 0:half] = (h0 * inverse * g[0:1, 0:half]).astype(jnp.bfloat16)
        rows[e, at_k, half:features] = (h1 * inverse * g[0:1, half:features]).astype(jnp.bfloat16)

        @pl.when(has_up)
        def _():
            x_up(e, k).start()

        @pl.when(has_down)
        def _():
            x_down(e, k).start()

    w_from_part(4)
    units = 2 * wgu.shape[3]
    dims = (((1,), (1,)), ((), ()))
    down_width = features // Z_CUTS

    def turn(k):
        return Z_CUTS // 2 * jnp.where(k < Z_CUTS // 2, 1 - s, s) + k % (Z_CUTS // 2)

    def arrive_near(k):
        @pl.when(middle)
        def _():
            x_up(e - 1, k).wait_recv()
            x_up(e - 1, k).start()
            x_down(e + 1, k).wait_recv()
            x_down(e + 1, k).start()

    def arrive(t):
        @pl.when(jnp.logical_and(jnp.logical_not(middle), t > 0))
        def _():
            for k in range(X_CUTS):
                x_up(slot_of(t, e, total), k).wait_recv()

        @pl.when(t == 1)
        def _():
            for k in range(X_CUTS):
                arrive_near(k)

    def arrive_far(t):
        for k in range(X_CUTS):
            @pl.when(jnp.logical_and(middle, t == 1 + k))
            def _():
                @pl.when(low_side)
                def _():
                    x_down(last, k).wait_recv()
                    x_down(last, k).start()

                @pl.when(jnp.logical_not(low_side))
                def _():
                    x_up(0, k).wait_recv()
                    x_up(0, k).start()

    def expert_step(t, carry):
        i = slot_of(t, e, total)

        @pl.when(t == 0)
        def _():
            whole(wgu.at[1 - h, pl.ds(0, 2), s], sib_recv.at[11])

        arrive(t)
        x = rows[i]
        activations = []
        for which in range(2):
            gate_part = lax.dot_general(
                x, wgu[which, 0].reshape(units, features), dims, preferred_element_type=jnp.float32)
            up_part = lax.dot_general(
                x, wgu[which, 1].reshape(units, features), dims, preferred_element_type=jnp.float32)
            activations.append(
                (gate_part / (1.0 + jnp.exp(-gate_part)) * up_part).astype(jnp.bfloat16))
        gates_all = gate_cols[i, my_rows(s), :]
        gate_lane = lax.broadcasted_iota(jnp.int32, gates_all.shape, 1)
        weight = [
            jnp.sum(jnp.where(gate_lane == 2 * e + which, gates_all, 0.0), axis=1, keepdims=True)
            for which in range(2)
        ]

        arrive_far(t)

        @pl.when(t == 0)
        def _():
            w_from_part(5)
            whole(wgu.at[1 - h, 2, s], sib_recv.at[12])

        for k in range(Z_CUTS):
            c = turn(k)
            mixed = None
            for which in range(2):
                piece = weight[which] * jnp.dot(
                    activations[which],
                    wgu[which, 2, :, :, col(c, down_width)].reshape(units, down_width),
                    preferred_element_type=jnp.float32)
                mixed = piece if mixed is None else mixed + piece
            results[i, c] = mixed.astype(jnp.bfloat16)

            @pl.when(jnp.logical_and(i > e, jnp.logical_not(has_down)))
            def _():
                z_up(i, c).start()

            @pl.when(jnp.logical_and(i < e, jnp.logical_not(has_up)))
            def _():
                z_down(i, c).start()
        return carry

    lax.fori_loop(0, total, expert_step, 0)

    def add_chain(i, c):
        z_up(i, c).wait_recv()
        results[i, c] = (
            results[i, c].astype(jnp.float32) + chain_in[i, c].astype(jnp.float32)
        ).astype(jnp.bfloat16)

    def relay_up(i, k):
        c = turn(k)
        add_chain(i, c)
        z_up(i, c).start()

    def relay_down(i, k):
        c = turn(k)
        add_chain(i, c)
        z_down(i, c).start()

    @pl.when(jnp.logical_and(middle, low_side))
    def _():
        for k in range(Z_CUTS):
            relay_up(e + 1, k)
        for k in range(Z_CUTS + 2):
            if k < Z_CUTS:
                relay_up(last, k)
            if k >= 2:
                relay_down(0, k - 2)

    @pl.when(jnp.logical_and(middle, jnp.logical_not(low_side)))
    def _():
        for k in range(Z_CUTS):
            relay_down(e - 1, k)
        for k in range(Z_CUTS + 2):
            if k < Z_CUTS:
                relay_down(0, k)
            if k >= 2:
                relay_up(last, k - 2)

    def out_sib(q):
        return sibling(13 + q, out_buf.at[q], out.at[s, :, pl.ds(q * down_width, down_width)])

    for k in range(Z_CUTS):
        c = turn(k)
        q = k % 2

        @pl.when(has_down)
        def _():
            z_up(e, c).wait_recv()

        @pl.when(has_up)
        def _():
            place = total + c * (total + 1)
            block_ref = chain_in.at[total, c]
            remote(Z_UP, 0, Z_IN, place, block_ref, block_ref, {"ep": e + 1}).wait_recv()
        side = jnp.where(k < Z_CUTS // 2, 1 - s, s)
        value = results[e, c].astype(jnp.float32)
        value = value + jnp.where(has_down, chain_in[e, c].astype(jnp.float32), 0.0)
        value = value + jnp.where(has_up, chain_in[total, c].astype(jnp.float32), 0.0)
        value = hid[side, :, q * down_width:(q + 1) * down_width].astype(jnp.float32) + value
        if k < Z_CUTS // 2:
            out_buf[q] = value.astype(jnp.bfloat16)
            out_sib(q).start()
        else:
            out[s, :, q * down_width:(q + 1) * down_width] = value.astype(jnp.bfloat16)
    for q in range(2):
        out_sib(q).wait_recv()

    whole(wgu.at[h, :, s, pl.ds(0, cut)], send_sem.at[W_SIDE])
    whole(wgu.at[h, :, s, pl.ds(0, cut)], send_sem.at[W_PART])
    whole(wgu.at[1 - h, :, s], sib_send.at[11])
    whole(part_out, send_sem.at[P_SIDE])
    for copy in kv_sib + w_sib + [att_sib, att_own, hid_sib(0), hid_sib(1), out_sib(0), out_sib(1)]:
        copy.wait_send()

    for i in range(total):
        sends_up = [(N_UP, nbuf, i + 1), (C_UP, cbuf, i + 1), (X_UP, rows, i + 1),
                    (Z_UP, results, last - i)]
        sends_down = [(C_DOWN, cbuf, total - i), (X_DOWN, rows, total - i), (Z_DOWN, results, i)]
        sends = (sends_up if i < last else []) + (sends_down if i > 0 else [])

        @pl.when(e == i)
        def _():
            for kind, ref, count in sends:
                whole(ref.at[pl.ds(0, count)], send_sem.at[kind])


def fused_shards(
    queries, cache_keys, cache_values, page_len, new_keys, new_values, out_proj, residual,
    norm_gain, gate_up, w_down, expert_ids, gates,
):
    total = lax.axis_size("ep")
    all_experts = total * lax.axis_size("hd")
    query_rows = queries.shape[0]
    heads = queries.shape[1] // HD // 2
    block_rows, half = residual.shape
    features = 2 * half
    own_rows = block_rows // 2
    page_c, page = cache_keys.shape[0], new_keys.shape[0]
    hidden = w_down.shape[1]
    tiles = 4
    arrived = semaphore_places(total, tiles)[-1]
    anywhere = pl.BlockSpec(memory_space=pl.ANY)
    bf, f32 = jnp.bfloat16, jnp.float32
    ids_rows, gate_rows = expert_ids.T, gates.T
    out = pl.pallas_call(
        functools.partial(layer_kernel, total, tiles),
        out_shape=pltpu.VMEM((2, own_rows, half), bf),
        in_specs=[pl.BlockSpec(memory_space=pltpu.SMEM)] + [anywhere] * 12,
        out_specs=pl.BlockSpec(memory_space=pltpu.VMEM),
        scratch_shapes=[
            pltpu.VMEM((heads, query_rows, HD), bf),
            pltpu.VMEM((total, 2, 2 * page_c + 16, HD), bf),
            pltpu.VMEM((total, 2, 2 * page, HD), bf),
            pltpu.VMEM((heads, query_rows, HD), f32),
            pltpu.VMEM((heads, query_rows, HD), f32),
            pltpu.VMEM((heads, query_rows, HD), f32),
            pltpu.VMEM((2, query_rows, heads * HD), bf),
            pltpu.VMEM(out_proj.shape, bf),
            pltpu.VMEM((tiles, own_rows, half // 2), bf),
            pltpu.VMEM((tiles, own_rows, half // 2), bf),
            pltpu.VMEM((block_rows, half), bf),
            pltpu.VMEM((2, own_rows, half), bf),
            pltpu.VMEM((2, 3, 2, hidden, features), bf),
            pltpu.VMEM((total, own_rows, features), bf),
            pltpu.VMEM((total, Z_CUTS, own_rows, features // Z_CUTS), bf),
            pltpu.VMEM((total + 1, Z_CUTS, own_rows, features // Z_CUTS), bf),
            pltpu.SemaphoreType.DMA((10,)),
            pltpu.SemaphoreType.DMA((arrived,)),
            pltpu.SemaphoreType.DMA((14,)),
            pltpu.SemaphoreType.DMA((SIB_COUNT,)),
            pltpu.SemaphoreType.DMA((SIB_COUNT,)),
            pltpu.VMEM((block_rows, half), f32),
            pltpu.VMEM((2, own_rows, features // Z_CUTS), bf),
            pltpu.VMEM((total, 2 * own_rows, 128), f32),
            pltpu.VMEM(ids_rows.shape, jnp.int32),
            pltpu.VMEM(gate_rows.shape, bf),
            pltpu.VMEM(norm_gain.shape, bf),
        ],
        compiler_params=pltpu.CompilerParams(
            collective_id=0, has_side_effects=True, vmem_limit_bytes=58 * 1024 * 1024
        ),
    )(page_len, queries, cache_keys, cache_values, new_keys, new_values, out_proj, residual,
      norm_gain, gate_up, w_down, ids_rows, gate_rows)
    return out.reshape(block_rows, half)


def layer(*arguments):
    queries, page_rows, ids = arguments[0], arguments[4].shape[0], arguments[11]
    pair = lax.axis_size("ep") >= 4 and lax.axis_size("grp") == 2
    pair = pair and lax.axis_size("hd") == 2 and lax.axis_size("sub") == 2
    slots = block_sizes(ids.shape[0], lax.axis_size("ep"), lax.axis_size("hd"))[1]
    group_width = QH // KVH
    whole_heads = queries.shape[1] == 2 * group_width * HD
    whole_pages = page_rows == 128 and arguments[1].shape[0] == 128
    rows_fit = queries.shape[0] == 2 * page_rows and ids.shape == (128, 8)
    rows_fit = rows_fit and lax.axis_size("ep") == 4
    if pair and slots == ids.shape[0] and whole_heads and whole_pages and rows_fit:
        return fused_shards(*arguments)
    return shards(*arguments)


def solution(mesh):
    return jax.shard_map(
        layer,
        mesh=mesh,
        in_specs=(
            P(("grp", "ep"), "hd"),
            P(("grp", "ep", "sub"), None),
            P(("grp", "ep", "sub"), None),
            P(("grp", "ep", "sub")),
            P(("grp", "ep", "sub"), None),
            P(("grp", "ep", "sub"), None),
            P("hd", "sub"),
            P(("grp", "ep", "hd"), "sub"),
            P(),
            P(("ep", "hd"), None, "sub", None),
            P(("ep", "hd"), "sub", None),
            P(("grp", "ep", "hd"), None),
            P(("grp", "ep", "hd"), None),
        ),
        out_specs=P(("grp", "ep", "hd"), "sub"),
        check_vma=False,
    )
```

```python
import functools
import math

import jax
import jax.numpy as jnp
from jax import lax
from jax.experimental import pallas as pl
from jax.experimental.pallas import tpu as pltpu
from jax.sharding import PartitionSpec as P

QH = 32
KVH = 4
HD = 128
GROUPS_ROW = 4


NEG_FILL = -1e30
EPSILON = 1e-06
KEY_BLOCK = 1024
FAR_RANK = 1073741824
MESH = pl.DeviceIdType.MESH


def joined(x, axis, join):
    gathered = jax.tree.map(
        lambda a, kind: lax.all_gather(a.astype(kind), axis),
        x,
        jax.tree.map(lambda a: jnp.bfloat16 if a.dtype == jnp.float32 else a.dtype, x),
    )

    def take(source):
        return jax.tree.map(
            lambda a, own: lax.dynamic_index_in_dim(a, source, 0, False).astype(own.dtype),
            gathered,
            x,
        )

    return lax.fori_loop(
        1, lax.axis_size(axis), lambda source, state: join(state, take(source)), take(0)
    )


def block_sizes(block_rows, group_total, experts_group):
    group_slots = min(block_rows, 3 * GROUPS_ROW * block_rows // (2 * group_total))
    return (group_slots, 2 * group_slots // experts_group)


def attend_block(fold_state, packed, key_rank, query_heads, row_ids, kv_heads):
    running_max, weight_sum, weighted = fold_state
    half_cols = packed.shape[1] // 2
    length = packed.shape[0]
    key_part = packed[:, :half_cols].reshape(length, kv_heads, half_cols // kv_heads)
    value_part = packed[:, half_cols:].reshape(length, kv_heads, half_cols // kv_heads)
    scores = jnp.einsum(
        "rkqd,lkd->rkql", query_heads, key_part, preferred_element_type=jnp.float32
    ) * (1.0 / math.sqrt(HD))
    allowed = (key_rank[None, :] <= row_ids[:, None])[:, None, None, :]
    masked = jnp.where(allowed, scores, NEG_FILL)
    new_max = jnp.maximum(running_max, jnp.max(masked, axis=3))
    factor = jnp.exp(running_max - new_max)
    exp_terms = jnp.where(allowed, jnp.exp(scores - new_max[..., None]), 0.0)
    weight_sum = weight_sum * factor + jnp.sum(exp_terms, axis=3)
    weighted = weighted * factor[..., None] + jnp.einsum(
        "rkql,lkd->rkqd",
        exp_terms.astype(jnp.bfloat16),
        value_part,
        preferred_element_type=jnp.float32,
    )
    return (new_max, weight_sum, weighted)


def join_parts(first_part, second_part):
    first_max, first_sum, first_weighted = first_part
    second_max, second_sum, second_weighted = second_part
    joint_max = jnp.maximum(first_max, second_max)
    first_factor = jnp.exp(first_max - joint_max)
    second_factor = jnp.exp(second_max - joint_max)
    joint_sum = first_sum * first_factor + second_sum * second_factor
    joint_weighted = (
        first_weighted * first_factor[..., None] + second_weighted * second_factor[..., None]
    )
    return (joint_max, joint_sum, joint_weighted)


def shards(
    queries,
    cache_keys,
    cache_values,
    page_len,
    new_keys,
    new_values,
    out_proj,
    residual,
    norm_gain,
    gate_up,
    w_down,
    expert_ids,
    gates,
):
    query_rows = queries.shape[0]
    heads_here = queries.shape[1] // HD
    group_width = QH // KVH
    kv_heads = max(1, heads_here // group_width)
    per_kv = heads_here // kv_heads
    kv_first = lax.axis_index("hd") * heads_here // group_width

    def kv_columns(source):
        return lax.dynamic_slice_in_dim(source, kv_first * HD, kv_heads * HD, 1)

    local_keys = jnp.concatenate([kv_columns(cache_keys), kv_columns(new_keys)], axis=0)
    local_values = jnp.concatenate([kv_columns(cache_values), kv_columns(new_values)], axis=0)
    packed_local = jnp.concatenate([local_keys, local_values], axis=1)
    cache_rows = cache_keys.shape[0]
    new_rows = new_keys.shape[0]
    cache_rank = jnp.where(
        jnp.arange(cache_rows, dtype=jnp.int32) < page_len[0], -1, FAR_RANK
    ).astype(jnp.int32)
    new_block = lax.axis_index("ep") * lax.axis_size("sub") + lax.axis_index("sub")
    new_rank = new_block * new_rows + jnp.arange(new_rows, dtype=jnp.int32)
    rank_local = jnp.concatenate([cache_rank, new_rank], axis=0)
    row_ids = lax.axis_index("ep") * query_rows + jnp.arange(query_rows, dtype=jnp.int32)
    query_heads = queries.reshape(query_rows, kv_heads, per_kv, HD)

    def fold_keys(fold_state, piece_data):
        packed, key_rank = piece_data
        length = packed.shape[0]
        if length > KEY_BLOCK and length % KEY_BLOCK == 0:
            block_count = length // KEY_BLOCK

            def scan_step(inner_state, block_data):
                return (
                    attend_block(
                        inner_state, block_data[0], block_data[1], query_heads, row_ids, kv_heads
                    ),
                    None,
                )

            fold_state, _ = lax.scan(
                scan_step,
                fold_state,
                (
                    packed.reshape(block_count, KEY_BLOCK, packed.shape[1]),
                    key_rank.reshape(block_count, KEY_BLOCK),
                ),
            )
            return fold_state
        return attend_block(fold_state, packed, key_rank, query_heads, row_ids, kv_heads)

    start_state = (
        jnp.full((query_rows, kv_heads, per_kv), NEG_FILL, jnp.float32),
        jnp.zeros((query_rows, kv_heads, per_kv), jnp.float32),
        jnp.zeros((query_rows, kv_heads, per_kv, HD), jnp.float32),
    )
    fold_state = fold_keys(
        start_state,
        (
            lax.all_gather(packed_local, "ep", axis=0, tiled=True),
            lax.all_gather(rank_local, "ep", axis=0, tiled=True),
        ),
    )
    running_max, weight_sum, weighted = joined(fold_state, "sub", join_parts)
    attended = (
        (weighted / weight_sum[..., None]).reshape(query_rows, heads_here * HD).astype(jnp.bfloat16)
    )
    projected = lax.psum_scatter(
        jnp.dot(attended, out_proj, preferred_element_type=jnp.float32).astype(jnp.bfloat16),
        "hd",
        scatter_dimension=0,
        tiled=True,
    ).astype(jnp.float32)
    hidden_half = (residual.astype(jnp.float32) + projected).astype(jnp.bfloat16)
    widened = hidden_half.astype(jnp.float32)
    features = norm_gain.shape[0]
    half_width = hidden_half.shape[1]
    square_sum = lax.psum(jnp.sum(widened * widened, axis=1), "sub")
    gain_half = lax.dynamic_slice_in_dim(
        norm_gain, lax.axis_index("sub") * half_width, half_width, 0
    )
    normed = (
        widened
        * lax.rsqrt(square_sum[:, None] / features + EPSILON)
        * gain_half.astype(jnp.float32)
    ).astype(jnp.bfloat16)
    pair_weights = gate_up[0].reshape(-1, features)
    hidden_units = w_down.shape[1]
    group_total = lax.axis_size("ep")
    group_experts = lax.axis_size("hd")
    all_experts = group_total * group_experts
    block_rows = expert_ids.shape[0]
    group_slots, expert_slots = block_sizes(block_rows, group_total, group_experts)
    chosen = (
        expert_ids[:, :, None] == jnp.arange(all_experts, dtype=jnp.int32)[None, None, :]
    ).astype(jnp.int32)
    named_count = jnp.sum(chosen, axis=1)
    earlier = jnp.cumsum(named_count, axis=0) - named_count
    slot_index = jnp.sum(chosen * earlier[:, None, :], axis=2)
    position = expert_ids * expert_slots + slot_index
    slot_columns = jnp.arange(all_experts * expert_slots, dtype=jnp.int32)
    gate_table = jnp.sum(
        jnp.where(
            position[:, :, None] == slot_columns[None, None, :],
            gates.astype(jnp.float32)[:, :, None],
            0.0,
        ),
        axis=1,
    ).astype(jnp.bfloat16)
    placed = (gate_table != 0).astype(jnp.bfloat16)
    outgoing = jnp.einsum("rq,rd->qd", placed, normed, preferred_element_type=jnp.float32).astype(
        jnp.bfloat16
    )
    outgoing = outgoing.reshape(all_experts, expert_slots, normed.shape[1])
    arrived = lax.all_to_all(outgoing, ("ep", "hd"), split_axis=0, concat_axis=0, tiled=True)
    lead_shape = arrived.shape[:-1]
    rows_in = arrived.reshape(-1, arrived.shape[-1])
    rows_in = lax.all_gather(rows_in, "sub", axis=1, tiled=True)
    projected_pair = jnp.einsum(
        "rd,fd->rf", rows_in, pair_weights, preferred_element_type=jnp.float32
    )
    activation = (
        jax.nn.silu(projected_pair[:, :hidden_units]) * projected_pair[:, hidden_units:]
    ).astype(jnp.bfloat16)
    partial_out = jnp.dot(activation, w_down[0], preferred_element_type=jnp.float32)
    expert_out = lax.psum_scatter(
        partial_out.astype(jnp.bfloat16), "sub", scatter_dimension=1, tiled=True
    )
    results = expert_out.reshape(lead_shape + (expert_out.shape[1],))
    returned = lax.all_to_all(results, ("ep", "hd"), split_axis=0, concat_axis=0, tiled=True)
    mixture = jnp.dot(
        gate_table,
        returned.reshape(all_experts * expert_slots, half_width),
        preferred_element_type=jnp.float32,
    )
    return (widened + mixture).astype(jnp.bfloat16)


def slot_of(step, place, total):
    near = jnp.minimum(place, total - 1 - place)
    odd = place - (step + 1) // 2
    even = place + step // 2
    beside = jnp.where(step % 2 == 1, odd, even)
    beyond = jnp.where(place < total - 1 - place, step, total - 1 - step)
    return jnp.where(step <= 2 * near, beside, beyond)


(C_UP, C_DOWN, N_UP, X_UP, X_DOWN, W_SIDE, W_PART, Z_UP, Z_DOWN, P_SIDE) = range(10)
(C_IN, N_IN, X_IN, W_SIDE_IN, W_PART_IN, Z_IN, P_IN) = range(7)
SIB_COUNT = 15
W_PIECES = 6
X_CUTS = 2
Z_CUTS = 4
LOG2_E = math.log2(math.e)


def semaphore_places(total, tiles):
    arrived = (total, total, X_CUTS * total, W_PIECES, W_PIECES, Z_CUTS * (total + 1), tiles)
    return [sum(arrived[:i]) for i in range(len(arrived) + 1)]


def layer_kernel(
    total, tiles,
    page_len, queries, cache_keys, cache_values, new_keys, new_values, out_proj, residual, gain,
    gate_up, w_down, ids_t, gates_t,
    out,
    q_v, cbuf, nbuf, m_v, l_v, acc_v, att, proj_w, part_out, part_in, res_v, hid, wgu,
    rows, results, chain_in,
    send_sem, recv_sem, load_sem, sib_send, sib_recv, proj_f, out_buf, gate_cols, ids_v, gates_v, gain_v,
):
    e = lax.axis_index("ep")
    h = lax.axis_index("hd")
    s = lax.axis_index("sub")
    part = lax.axis_index("grp")
    last = total - 1
    heads = q_v.shape[0]
    page = new_keys.shape[0]
    page_c = cache_keys.shape[0]
    half = out.shape[2]
    own_rows = out.shape[1]
    features = 2 * half
    scale = LOG2_E / math.sqrt(HD)
    has_up = e < last
    arrived_at = semaphore_places(total, tiles)
    has_down = e > 0

    def col(index, width):
        return pl.ds(pl.multiple_of(index * width, width), width)

    def local(index, src, dst):
        return pltpu.make_async_copy(src, dst, load_sem.at[index])

    barrier = pltpu.get_barrier_semaphore()
    pl.semaphore_signal(barrier, inc=1, device_id={"sub": 1 - s}, device_id_type=MESH)
    pl.semaphore_signal(barrier, inc=1, device_id={"hd": 1 - h}, device_id_type=MESH)
    pl.semaphore_signal(barrier, inc=1, device_id={"grp": 1 - part}, device_id_type=MESH)

    @pl.when(has_up)
    def _():
        pl.semaphore_signal(barrier, inc=1, device_id={"ep": e + 1}, device_id_type=MESH)

    @pl.when(has_down)
    def _():
        pl.semaphore_signal(barrier, inc=1, device_id={"ep": e - 1}, device_id_type=MESH)

    def whole(ref, semaphore):
        pltpu.make_async_copy(ref, ref, semaphore).wait()

    mine = 2 * h + s
    loads = [
        local(0, cache_keys.at[:, col(mine, HD)], cbuf.at[e, s, pl.ds(0, page_c)]),
        local(1, cache_values.at[:, col(mine, HD)], cbuf.at[e, s, pl.ds(page_c, page_c)]),
        local(3, new_keys.at[:, col(mine, HD)], nbuf.at[e, s, pl.ds(0, page)]),
        local(4, new_values.at[:, col(mine, HD)], nbuf.at[e, s, pl.ds(page, page)]),
    ]
    q_loads = [
        local(13, queries.at[:, col(s * heads + i, HD)], q_v.at[i]) for i in range(heads)
    ]
    w_loads = [
        local(5, out_proj, proj_w),
        local(6, residual, res_v),
        local(9, gate_up.at[0], wgu.at[h, pl.ds(0, 2), s]),
        local(10, w_down.at[0], wgu.at[h, 2, s]),
    ]
    small_loads = [local(2, ids_t, ids_v), local(11, gates_t, gates_v), local(12, gain, gain_v)]
    for copy in small_loads + loads + q_loads + w_loads:
        copy.start()

    experts = 2 * total
    lane = lax.broadcasted_iota(jnp.int32, (8, HD), 1)
    seen = jnp.where(lane < page_len[0], 0.0, NEG_FILL)
    for copy in small_loads:
        copy.wait()
    ids = ids_v[...]
    gate_values = gates_v[...].astype(jnp.float32)
    place = lax.broadcasted_iota(jnp.int32, (8, HD), 0)
    by_expert = jnp.zeros((8, HD), jnp.float32)
    for x in range(experts):
        one_row = jnp.sum(jnp.where(ids == x, gate_values, 0.0), axis=0, keepdims=True)
        by_expert = jnp.where(place == x, one_row, by_expert)
    cbuf[e, s, 2 * page_c:2 * page_c + 16, :] = jnp.concatenate(
        [seen, by_expert], axis=0).astype(jnp.bfloat16)

    pl.semaphore_wait(barrier, 3 + has_up.astype(jnp.int32) + has_down.astype(jnp.int32))

    def sibling(index, src, dst, arrival=None):
        return pltpu.make_async_remote_copy(
            src_ref=src, dst_ref=dst, send_sem=sib_send.at[index],
            recv_sem=sib_recv.at[index if arrival is None else arrival],
            device_id={"sub": 1 - s}, device_id_type=MESH)

    def remote(kind, index, arrival, slot, src, dst, where):
        return pltpu.make_async_remote_copy(
            src_ref=src, dst_ref=dst, send_sem=send_sem.at[kind],
            recv_sem=recv_sem.at[arrived_at[arrival] + slot], device_id=where, device_id_type=MESH)

    theirs = 2 * h + 1 - s
    kv_sib = [
        sibling(0, cache_keys.at[:, col(theirs, HD)], cbuf.at[e, s, pl.ds(0, page_c)]),
        sibling(1, cache_values.at[:, col(theirs, HD)], cbuf.at[e, s, pl.ds(page_c, page_c)]),
        sibling(2, cbuf.at[e, s, pl.ds(2 * page_c, 16)], cbuf.at[e, s, pl.ds(2 * page_c, 16)]),
        sibling(3, new_keys.at[:, col(theirs, HD)], nbuf.at[e, s, pl.ds(0, page)]),
        sibling(4, new_values.at[:, col(theirs, HD)], nbuf.at[e, s, pl.ds(page, page)]),
    ]
    w_sib = [
        sibling(5, gate_up.at[0], wgu.at[h, pl.ds(0, 2), s]),
        sibling(6, w_down.at[0], wgu.at[h, 2, s]),
    ]
    for copy in kv_sib:
        copy.start()

    cut = wgu.shape[3] // 2
    piece_rows = cut // 2

    def cut_rows(which, piece):
        return pl.ds(pl.multiple_of(which * cut + piece % 2 * piece_rows, piece_rows), piece_rows)

    def w_block(piece, which):
        return wgu.at[1 - h, piece // 2, s, cut_rows(which, piece)]

    def w_side(piece):
        kind = piece // 2
        src = (w_down.at[0, cut_rows(part, piece)] if kind == 2
               else gate_up.at[0, kind, cut_rows(part, piece)])
        return remote(W_SIDE, piece, W_SIDE_IN, piece, src,
                      wgu.at[h, kind, s, cut_rows(part, piece)], {"hd": 1 - h})

    def w_part(piece):
        block_ref = w_block(piece, part)
        return remote(W_PART, piece, W_PART_IN, piece, block_ref, block_ref, {"grp": 1 - part})

    def w_near(piece, which):
        block_ref = w_block(piece, jnp.where(which == 0, part, 1 - part))
        return sibling(11, block_ref, block_ref, 11 + piece // 4)

    def w_from_side(piece):
        block_ref = w_block(piece, part)
        remote(W_SIDE, piece, W_SIDE_IN, piece, block_ref, block_ref, {"hd": 1 - h}).wait_recv()
        w_part(piece).start()
        w_near(piece, 0).start()

    def w_from_part(piece):
        w_part(piece).wait_recv()
        w_near(piece, 1).start()

    for piece in range(W_PIECES):
        w_side(piece).start()

    def c_up(i):
        return remote(C_UP, i, C_IN, i, cbuf.at[i], cbuf.at[i], {"ep": e + 1})

    def c_down(i):
        return remote(C_DOWN, i, C_IN, i, cbuf.at[i], cbuf.at[i], {"ep": e - 1})

    def n_up(i):
        return remote(N_UP, i, N_IN, i, nbuf.at[i], nbuf.at[i], {"ep": e + 1})

    for copy in loads:
        copy.wait()
    for copy in kv_sib:
        copy.wait_recv()

    @pl.when(has_up)
    def _():
        n_up(e).start()
        c_up(e).start()

    @pl.when(has_down)
    def _():
        c_down(e).start()

    for copy in w_sib:
        copy.start()
    whole(q_v, load_sem.at[13])

    def parts_of(buf, index, size):
        return (buf[index, :, 0:size, :].reshape(2 * size, HD),
                buf[index, :, size:2 * size, :].reshape(2 * size, HD))

    def attend(index, with_cache, with_new, causal, first=False):
        pieces = []
        if with_cache:
            pieces.append(parts_of(cbuf, index, page_c))
            line = jnp.concatenate(
                [cbuf[index, 0, 2 * page_c:2 * page_c + 16, :],
                 cbuf[index, 1, 2 * page_c:2 * page_c + 16, :]], axis=1)[0:1].astype(jnp.float32)
        if with_new:
            pieces.append(parts_of(nbuf, index, page))

        def one_head(i, carry):
            query = q_v[i]
            scores = []
            for place, (key_part, _) in enumerate(pieces):
                one = lax.dot_general(
                    query, key_part, (((1,), (1,)), ((), ())), preferred_element_type=jnp.float32)
                if with_cache and place == 0:
                    one = one + line
                elif causal:
                    r = lax.broadcasted_iota(jnp.int32, one.shape, 0)
                    c = lax.broadcasted_iota(jnp.int32, one.shape, 1)
                    one = jnp.where(c <= r, one, NEG_FILL)
                scores.append(one)
            top = jnp.max(functools.reduce(
                jnp.maximum, [one[:, j:j + HD] for one in scores for j in range(0, one.shape[1], HD)]),
                axis=1, keepdims=True)
            if first:
                new = jnp.broadcast_to(top, m_v.shape[1:])
            else:
                old = m_v[i]
                new = jnp.maximum(old, top)
                factor = jnp.exp2((old - new) * scale)
            new_col = new[:, 0:1]
            weighted = None
            lane_sum = None
            for one, (_, value_part) in zip(scores, pieces):
                p = jnp.exp2((one - new_col) * scale)
                term = jnp.dot(p.astype(jnp.bfloat16), value_part, preferred_element_type=jnp.float32)
                weighted = term if weighted is None else weighted + term
                for j in range(0, p.shape[1], HD):
                    piece_sum = p[:, j:j + HD]
                    lane_sum = piece_sum if lane_sum is None else lane_sum + piece_sum
            m_v[i] = new
            if first:
                l_v[i] = lane_sum
                acc_v[i] = weighted
            else:
                l_v[i] = l_v[i] * factor + lane_sum
                acc_v[i] = acc_v[i] * factor + weighted
            return carry

        lax.fori_loop(0, heads, one_head, 0, unroll=8)

    attend(e, True, True, True, True)

    middle = jnp.logical_and(has_up, has_down)
    low_side = e < total // 2

    def kv_arrive(t):
        @pl.when(jnp.logical_not(middle))
        def _():
            i = slot_of(t, e, total)

            @pl.when(i < e)
            def _():
                n_up(i).wait_recv()
            c_up(i).wait_recv()

        @pl.when(jnp.logical_and(middle, t == 1))
        def _():
            n_up(e - 1).wait_recv()
            n_up(e - 1).start()
            c_down(e + 1).wait_recv()
            c_down(e + 1).start()
            c_up(e - 1).wait_recv()
            c_up(e - 1).start()

        @pl.when(jnp.logical_and(jnp.logical_and(middle, low_side), t == 2))
        def _():
            c_down(last).wait_recv()
            c_down(last).start()

        @pl.when(jnp.logical_and(middle, jnp.logical_not(low_side)))
        def _():
            @pl.when(t == 2)
            def _():
                n_up(0).wait_recv()
                n_up(0).start()

            @pl.when(t == 3)
            def _():
                c_up(0).wait_recv()
                c_up(0).start()

    def kv_step(t, carry):
        i = slot_of(t, e, total)
        below = i < e
        kv_arrive(t)

        @pl.when(t == 1)
        def _():
            w_from_side(0)

        @pl.when(jnp.logical_and(t == 3, jnp.logical_not(middle)))
        def _():
            w_from_side(3)

        @pl.when(below)
        def _():
            attend(i, True, True, False)

        @pl.when(jnp.logical_not(below))
        def _():
            attend(i, True, False, False)

        @pl.when(t == 1)
        def _():
            w_from_side(1)

        @pl.when(t == 2)
        def _():
            w_from_side(2)

        @pl.when(t == 3)
        def _():
            @pl.when(middle)
            def _():
                w_from_side(3)
            w_from_part(0)
        return carry

    lax.fori_loop(1, total, kv_step, 0)

    def gate_step(i, carry):
        flat = cbuf[i, 0, 2 * page_c:2 * page_c + 16, :].astype(jnp.float32)[8:16]
        gate_cols[i] = jnp.concatenate(
            [flat, jnp.zeros((HD - 8, HD), jnp.float32)], axis=0).T
        return carry

    block = 2 * own_rows

    def block_at(which):
        return pl.ds(pl.multiple_of(which * block, block), block)

    def att_rows(which):
        return att.at[s, block_at(which)]

    def finish(which):
        for i in range(heads):
            att[s, block_at(which), i * HD:(i + 1) * HD] = (
                acc_v[i, block_at(which), :]
                / jnp.sum(l_v[i, block_at(which), :], axis=1, keepdims=True)).astype(jnp.bfloat16)

    finish(1 - h)
    att_sib = sibling(7, att_rows(1 - h), att_rows(1 - h))
    att_sib.start()
    finish(h)
    att_own = sibling(9, att_rows(h), att_rows(h))
    att_own.start()
    for copy in w_loads[:2]:
        copy.wait()
    att_sib.wait_recv()

    width = half // tiles
    side_width = half // (tiles // X_CUTS)
    contract = att.shape[2]

    x_rows = own_rows // X_CUTS

    def x_cut(i, k):
        return rows.at[i, pl.ds(k * x_rows, x_rows)]

    def x_up(i, k):
        return remote(X_UP, X_CUTS * i + k, X_IN, X_CUTS * i + k, x_cut(i, k), x_cut(i, k),
                      {"ep": e + 1})

    def x_down(i, k):
        return remote(X_DOWN, X_CUTS * i + k, X_IN, X_CUTS * i + k, x_cut(i, k), x_cut(i, k),
                      {"ep": e - 1})

    def z_up(i, c):
        place = i + c * (total + 1)
        return remote(Z_UP, i + c * total, Z_IN, place, results.at[i, c], chain_in.at[i, c], {"ep": e + 1})

    def z_down(i, c):
        slot = jnp.where(i == e - 1, total, i)
        return remote(Z_DOWN, i + c * total, Z_IN, slot + c * (total + 1),
                      results.at[i, c], chain_in.at[slot, c], {"ep": e - 1})

    def project(a0, a1, j, size):
        return jnp.dot(
            a0, proj_w[0:contract, col(j, size)], preferred_element_type=jnp.float32
        ) + jnp.dot(
            a1, proj_w[contract:2 * contract, col(j, size)], preferred_element_type=jnp.float32)

    def p_side(j):
        return remote(P_SIDE, j, P_IN, j, part_out.at[j], part_in.at[j], {"hd": 1 - h})

    def project_theirs(j, carry):
        first = (1 - h) * block + j // (tiles // X_CUTS) * x_rows
        a0, a1 = [
            jnp.concatenate([
                att[which, pl.ds(pl.multiple_of(first + u * own_rows, x_rows), x_rows), :]
                for u in range(2)], axis=0)
            for which in range(2)]
        part_out[j] = project(a0, a1, j % (tiles // X_CUTS), side_width).astype(jnp.bfloat16)
        p_side(j).start()
        return carry

    lax.fori_loop(0, tiles, project_theirs, 0)
    w_from_side(4)
    w_from_part(1)
    att_own.wait_recv()

    def project_keep(j, carry):
        own = pl.ds(pl.multiple_of(h * block, block), block)
        proj_f[:, col(j, width)] = project(att[0, own, :], att[1, own, :], j, width)
        return carry

    lax.fori_loop(0, tiles, project_keep, 0)
    lax.fori_loop(0, total, gate_step, 0)
    w_from_side(5)
    w_from_part(2)
    w_from_part(3)

    def my_rows(which):
        return pl.ds(pl.multiple_of(which * own_rows, own_rows), own_rows)

    def my_cut(which, k):
        return pl.ds(pl.multiple_of(which * own_rows + k * x_rows, x_rows), x_rows)

    def hid_sib(k):
        return sibling(8 + 2 * k, res_v.at[my_cut(1 - s, k)], hid.at[s, pl.ds(k * x_rows, x_rows)])

    for copy in w_loads[2:]:
        copy.wait()
    for copy in w_sib:
        copy.wait_recv()
    g = gain_v[...].astype(jnp.float32).reshape(1, features)
    for k in range(X_CUTS):
        for j in range(tiles // X_CUTS):
            place = k * (tiles // X_CUTS) + j
            span = slice(j * side_width, (j + 1) * side_width)
            p_side(place).wait_recv()
            for u in range(2):
                cut_u = slice(u * own_rows + k * x_rows, u * own_rows + (k + 1) * x_rows)
                res_v[cut_u, span] = (
                    res_v[cut_u, span].astype(jnp.float32)
                    + (proj_f[cut_u, span]
                       + part_in[place, u * x_rows:(u + 1) * x_rows, :].astype(jnp.float32))
                ).astype(jnp.bfloat16)
        hid_sib(k).start()
        at_k = slice(k * x_rows, (k + 1) * x_rows)
        hid[s, at_k] = res_v[my_cut(s, k), :]
        hid_sib(k).wait_recv()
        h0 = hid[0, at_k].astype(jnp.float32)
        h1 = hid[1, at_k].astype(jnp.float32)
        square = jnp.sum(h0 * h0, axis=1, keepdims=True) + jnp.sum(h1 * h1, axis=1, keepdims=True)
        inverse = lax.rsqrt(square / features + EPSILON)
        rows[e, at_k, 0:half] = (h0 * inverse * g[0:1, 0:half]).astype(jnp.bfloat16)
        rows[e, at_k, half:features] = (h1 * inverse * g[0:1, half:features]).astype(jnp.bfloat16)

        @pl.when(has_up)
        def _():
            x_up(e, k).start()

        @pl.when(has_down)
        def _():
            x_down(e, k).start()

    w_from_part(4)
    units = 2 * wgu.shape[3]
    dims = (((1,), (1,)), ((), ()))
    down_width = features // Z_CUTS

    def turn(k):
        return Z_CUTS // 2 * jnp.where(k < Z_CUTS // 2, 1 - s, s) + k % (Z_CUTS // 2)

    def arrive_near(k):
        @pl.when(middle)
        def _():
            x_up(e - 1, k).wait_recv()
            x_up(e - 1, k).start()
            x_down(e + 1, k).wait_recv()
            x_down(e + 1, k).start()

    def arrive(t):
        @pl.when(jnp.logical_and(jnp.logical_not(middle), t > 0))
        def _():
            for k in range(X_CUTS):
                x_up(slot_of(t, e, total), k).wait_recv()

        @pl.when(t == 1)
        def _():
            for k in range(X_CUTS):
                arrive_near(k)

    def arrive_far(t):
        for k in range(X_CUTS):
            @pl.when(jnp.logical_and(middle, t == 1 + k))
            def _():
                @pl.when(low_side)
                def _():
                    x_down(last, k).wait_recv()
                    x_down(last, k).start()

                @pl.when(jnp.logical_not(low_side))
                def _():
                    x_up(0, k).wait_recv()
                    x_up(0, k).start()

    def expert_step(t, carry):
        i = slot_of(t, e, total)

        @pl.when(t == 0)
        def _():
            whole(wgu.at[1 - h, pl.ds(0, 2), s], sib_recv.at[11])

        arrive(t)
        x = rows[i]
        activations = []
        for which in range(2):
            gate_part = lax.dot_general(
                wgu[which, 0].reshape(units, features), x, dims, preferred_element_type=jnp.float32)
            up_part = lax.dot_general(
                wgu[which, 1].reshape(units, features), x, dims, preferred_element_type=jnp.float32)
            activations.append(
                (gate_part / (1.0 + jnp.exp(-gate_part)) * up_part).T.astype(jnp.bfloat16))
        gates_all = gate_cols[i, my_rows(s), :]
        gate_lane = lax.broadcasted_iota(jnp.int32, gates_all.shape, 1)
        weight = [
            jnp.sum(jnp.where(gate_lane == 2 * e + which, gates_all, 0.0), axis=1, keepdims=True)
            for which in range(2)
        ]

        arrive_far(t)

        @pl.when(t == 0)
        def _():
            w_from_part(5)
            whole(wgu.at[1 - h, 2, s], sib_recv.at[12])

        for k in range(Z_CUTS):
            c = turn(k)
            mixed = None
            for which in range(2):
                piece = weight[which] * jnp.dot(
                    activations[which],
                    wgu[which, 2, :, :, col(c, down_width)].reshape(units, down_width),
                    preferred_element_type=jnp.float32)
                mixed = piece if mixed is None else mixed + piece
            results[i, c] = mixed.astype(jnp.bfloat16)

            @pl.when(jnp.logical_and(i > e, jnp.logical_not(has_down)))
            def _():
                z_up(i, c).start()

            @pl.when(jnp.logical_and(i < e, jnp.logical_not(has_up)))
            def _():
                z_down(i, c).start()
        return carry

    lax.fori_loop(0, total, expert_step, 0)

    def add_chain(i, c):
        z_up(i, c).wait_recv()
        results[i, c] = (
            results[i, c].astype(jnp.float32) + chain_in[i, c].astype(jnp.float32)
        ).astype(jnp.bfloat16)

    def relay_up(i, k):
        c = turn(k)
        add_chain(i, c)
        z_up(i, c).start()

    def relay_down(i, k):
        c = turn(k)
        add_chain(i, c)
        z_down(i, c).start()

    @pl.when(jnp.logical_and(middle, low_side))
    def _():
        for k in range(Z_CUTS):
            relay_up(e + 1, k)
        for k in range(Z_CUTS + 2):
            if k < Z_CUTS:
                relay_up(last, k)
            if k >= 2:
                relay_down(0, k - 2)

    @pl.when(jnp.logical_and(middle, jnp.logical_not(low_side)))
    def _():
        for k in range(Z_CUTS):
            relay_down(e - 1, k)
        for k in range(Z_CUTS + 2):
            if k < Z_CUTS:
                relay_down(0, k)
            if k >= 2:
                relay_up(last, k - 2)

    def out_sib(q):
        return sibling(13 + q, out_buf.at[q], out.at[s, :, pl.ds(q * down_width, down_width)])

    for k in range(Z_CUTS):
        c = turn(k)
        q = k % 2

        @pl.when(has_down)
        def _():
            z_up(e, c).wait_recv()

        @pl.when(has_up)
        def _():
            place = total + c * (total + 1)
            block_ref = chain_in.at[total, c]
            remote(Z_UP, 0, Z_IN, place, block_ref, block_ref, {"ep": e + 1}).wait_recv()
        side = jnp.where(k < Z_CUTS // 2, 1 - s, s)
        value = results[e, c].astype(jnp.float32)
        value = value + jnp.where(has_down, chain_in[e, c].astype(jnp.float32), 0.0)
        value = value + jnp.where(has_up, chain_in[total, c].astype(jnp.float32), 0.0)
        value = hid[side, :, q * down_width:(q + 1) * down_width].astype(jnp.float32) + value
        if k < Z_CUTS // 2:
            out_buf[q] = value.astype(jnp.bfloat16)
            out_sib(q).start()
        else:
            out[s, :, q * down_width:(q + 1) * down_width] = value.astype(jnp.bfloat16)
    for q in range(2):
        out_sib(q).wait_recv()

    whole(wgu.at[h, :, s, pl.ds(0, cut)], send_sem.at[W_SIDE])
    whole(wgu.at[h, :, s, pl.ds(0, cut)], send_sem.at[W_PART])
    whole(wgu.at[1 - h, :, s], sib_send.at[11])
    whole(part_out, send_sem.at[P_SIDE])
    for copy in kv_sib + w_sib + [att_sib, att_own, hid_sib(0), hid_sib(1), out_sib(0), out_sib(1)]:
        copy.wait_send()

    for i in range(total):
        sends_up = [(N_UP, nbuf, i + 1), (C_UP, cbuf, i + 1), (X_UP, rows, i + 1),
                    (Z_UP, results, last - i)]
        sends_down = [(C_DOWN, cbuf, total - i), (X_DOWN, rows, total - i), (Z_DOWN, results, i)]
        sends = (sends_up if i < last else []) + (sends_down if i > 0 else [])

        @pl.when(e == i)
        def _():
            for kind, ref, count in sends:
                whole(ref.at[pl.ds(0, count)], send_sem.at[kind])


def fused_shards(
    queries, cache_keys, cache_values, page_len, new_keys, new_values, out_proj, residual,
    norm_gain, gate_up, w_down, expert_ids, gates,
):
    total = lax.axis_size("ep")
    all_experts = total * lax.axis_size("hd")
    query_rows = queries.shape[0]
    heads = queries.shape[1] // HD // 2
    block_rows, half = residual.shape
    features = 2 * half
    own_rows = block_rows // 2
    page_c, page = cache_keys.shape[0], new_keys.shape[0]
    hidden = w_down.shape[1]
    tiles = 4
    arrived = semaphore_places(total, tiles)[-1]
    anywhere = pl.BlockSpec(memory_space=pl.ANY)
    bf, f32 = jnp.bfloat16, jnp.float32
    ids_rows, gate_rows = expert_ids.T, gates.T
    out = pl.pallas_call(
        functools.partial(layer_kernel, total, tiles),
        out_shape=pltpu.VMEM((2, own_rows, half), bf),
        in_specs=[pl.BlockSpec(memory_space=pltpu.SMEM)] + [anywhere] * 12,
        out_specs=pl.BlockSpec(memory_space=pltpu.VMEM),
        scratch_shapes=[
            pltpu.VMEM((heads, query_rows, HD), bf),
            pltpu.VMEM((total, 2, 2 * page_c + 16, HD), bf),
            pltpu.VMEM((total, 2, 2 * page, HD), bf),
            pltpu.VMEM((heads, query_rows, HD), f32),
            pltpu.VMEM((heads, query_rows, HD), f32),
            pltpu.VMEM((heads, query_rows, HD), f32),
            pltpu.VMEM((2, query_rows, heads * HD), bf),
            pltpu.VMEM(out_proj.shape, bf),
            pltpu.VMEM((tiles, own_rows, half // 2), bf),
            pltpu.VMEM((tiles, own_rows, half // 2), bf),
            pltpu.VMEM((block_rows, half), bf),
            pltpu.VMEM((2, own_rows, half), bf),
            pltpu.VMEM((2, 3, 2, hidden, features), bf),
            pltpu.VMEM((total, own_rows, features), bf),
            pltpu.VMEM((total, Z_CUTS, own_rows, features // Z_CUTS), bf),
            pltpu.VMEM((total + 1, Z_CUTS, own_rows, features // Z_CUTS), bf),
            pltpu.SemaphoreType.DMA((10,)),
            pltpu.SemaphoreType.DMA((arrived,)),
            pltpu.SemaphoreType.DMA((14,)),
            pltpu.SemaphoreType.DMA((SIB_COUNT,)),
            pltpu.SemaphoreType.DMA((SIB_COUNT,)),
            pltpu.VMEM((block_rows, half), f32),
            pltpu.VMEM((2, own_rows, features // Z_CUTS), bf),
            pltpu.VMEM((total, 2 * own_rows, 128), f32),
            pltpu.VMEM(ids_rows.shape, jnp.int32),
            pltpu.VMEM(gate_rows.shape, bf),
            pltpu.VMEM(norm_gain.shape, bf),
        ],
        compiler_params=pltpu.CompilerParams(
            collective_id=0, has_side_effects=True, vmem_limit_bytes=58 * 1024 * 1024
        ),
    )(page_len, queries, cache_keys, cache_values, new_keys, new_values, out_proj, residual,
      norm_gain, gate_up, w_down, ids_rows, gate_rows)
    return out.reshape(block_rows, half)


def layer(*arguments):
    queries, page_rows, ids = arguments[0], arguments[4].shape[0], arguments[11]
    pair = lax.axis_size("ep") >= 4 and lax.axis_size("grp") == 2
    pair = pair and lax.axis_size("hd") == 2 and lax.axis_size("sub") == 2
    slots = block_sizes(ids.shape[0], lax.axis_size("ep"), lax.axis_size("hd"))[1]
    group_width = QH // KVH
    whole_heads = queries.shape[1] == 2 * group_width * HD
    whole_pages = page_rows == 128 and arguments[1].shape[0] == 128
    rows_fit = queries.shape[0] == 2 * page_rows and ids.shape == (128, 8)
    rows_fit = rows_fit and lax.axis_size("ep") == 4
    if pair and slots == ids.shape[0] and whole_heads and whole_pages and rows_fit:
        return fused_shards(*arguments)
    return shards(*arguments)


def solution(mesh):
    return jax.shard_map(
        layer,
        mesh=mesh,
        in_specs=(
            P(("grp", "ep"), "hd"),
            P(("grp", "ep", "sub"), None),
            P(("grp", "ep", "sub"), None),
            P(("grp", "ep", "sub")),
            P(("grp", "ep", "sub"), None),
            P(("grp", "ep", "sub"), None),
            P("hd", "sub"),
            P(("grp", "ep", "hd"), "sub"),
            P(),
            P(("ep", "hd"), None, "sub", None),
            P(("ep", "hd"), "sub", None),
            P(("grp", "ep", "hd"), None),
            P(("grp", "ep", "hd"), None),
        ),
        out_specs=P(("grp", "ep", "hd"), "sub"),
        check_vma=False,
    )
```

```python
import functools
import math

import jax
import jax.numpy as jnp
from jax import lax
from jax.experimental import pallas as pl
from jax.experimental.pallas import tpu as pltpu
from jax.sharding import PartitionSpec as P

QH = 32
KVH = 4
HD = 128
GROUPS_ROW = 4


NEG_FILL = -1e30
EPSILON = 1e-06
KEY_BLOCK = 1024
FAR_RANK = 1073741824
MESH = pl.DeviceIdType.MESH


def joined(x, axis, join):
    gathered = jax.tree.map(
        lambda a, kind: lax.all_gather(a.astype(kind), axis),
        x,
        jax.tree.map(lambda a: jnp.bfloat16 if a.dtype == jnp.float32 else a.dtype, x),
    )

    def take(source):
        return jax.tree.map(
            lambda a, own: lax.dynamic_index_in_dim(a, source, 0, False).astype(own.dtype),
            gathered,
            x,
        )

    return lax.fori_loop(
        1, lax.axis_size(axis), lambda source, state: join(state, take(source)), take(0)
    )


def block_sizes(block_rows, group_total, experts_group):
    group_slots = min(block_rows, 3 * GROUPS_ROW * block_rows // (2 * group_total))
    return (group_slots, 2 * group_slots // experts_group)


def attend_block(fold_state, packed, key_rank, query_heads, row_ids, kv_heads):
    running_max, weight_sum, weighted = fold_state
    half_cols = packed.shape[1] // 2
    length = packed.shape[0]
    key_part = packed[:, :half_cols].reshape(length, kv_heads, half_cols // kv_heads)
    value_part = packed[:, half_cols:].reshape(length, kv_heads, half_cols // kv_heads)
    scores = jnp.einsum(
        "rkqd,lkd->rkql", query_heads, key_part, preferred_element_type=jnp.float32
    ) * (1.0 / math.sqrt(HD))
    allowed = (key_rank[None, :] <= row_ids[:, None])[:, None, None, :]
    masked = jnp.where(allowed, scores, NEG_FILL)
    new_max = jnp.maximum(running_max, jnp.max(masked, axis=3))
    factor = jnp.exp(running_max - new_max)
    exp_terms = jnp.where(allowed, jnp.exp(scores - new_max[..., None]), 0.0)
    weight_sum = weight_sum * factor + jnp.sum(exp_terms, axis=3)
    weighted = weighted * factor[..., None] + jnp.einsum(
        "rkql,lkd->rkqd",
        exp_terms.astype(jnp.bfloat16),
        value_part,
        preferred_element_type=jnp.float32,
    )
    return (new_max, weight_sum, weighted)


def join_parts(first_part, second_part):
    first_max, first_sum, first_weighted = first_part
    second_max, second_sum, second_weighted = second_part
    joint_max = jnp.maximum(first_max, second_max)
    first_factor = jnp.exp(first_max - joint_max)
    second_factor = jnp.exp(second_max - joint_max)
    joint_sum = first_sum * first_factor + second_sum * second_factor
    joint_weighted = (
        first_weighted * first_factor[..., None] + second_weighted * second_factor[..., None]
    )
    return (joint_max, joint_sum, joint_weighted)


def shards(
    queries,
    cache_keys,
    cache_values,
    page_len,
    new_keys,
    new_values,
    out_proj,
    residual,
    norm_gain,
    gate_up,
    w_down,
    expert_ids,
    gates,
):
    query_rows = queries.shape[0]
    heads_here = queries.shape[1] // HD
    group_width = QH // KVH
    kv_heads = max(1, heads_here // group_width)
    per_kv = heads_here // kv_heads
    kv_first = lax.axis_index("hd") * heads_here // group_width

    def kv_columns(source):
        return lax.dynamic_slice_in_dim(source, kv_first * HD, kv_heads * HD, 1)

    local_keys = jnp.concatenate([kv_columns(cache_keys), kv_columns(new_keys)], axis=0)
    local_values = jnp.concatenate([kv_columns(cache_values), kv_columns(new_values)], axis=0)
    packed_local = jnp.concatenate([local_keys, local_values], axis=1)
    cache_rows = cache_keys.shape[0]
    new_rows = new_keys.shape[0]
    cache_rank = jnp.where(
        jnp.arange(cache_rows, dtype=jnp.int32) < page_len[0], -1, FAR_RANK
    ).astype(jnp.int32)
    new_block = lax.axis_index("ep") * lax.axis_size("sub") + lax.axis_index("sub")
    new_rank = new_block * new_rows + jnp.arange(new_rows, dtype=jnp.int32)
    rank_local = jnp.concatenate([cache_rank, new_rank], axis=0)
    row_ids = lax.axis_index("ep") * query_rows + jnp.arange(query_rows, dtype=jnp.int32)
    query_heads = queries.reshape(query_rows, kv_heads, per_kv, HD)

    def fold_keys(fold_state, piece_data):
        packed, key_rank = piece_data
        length = packed.shape[0]
        if length > KEY_BLOCK and length % KEY_BLOCK == 0:
            block_count = length // KEY_BLOCK

            def scan_step(inner_state, block_data):
                return (
                    attend_block(
                        inner_state, block_data[0], block_data[1], query_heads, row_ids, kv_heads
                    ),
                    None,
                )

            fold_state, _ = lax.scan(
                scan_step,
                fold_state,
                (
                    packed.reshape(block_count, KEY_BLOCK, packed.shape[1]),
                    key_rank.reshape(block_count, KEY_BLOCK),
                ),
            )
            return fold_state
        return attend_block(fold_state, packed, key_rank, query_heads, row_ids, kv_heads)

    start_state = (
        jnp.full((query_rows, kv_heads, per_kv), NEG_FILL, jnp.float32),
        jnp.zeros((query_rows, kv_heads, per_kv), jnp.float32),
        jnp.zeros((query_rows, kv_heads, per_kv, HD), jnp.float32),
    )
    fold_state = fold_keys(
        start_state,
        (
            lax.all_gather(packed_local, "ep", axis=0, tiled=True),
            lax.all_gather(rank_local, "ep", axis=0, tiled=True),
        ),
    )
    running_max, weight_sum, weighted = joined(fold_state, "sub", join_parts)
    attended = (
        (weighted / weight_sum[..., None]).reshape(query_rows, heads_here * HD).astype(jnp.bfloat16)
    )
    projected = lax.psum_scatter(
        jnp.dot(attended, out_proj, preferred_element_type=jnp.float32).astype(jnp.bfloat16),
        "hd",
        scatter_dimension=0,
        tiled=True,
    ).astype(jnp.float32)
    hidden_half = (residual.astype(jnp.float32) + projected).astype(jnp.bfloat16)
    widened = hidden_half.astype(jnp.float32)
    features = norm_gain.shape[0]
    half_width = hidden_half.shape[1]
    square_sum = lax.psum(jnp.sum(widened * widened, axis=1), "sub")
    gain_half = lax.dynamic_slice_in_dim(
        norm_gain, lax.axis_index("sub") * half_width, half_width, 0
    )
    normed = (
        widened
        * lax.rsqrt(square_sum[:, None] / features + EPSILON)
        * gain_half.astype(jnp.float32)
    ).astype(jnp.bfloat16)
    pair_weights = gate_up[0].reshape(-1, features)
    hidden_units = w_down.shape[1]
    group_total = lax.axis_size("ep")
    group_experts = lax.axis_size("hd")
    all_experts = group_total * group_experts
    block_rows = expert_ids.shape[0]
    group_slots, expert_slots = block_sizes(block_rows, group_total, group_experts)
    chosen = (
        expert_ids[:, :, None] == jnp.arange(all_experts, dtype=jnp.int32)[None, None, :]
    ).astype(jnp.int32)
    named_count = jnp.sum(chosen, axis=1)
    earlier = jnp.cumsum(named_count, axis=0) - named_count
    slot_index = jnp.sum(chosen * earlier[:, None, :], axis=2)
    position = expert_ids * expert_slots + slot_index
    slot_columns = jnp.arange(all_experts * expert_slots, dtype=jnp.int32)
    gate_table = jnp.sum(
        jnp.where(
            position[:, :, None] == slot_columns[None, None, :],
            gates.astype(jnp.float32)[:, :, None],
            0.0,
        ),
        axis=1,
    ).astype(jnp.bfloat16)
    placed = (gate_table != 0).astype(jnp.bfloat16)
    outgoing = jnp.einsum("rq,rd->qd", placed, normed, preferred_element_type=jnp.float32).astype(
        jnp.bfloat16
    )
    outgoing = outgoing.reshape(all_experts, expert_slots, normed.shape[1])
    arrived = lax.all_to_all(outgoing, ("ep", "hd"), split_axis=0, concat_axis=0, tiled=True)
    lead_shape = arrived.shape[:-1]
    rows_in = arrived.reshape(-1, arrived.shape[-1])
    rows_in = lax.all_gather(rows_in, "sub", axis=1, tiled=True)
    projected_pair = jnp.einsum(
        "rd,fd->rf", rows_in, pair_weights, preferred_element_type=jnp.float32
    )
    activation = (
        jax.nn.silu(projected_pair[:, :hidden_units]) * projected_pair[:, hidden_units:]
    ).astype(jnp.bfloat16)
    partial_out = jnp.dot(activation, w_down[0], preferred_element_type=jnp.float32)
    expert_out = lax.psum_scatter(
        partial_out.astype(jnp.bfloat16), "sub", scatter_dimension=1, tiled=True
    )
    results = expert_out.reshape(lead_shape + (expert_out.shape[1],))
    returned = lax.all_to_all(results, ("ep", "hd"), split_axis=0, concat_axis=0, tiled=True)
    mixture = jnp.dot(
        gate_table,
        returned.reshape(all_experts * expert_slots, half_width),
        preferred_element_type=jnp.float32,
    )
    return (widened + mixture).astype(jnp.bfloat16)


def slot_of(step, place, total):
    near = jnp.minimum(place, total - 1 - place)
    odd = place - (step + 1) // 2
    even = place + step // 2
    beside = jnp.where(step % 2 == 1, odd, even)
    beyond = jnp.where(place < total - 1 - place, step, total - 1 - step)
    return jnp.where(step <= 2 * near, beside, beyond)


(C_UP, C_DOWN, N_UP, X_UP, X_DOWN, W_SIDE, W_PART, Z_UP, Z_DOWN, P_SIDE) = range(10)
(C_IN, N_IN, X_IN, W_SIDE_IN, W_PART_IN, Z_IN, P_IN) = range(7)
SIB_COUNT = 15
W_PIECES = 6
X_CUTS = 2
Z_CUTS = 4
LOG2_E = math.log2(math.e)


def semaphore_places(total, tiles):
    arrived = (total, total, X_CUTS * total, W_PIECES, W_PIECES, Z_CUTS * (total + 1), tiles)
    return [sum(arrived[:i]) for i in range(len(arrived) + 1)]


def layer_kernel(
    total, tiles,
    page_len, queries, cache_keys, cache_values, new_keys, new_values, out_proj, residual, gain,
    gate_up, w_down, ids_t, gates_t,
    out,
    q_v, cbuf, nbuf, m_v, l_v, acc_v, att, proj_w, part_out, part_in, res_v, hid, wgu,
    rows, results, chain_in,
    send_sem, recv_sem, load_sem, sib_send, sib_recv, proj_f, out_buf, gate_cols, ids_v, gates_v, gain_v,
):
    e = lax.axis_index("ep")
    h = lax.axis_index("hd")
    s = lax.axis_index("sub")
    part = lax.axis_index("grp")
    last = total - 1
    heads = q_v.shape[0]
    page = new_keys.shape[0]
    page_c = cache_keys.shape[0]
    half = out.shape[2]
    own_rows = out.shape[1]
    features = 2 * half
    scale = LOG2_E / math.sqrt(HD)
    has_up = e < last
    arrived_at = semaphore_places(total, tiles)
    has_down = e > 0

    def col(index, width):
        return pl.ds(pl.multiple_of(index * width, width), width)

    def local(index, src, dst):
        return pltpu.make_async_copy(src, dst, load_sem.at[index])

    barrier = pltpu.get_barrier_semaphore()
    pl.semaphore_signal(barrier, inc=1, device_id={"sub": 1 - s}, device_id_type=MESH)
    pl.semaphore_signal(barrier, inc=1, device_id={"hd": 1 - h}, device_id_type=MESH)
    pl.semaphore_signal(barrier, inc=1, device_id={"grp": 1 - part}, device_id_type=MESH)

    @pl.when(has_up)
    def _():
        pl.semaphore_signal(barrier, inc=1, device_id={"ep": e + 1}, device_id_type=MESH)

    @pl.when(has_down)
    def _():
        pl.semaphore_signal(barrier, inc=1, device_id={"ep": e - 1}, device_id_type=MESH)

    def whole(ref, semaphore):
        pltpu.make_async_copy(ref, ref, semaphore).wait()

    mine = 2 * h + s
    loads = [
        local(0, cache_keys.at[:, col(mine, HD)], cbuf.at[e, s, pl.ds(0, page_c)]),
        local(1, cache_values.at[:, col(mine, HD)], cbuf.at[e, s, pl.ds(page_c, page_c)]),
        local(3, new_keys.at[:, col(mine, HD)], nbuf.at[e, s, pl.ds(0, page)]),
        local(4, new_values.at[:, col(mine, HD)], nbuf.at[e, s, pl.ds(page, page)]),
    ]
    q_loads = [
        local(13, queries.at[:, col(s * heads + i, HD)], q_v.at[i]) for i in range(heads)
    ]
    w_loads = [
        local(5, out_proj, proj_w),
        local(6, residual, res_v),
        local(9, gate_up.at[0], wgu.at[h, pl.ds(0, 2), s]),
        local(10, w_down.at[0], wgu.at[h, 2, s]),
    ]
    small_loads = [local(2, ids_t, ids_v), local(11, gates_t, gates_v), local(12, gain, gain_v)]
    for copy in small_loads + loads + q_loads + w_loads:
        copy.start()

    experts = 2 * total
    lane = lax.broadcasted_iota(jnp.int32, (8, HD), 1)
    seen = jnp.where(lane < page_len[0], 0.0, NEG_FILL)
    for copy in small_loads:
        copy.wait()
    ids = ids_v[...]
    gate_values = gates_v[...].astype(jnp.float32)
    place = lax.broadcasted_iota(jnp.int32, (8, HD), 0)
    by_expert = jnp.zeros((8, HD), jnp.float32)
    for x in range(experts):
        one_row = jnp.sum(jnp.where(ids == x, gate_values, 0.0), axis=0, keepdims=True)
        by_expert = jnp.where(place == x, one_row, by_expert)
    cbuf[e, s, 2 * page_c:2 * page_c + 16, :] = jnp.concatenate(
        [seen, by_expert], axis=0).astype(jnp.bfloat16)

    pl.semaphore_wait(barrier, 3 + has_up.astype(jnp.int32) + has_down.astype(jnp.int32))

    def sibling(index, src, dst, arrival=None):
        return pltpu.make_async_remote_copy(
            src_ref=src, dst_ref=dst, send_sem=sib_send.at[index],
            recv_sem=sib_recv.at[index if arrival is None else arrival],
            device_id={"sub": 1 - s}, device_id_type=MESH)

    def remote(kind, index, arrival, slot, src, dst, where):
        return pltpu.make_async_remote_copy(
            src_ref=src, dst_ref=dst, send_sem=send_sem.at[kind],
            recv_sem=recv_sem.at[arrived_at[arrival] + slot], device_id=where, device_id_type=MESH)

    theirs = 2 * h + 1 - s
    kv_sib = [
        sibling(0, cache_keys.at[:, col(theirs, HD)], cbuf.at[e, s, pl.ds(0, page_c)]),
        sibling(1, cache_values.at[:, col(theirs, HD)], cbuf.at[e, s, pl.ds(page_c, page_c)]),
        sibling(2, cbuf.at[e, s, pl.ds(2 * page_c, 16)], cbuf.at[e, s, pl.ds(2 * page_c, 16)]),
        sibling(3, new_keys.at[:, col(theirs, HD)], nbuf.at[e, s, pl.ds(0, page)]),
        sibling(4, new_values.at[:, col(theirs, HD)], nbuf.at[e, s, pl.ds(page, page)]),
    ]
    w_sib = [
        sibling(5, gate_up.at[0], wgu.at[h, pl.ds(0, 2), s]),
        sibling(6, w_down.at[0], wgu.at[h, 2, s]),
    ]
    for copy in kv_sib:
        copy.start()

    cut = wgu.shape[3] // 2
    piece_rows = cut // 2

    def cut_rows(which, piece):
        return pl.ds(pl.multiple_of(which * cut + piece % 2 * piece_rows, piece_rows), piece_rows)

    def w_block(piece, which):
        return wgu.at[1 - h, piece // 2, s, cut_rows(which, piece)]

    def w_side(piece):
        kind = piece // 2
        src = (w_down.at[0, cut_rows(part, piece)] if kind == 2
               else gate_up.at[0, kind, cut_rows(part, piece)])
        return remote(W_SIDE, piece, W_SIDE_IN, piece, src,
                      wgu.at[h, kind, s, cut_rows(part, piece)], {"hd": 1 - h})

    def w_part(piece):
        block_ref = w_block(piece, part)
        return remote(W_PART, piece, W_PART_IN, piece, block_ref, block_ref, {"grp": 1 - part})

    def w_near(piece, which):
        block_ref = w_block(piece, jnp.where(which == 0, part, 1 - part))
        return sibling(11, block_ref, block_ref, 11 + piece // 4)

    def w_from_side(piece):
        block_ref = w_block(piece, part)
        remote(W_SIDE, piece, W_SIDE_IN, piece, block_ref, block_ref, {"hd": 1 - h}).wait_recv()
        w_part(piece).start()
        w_near(piece, 0).start()

    def w_from_part(piece):
        w_part(piece).wait_recv()
        w_near(piece, 1).start()

    for piece in range(W_PIECES):
        w_side(piece).start()

    def c_up(i):
        return remote(C_UP, i, C_IN, i, cbuf.at[i], cbuf.at[i], {"ep": e + 1})

    def c_down(i):
        return remote(C_DOWN, i, C_IN, i, cbuf.at[i], cbuf.at[i], {"ep": e - 1})

    def n_up(i):
        return remote(N_UP, i, N_IN, i, nbuf.at[i], nbuf.at[i], {"ep": e + 1})

    for copy in loads:
        copy.wait()
    for copy in kv_sib:
        copy.wait_recv()

    @pl.when(has_up)
    def _():
        n_up(e).start()
        c_up(e).start()

    @pl.when(has_down)
    def _():
        c_down(e).start()

    for copy in w_sib:
        copy.start()
    whole(q_v, load_sem.at[13])

    def parts_of(buf, index, size):
        return (buf[index, :, 0:size, :].reshape(2 * size, HD),
                buf[index, :, size:2 * size, :].reshape(2 * size, HD))

    def attend(index, with_cache, with_new, causal, first=False):
        pieces = []
        if with_cache:
            pieces.append(parts_of(cbuf, index, page_c))
            line = jnp.concatenate(
                [cbuf[index, 0, 2 * page_c:2 * page_c + 16, :],
                 cbuf[index, 1, 2 * page_c:2 * page_c + 16, :]], axis=1)[0:1].astype(jnp.float32)
        if with_new:
            pieces.append(parts_of(nbuf, index, page))

        def one_head(i, carry):
            query = q_v[i]
            scores = []
            for place, (key_part, _) in enumerate(pieces):
                one = lax.dot_general(
                    query, key_part, (((1,), (1,)), ((), ())), preferred_element_type=jnp.float32)
                if with_cache and place == 0:
                    one = one + line
                elif causal:
                    r = lax.broadcasted_iota(jnp.int32, one.shape, 0)
                    c = lax.broadcasted_iota(jnp.int32, one.shape, 1)
                    one = jnp.where(c <= r, one, NEG_FILL)
                scores.append(one)
            top = jnp.max(functools.reduce(
                jnp.maximum, [one[:, j:j + HD] for one in scores for j in range(0, one.shape[1], HD)]),
                axis=1, keepdims=True)
            if first:
                new = jnp.broadcast_to(top, m_v.shape[1:])
            else:
                old = m_v[i]
                new = jnp.maximum(old, top)
                factor = jnp.exp2((old - new) * scale)
            new_col = new[:, 0:1]
            weighted = None
            lane_sum = None
            for one, (_, value_part) in zip(scores, pieces):
                p = jnp.exp2((one - new_col) * scale)
                term = jnp.dot(p.astype(jnp.bfloat16), value_part, preferred_element_type=jnp.float32)
                weighted = term if weighted is None else weighted + term
                for j in range(0, p.shape[1], HD):
                    piece_sum = p[:, j:j + HD]
                    lane_sum = piece_sum if lane_sum is None else lane_sum + piece_sum
            m_v[i] = new
            if first:
                l_v[i] = lane_sum
                acc_v[i] = weighted
            else:
                l_v[i] = l_v[i] * factor + lane_sum
                acc_v[i] = acc_v[i] * factor + weighted
            return carry

        lax.fori_loop(0, heads, one_head, 0, unroll=8)

    attend(e, True, True, True, True)

    middle = jnp.logical_and(has_up, has_down)
    low_side = e < total // 2

    def kv_arrive(t):
        @pl.when(jnp.logical_not(middle))
        def _():
            i = slot_of(t, e, total)

            @pl.when(i < e)
            def _():
                n_up(i).wait_recv()
            c_up(i).wait_recv()

        @pl.when(jnp.logical_and(middle, t == 1))
        def _():
            n_up(e - 1).wait_recv()
            n_up(e - 1).start()
            c_down(e + 1).wait_recv()
            c_down(e + 1).start()
            c_up(e - 1).wait_recv()
            c_up(e - 1).start()

        @pl.when(jnp.logical_and(jnp.logical_and(middle, low_side), t == 2))
        def _():
            c_down(last).wait_recv()
            c_down(last).start()

        @pl.when(jnp.logical_and(middle, jnp.logical_not(low_side)))
        def _():
            @pl.when(t == 2)
            def _():
                n_up(0).wait_recv()
                n_up(0).start()

            @pl.when(t == 3)
            def _():
                c_up(0).wait_recv()
                c_up(0).start()

    def kv_step(t, carry):
        i = slot_of(t, e, total)
        below = i < e
        kv_arrive(t)

        @pl.when(t == 1)
        def _():
            w_from_side(0)

        @pl.when(jnp.logical_and(t == 3, jnp.logical_not(has_up)))
        def _():
            w_from_side(3)

        @pl.when(below)
        def _():
            attend(i, True, True, False)

        @pl.when(jnp.logical_not(below))
        def _():
            attend(i, True, False, False)

        @pl.when(t == 1)
        def _():
            w_from_side(1)

        @pl.when(t == 2)
        def _():
            w_from_side(2)

        @pl.when(t == 3)
        def _():
            @pl.when(has_up)
            def _():
                w_from_side(3)
            w_from_part(0)
        return carry

    lax.fori_loop(1, total, kv_step, 0)

    def gate_step(i, carry):
        flat = cbuf[i, 0, 2 * page_c:2 * page_c + 16, :].astype(jnp.float32)[8:16]
        gate_cols[i] = jnp.concatenate(
            [flat, jnp.zeros((HD - 8, HD), jnp.float32)], axis=0).T
        return carry

    block = 2 * own_rows

    def block_at(which):
        return pl.ds(pl.multiple_of(which * block, block), block)

    def att_rows(which):
        return att.at[s, block_at(which)]

    def finish(which):
        for i in range(heads):
            att[s, block_at(which), i * HD:(i + 1) * HD] = (
                acc_v[i, block_at(which), :]
                / jnp.sum(l_v[i, block_at(which), :], axis=1, keepdims=True)).astype(jnp.bfloat16)

    finish(1 - h)
    att_sib = sibling(7, att_rows(1 - h), att_rows(1 - h))
    att_sib.start()
    finish(h)
    att_own = sibling(9, att_rows(h), att_rows(h))
    att_own.start()
    for copy in w_loads[:2]:
        copy.wait()
    att_sib.wait_recv()

    width = half // tiles
    side_width = half // (tiles // X_CUTS)
    contract = att.shape[2]

    x_rows = own_rows // X_CUTS

    def x_cut(i, k):
        return rows.at[i, pl.ds(k * x_rows, x_rows)]

    def x_up(i, k):
        return remote(X_UP, X_CUTS * i + k, X_IN, X_CUTS * i + k, x_cut(i, k), x_cut(i, k),
                      {"ep": e + 1})

    def x_down(i, k):
        return remote(X_DOWN, X_CUTS * i + k, X_IN, X_CUTS * i + k, x_cut(i, k), x_cut(i, k),
                      {"ep": e - 1})

    def z_up(i, c):
        place = i + c * (total + 1)
        return remote(Z_UP, i + c * total, Z_IN, place, results.at[i, c], chain_in.at[i, c], {"ep": e + 1})

    def z_down(i, c):
        slot = jnp.where(i == e - 1, total, i)
        return remote(Z_DOWN, i + c * total, Z_IN, slot + c * (total + 1),
                      results.at[i, c], chain_in.at[slot, c], {"ep": e - 1})

    def project(a0, a1, j, size):
        return jnp.dot(
            a0, proj_w[0:contract, col(j, size)], preferred_element_type=jnp.float32
        ) + jnp.dot(
            a1, proj_w[contract:2 * contract, col(j, size)], preferred_element_type=jnp.float32)

    def p_side(j):
        return remote(P_SIDE, j, P_IN, j, part_out.at[j], part_in.at[j], {"hd": 1 - h})

    def project_theirs(j, carry):
        first = (1 - h) * block + j // (tiles // X_CUTS) * x_rows
        a0, a1 = [
            jnp.concatenate([
                att[which, pl.ds(pl.multiple_of(first + u * own_rows, x_rows), x_rows), :]
                for u in range(2)], axis=0)
            for which in range(2)]
        part_out[j] = project(a0, a1, j % (tiles // X_CUTS), side_width).astype(jnp.bfloat16)
        p_side(j).start()
        return carry

    lax.fori_loop(0, tiles, project_theirs, 0)
    w_from_side(4)
    w_from_part(1)
    att_own.wait_recv()

    def project_keep(j, carry):
        own = pl.ds(pl.multiple_of(h * block, block), block)
        proj_f[:, col(j, width)] = project(att[0, own, :], att[1, own, :], j, width)
        return carry

    lax.fori_loop(0, tiles, project_keep, 0)
    lax.fori_loop(0, total, gate_step, 0)
    w_from_side(5)
    w_from_part(2)
    w_from_part(3)

    def my_rows(which):
        return pl.ds(pl.multiple_of(which * own_rows, own_rows), own_rows)

    def my_cut(which, k):
        return pl.ds(pl.multiple_of(which * own_rows + k * x_rows, x_rows), x_rows)

    def hid_sib(k):
        return sibling(8 + 2 * k, res_v.at[my_cut(1 - s, k)], hid.at[s, pl.ds(k * x_rows, x_rows)])

    for copy in w_loads[2:]:
        copy.wait()
    for copy in w_sib:
        copy.wait_recv()
    g = gain_v[...].astype(jnp.float32).reshape(1, features)
    for k in range(X_CUTS):
        for j in range(tiles // X_CUTS):
            place = k * (tiles // X_CUTS) + j
            span = slice(j * side_width, (j + 1) * side_width)
            p_side(place).wait_recv()
            for u in range(2):
                cut_u = slice(u * own_rows + k * x_rows, u * own_rows + (k + 1) * x_rows)
                res_v[cut_u, span] = (
                    res_v[cut_u, span].astype(jnp.float32)
                    + (proj_f[cut_u, span]
                       + part_in[place, u * x_rows:(u + 1) * x_rows, :].astype(jnp.float32))
                ).astype(jnp.bfloat16)
        hid_sib(k).start()
        at_k = slice(k * x_rows, (k + 1) * x_rows)
        hid[s, at_k] = res_v[my_cut(s, k), :]
        hid_sib(k).wait_recv()
        h0 = hid[0, at_k].astype(jnp.float32)
        h1 = hid[1, at_k].astype(jnp.float32)
        square = jnp.sum(h0 * h0, axis=1, keepdims=True) + jnp.sum(h1 * h1, axis=1, keepdims=True)
        inverse = lax.rsqrt(square / features + EPSILON)
        rows[e, at_k, 0:half] = (h0 * inverse * g[0:1, 0:half]).astype(jnp.bfloat16)
        rows[e, at_k, half:features] = (h1 * inverse * g[0:1, half:features]).astype(jnp.bfloat16)

        @pl.when(has_up)
        def _():
            x_up(e, k).start()

        @pl.when(has_down)
        def _():
            x_down(e, k).start()

    w_from_part(4)
    units = 2 * wgu.shape[3]
    dims = (((1,), (1,)), ((), ()))
    down_width = features // Z_CUTS

    def turn(k):
        return Z_CUTS // 2 * jnp.where(k < Z_CUTS // 2, 1 - s, s) + k % (Z_CUTS // 2)

    def arrive_near(k):
        @pl.when(middle)
        def _():
            x_up(e - 1, k).wait_recv()
            x_up(e - 1, k).start()
            x_down(e + 1, k).wait_recv()
            x_down(e + 1, k).start()

    def arrive(t):
        @pl.when(jnp.logical_and(jnp.logical_not(middle), t > 0))
        def _():
            for k in range(X_CUTS):
                x_up(slot_of(t, e, total), k).wait_recv()

        @pl.when(t == 1)
        def _():
            for k in range(X_CUTS):
                arrive_near(k)

    def arrive_far(t):
        for k in range(X_CUTS):
            @pl.when(jnp.logical_and(middle, t == 1 + k))
            def _():
                @pl.when(low_side)
                def _():
                    x_down(last, k).wait_recv()
                    x_down(last, k).start()

                @pl.when(jnp.logical_not(low_side))
                def _():
                    x_up(0, k).wait_recv()
                    x_up(0, k).start()

    def expert_step(t, carry):
        i = slot_of(t, e, total)

        @pl.when(t == 0)
        def _():
            whole(wgu.at[1 - h, pl.ds(0, 2), s], sib_recv.at[11])

        arrive(t)
        x = rows[i]
        activations = []
        for which in range(2):
            gate_part = lax.dot_general(
                wgu[which, 0].reshape(units, features), x, dims, preferred_element_type=jnp.float32)
            up_part = lax.dot_general(
                wgu[which, 1].reshape(units, features), x, dims, preferred_element_type=jnp.float32)
            activations.append(
                (gate_part / (1.0 + jnp.exp(-gate_part)) * up_part).T.astype(jnp.bfloat16))
        gates_all = gate_cols[i, my_rows(s), :]
        gate_lane = lax.broadcasted_iota(jnp.int32, gates_all.shape, 1)
        weight = [
            jnp.sum(jnp.where(gate_lane == 2 * e + which, gates_all, 0.0), axis=1, keepdims=True)
            for which in range(2)
        ]

        arrive_far(t)

        @pl.when(t == 0)
        def _():
            w_from_part(5)
            whole(wgu.at[1 - h, 2, s], sib_recv.at[12])

        for k in range(Z_CUTS):
            c = turn(k)
            mixed = None
            for which in range(2):
                piece = weight[which] * jnp.dot(
                    activations[which],
                    wgu[which, 2, :, :, col(c, down_width)].reshape(units, down_width),
                    preferred_element_type=jnp.float32)
                mixed = piece if mixed is None else mixed + piece
            results[i, c] = mixed.astype(jnp.bfloat16)

            @pl.when(jnp.logical_and(i > e, jnp.logical_not(has_down)))
            def _():
                z_up(i, c).start()

            @pl.when(jnp.logical_and(i < e, jnp.logical_not(has_up)))
            def _():
                z_down(i, c).start()
        return carry

    lax.fori_loop(0, total, expert_step, 0)

    def add_chain(i, c):
        z_up(i, c).wait_recv()
        results[i, c] = (
            results[i, c].astype(jnp.float32) + chain_in[i, c].astype(jnp.float32)
        ).astype(jnp.bfloat16)

    def relay_up(i, k):
        c = turn(k)
        add_chain(i, c)
        z_up(i, c).start()

    def relay_down(i, k):
        c = turn(k)
        add_chain(i, c)
        z_down(i, c).start()

    @pl.when(jnp.logical_and(middle, low_side))
    def _():
        for k in range(Z_CUTS):
            relay_up(e + 1, k)
        for k in range(Z_CUTS + 2):
            if k < Z_CUTS:
                relay_up(last, k)
            if k >= 2:
                relay_down(0, k - 2)

    @pl.when(jnp.logical_and(middle, jnp.logical_not(low_side)))
    def _():
        for k in range(Z_CUTS):
            relay_down(e - 1, k)
        for k in range(Z_CUTS + 2):
            if k < Z_CUTS:
                relay_down(0, k)
            if k >= 2:
                relay_up(last, k - 2)

    def out_sib(q):
        return sibling(13 + q, out_buf.at[q], out.at[s, :, pl.ds(q * down_width, down_width)])

    for k in range(Z_CUTS):
        c = turn(k)
        q = k % 2

        @pl.when(has_down)
        def _():
            z_up(e, c).wait_recv()

        @pl.when(has_up)
        def _():
            place = total + c * (total + 1)
            block_ref = chain_in.at[total, c]
            remote(Z_UP, 0, Z_IN, place, block_ref, block_ref, {"ep": e + 1}).wait_recv()
        side = jnp.where(k < Z_CUTS // 2, 1 - s, s)
        value = results[e, c].astype(jnp.float32)
        value = value + jnp.where(has_down, chain_in[e, c].astype(jnp.float32), 0.0)
        value = value + jnp.where(has_up, chain_in[total, c].astype(jnp.float32), 0.0)
        value = hid[side, :, q * down_width:(q + 1) * down_width].astype(jnp.float32) + value
        if k < Z_CUTS // 2:
            out_buf[q] = value.astype(jnp.bfloat16)
            out_sib(q).start()
        else:
            out[s, :, q * down_width:(q + 1) * down_width] = value.astype(jnp.bfloat16)
    for q in range(2):
        out_sib(q).wait_recv()

    whole(wgu.at[h, :, s, pl.ds(0, cut)], send_sem.at[W_SIDE])
    whole(wgu.at[h, :, s, pl.ds(0, cut)], send_sem.at[W_PART])
    whole(wgu.at[1 - h, :, s], sib_send.at[11])
    whole(part_out, send_sem.at[P_SIDE])
    for copy in kv_sib + w_sib + [att_sib, att_own, hid_sib(0), hid_sib(1), out_sib(0), out_sib(1)]:
        copy.wait_send()

    for i in range(total):
        sends_up = [(N_UP, nbuf, i + 1), (C_UP, cbuf, i + 1), (X_UP, rows, i + 1),
                    (Z_UP, results, last - i)]
        sends_down = [(C_DOWN, cbuf, total - i), (X_DOWN, rows, total - i), (Z_DOWN, results, i)]
        sends = (sends_up if i < last else []) + (sends_down if i > 0 else [])

        @pl.when(e == i)
        def _():
            for kind, ref, count in sends:
                whole(ref.at[pl.ds(0, count)], send_sem.at[kind])


def fused_shards(
    queries, cache_keys, cache_values, page_len, new_keys, new_values, out_proj, residual,
    norm_gain, gate_up, w_down, expert_ids, gates,
):
    total = lax.axis_size("ep")
    all_experts = total * lax.axis_size("hd")
    query_rows = queries.shape[0]
    heads = queries.shape[1] // HD // 2
    block_rows, half = residual.shape
    features = 2 * half
    own_rows = block_rows // 2
    page_c, page = cache_keys.shape[0], new_keys.shape[0]
    hidden = w_down.shape[1]
    tiles = 4
    arrived = semaphore_places(total, tiles)[-1]
    anywhere = pl.BlockSpec(memory_space=pl.ANY)
    bf, f32 = jnp.bfloat16, jnp.float32
    ids_rows, gate_rows = expert_ids.T, gates.T
    out = pl.pallas_call(
        functools.partial(layer_kernel, total, tiles),
        out_shape=pltpu.VMEM((2, own_rows, half), bf),
        in_specs=[pl.BlockSpec(memory_space=pltpu.SMEM)] + [anywhere] * 12,
        out_specs=pl.BlockSpec(memory_space=pltpu.VMEM),
        scratch_shapes=[
            pltpu.VMEM((heads, query_rows, HD), bf),
            pltpu.VMEM((total, 2, 2 * page_c + 16, HD), bf),
            pltpu.VMEM((total, 2, 2 * page, HD), bf),
            pltpu.VMEM((heads, query_rows, HD), f32),
            pltpu.VMEM((heads, query_rows, HD), f32),
            pltpu.VMEM((heads, query_rows, HD), f32),
            pltpu.VMEM((2, query_rows, heads * HD), bf),
            pltpu.VMEM(out_proj.shape, bf),
            pltpu.VMEM((tiles, own_rows, half // 2), bf),
            pltpu.VMEM((tiles, own_rows, half // 2), bf),
            pltpu.VMEM((block_rows, half), bf),
            pltpu.VMEM((2, own_rows, half), bf),
            pltpu.VMEM((2, 3, 2, hidden, features), bf),
            pltpu.VMEM((total, own_rows, features), bf),
            pltpu.VMEM((total, Z_CUTS, own_rows, features // Z_CUTS), bf),
            pltpu.VMEM((total + 1, Z_CUTS, own_rows, features // Z_CUTS), bf),
            pltpu.SemaphoreType.DMA((10,)),
            pltpu.SemaphoreType.DMA((arrived,)),
            pltpu.SemaphoreType.DMA((14,)),
            pltpu.SemaphoreType.DMA((SIB_COUNT,)),
            pltpu.SemaphoreType.DMA((SIB_COUNT,)),
            pltpu.VMEM((block_rows, half), f32),
            pltpu.VMEM((2, own_rows, features // Z_CUTS), bf),
            pltpu.VMEM((total, 2 * own_rows, 128), f32),
            pltpu.VMEM(ids_rows.shape, jnp.int32),
            pltpu.VMEM(gate_rows.shape, bf),
            pltpu.VMEM(norm_gain.shape, bf),
        ],
        compiler_params=pltpu.CompilerParams(
            collective_id=0, has_side_effects=True, vmem_limit_bytes=58 * 1024 * 1024
        ),
    )(page_len, queries, cache_keys, cache_values, new_keys, new_values, out_proj, residual,
      norm_gain, gate_up, w_down, ids_rows, gate_rows)
    return out.reshape(block_rows, half)


def layer(*arguments):
    queries, page_rows, ids = arguments[0], arguments[4].shape[0], arguments[11]
    pair = lax.axis_size("ep") >= 4 and lax.axis_size("grp") == 2
    pair = pair and lax.axis_size("hd") == 2 and lax.axis_size("sub") == 2
    slots = block_sizes(ids.shape[0], lax.axis_size("ep"), lax.axis_size("hd"))[1]
    group_width = QH // KVH
    whole_heads = queries.shape[1] == 2 * group_width * HD
    whole_pages = page_rows == 128 and arguments[1].shape[0] == 128
    rows_fit = queries.shape[0] == 2 * page_rows and ids.shape == (128, 8)
    rows_fit = rows_fit and lax.axis_size("ep") == 4
    if pair and slots == ids.shape[0] and whole_heads and whole_pages and rows_fit:
        return fused_shards(*arguments)
    return shards(*arguments)


def solution(mesh):
    return jax.shard_map(
        layer,
        mesh=mesh,
        in_specs=(
            P(("grp", "ep"), "hd"),
            P(("grp", "ep", "sub"), None),
            P(("grp", "ep", "sub"), None),
            P(("grp", "ep", "sub")),
            P(("grp", "ep", "sub"), None),
            P(("grp", "ep", "sub"), None),
            P("hd", "sub"),
            P(("grp", "ep", "hd"), "sub"),
            P(),
            P(("ep", "hd"), None, "sub", None),
            P(("ep", "hd"), "sub", None),
            P(("grp", "ep", "hd"), None),
            P(("grp", "ep", "hd"), None),
        ),
        out_specs=P(("grp", "ep", "hd"), "sub"),
        check_vma=False,
    )
```
